32 devices in a mesh: gx: 16 (over z, y, x), gy: 2 (over core).
Axes of the slice: x: 2, y: 2, z: 4, core: 2. Of those that a mesh axis runs over, the one named last changes fastest.
Arguments:
- scalars: bfloat16 [16, 2, 256, 2048], P('gx', 'gy'), may hold values from -6 to 6
- tensors: bfloat16 [16, 2, 9, 64, 2048], P('gx', 'gy'), may hold values from -6 to 6
- vectors: float32 [16, 2, 3, 2048], P('gx', 'gy'), may hold values from -1 to 1
- species: int32 [16, 2, 2048], P('gx', 'gy'), may hold values from 0 to 3
- species_table: float32 [256, 4], replicated, may hold values from -3 to 3
- reverse: int32 [16, 2, 2048], P('gx', 'gy'), may hold values from 0 to 2559, as said below
- send_index: int32 [16, 2, 8, 64], P('gx', 'gy'), may hold values from 0 to 2047, as said below
- counts: int32 [16, 2, 8], P('gx', 'gy'), may hold values from 32 to 64, as said below
- w_query: bfloat16 [256, 256], replicated, may hold values from -0.375 to 0.375
- w_key: bfloat16 [256, 256], replicated, may hold values from -0.375 to 0.375
- w_value: bfloat16 [256, 256], replicated, may hold values from -0.375 to 0.375
- w_output: bfloat16 [256, 256], replicated, may hold values from -0.375 to 0.375
- w_invariant: bfloat16 [256, 192], replicated, may hold values from -0.4375 to 0.4375
- w_message: bfloat16 [256, 256], replicated, may hold values from -0.375 to 0.375
- w_gate: bfloat16 [192, 256], replicated, may hold values from -0.375 to 0.375
- w_radial: bfloat16 [192, 256], replicated, may hold values from -0.375 to 0.375
- w_mixing: bfloat16 [64, 64], replicated, may hold values from -0.75 to 0.75
- w_expand: bfloat16 [512, 256], replicated, may hold values from -0.375 to 0.375
- w_reverse: bfloat16 [512, 256], replicated, may hold values from -0.375 to 0.375
- w_contract: bfloat16 [256, 512], replicated, may hold values from -0.25 to 0.25
Outputs:
- new_scalars: bfloat16 [16, 2, 256, 2048], P('gx', 'gy')
- new_tensors: bfloat16 [16, 2, 9, 64, 2048], P('gx', 'gy')
The draws below stay inside these ranges and needn't reach their ends.
Inputs may be any that keep to these rules, and one draw needn't show every extreme that they name: counts[p] of a domain equals the count of its partner in direction p toward it (the opposite direction); some domain has 64 live slots toward some partner in every direction. `send_index`: live slots of a domain name distinct edges; slots at or above the count hold 0. The edge in live slot s of block p has as reverse slot s of the block received in the opposite direction; every live received slot is named by exactly one edge, no empty slot is named, and the other edges are paired among themselves (at most one edge of a domain is its own reverse).
All inputs are finite; a program needn't handle non-finite values.
Results may differ from the reference program's by a relative error of at most 0.01.
Values may be sent and summed in bfloat16 or wider, within the bound.
No kernel may reach another device: no remote copies, remote signals or barrier semaphores. Data moves between devices by JAX's collectives and lax.ppermute only.
A program may use at most 64 MiB of HBM per device.

```python
import math
import jax
import jax.numpy as jnp
from jax import lax

C = 256
MUL = 64
FFN = 512
HEADS = 8
E_DEV = 2048
BLOCK = 64
DOM_X = 16
DOM_Y = 2


def boundary_plan(key):
    base = jax.random.fold_in(key, 11)
    key_count, key_perm = jax.random.split(base)
    halves = jax.random.randint(key_count, (DOM_X, DOM_Y, 4), BLOCK // 2, BLOCK + 1).astype(jnp.int32)
    halves = halves.at[0, 0, :].set(BLOCK)
    forward_ids = (0, 2, 4, 5)
    opposite_ids = (1, 3, 7, 6)
    steps_list = ((1, 0), (0, 1), (1, 1), (1, -1))
    columns = [None] * 8
    for number in range(4):
        step_x, step_y = steps_list[number]
        columns[forward_ids[number]] = halves[..., number]
        columns[opposite_ids[number]] = jnp.roll(halves[..., number], (step_x, step_y), axis=(0, 1))
    counts = jnp.stack(columns, axis=-1).astype(jnp.int32)
    keys = jax.random.split(key_perm, DOM_X * DOM_Y)
    perms = jax.vmap(lambda single: jax.random.permutation(single, E_DEV))(keys).astype(jnp.int32).reshape(DOM_X, DOM_Y, E_DEV)
    ends = jnp.cumsum(counts, axis=-1).astype(jnp.int32)
    starts = ends - counts
    slot_ids = jnp.arange(BLOCK, dtype=jnp.int32)
    positions = starts[..., None] + slot_ids
    live_slots = slot_ids < counts[..., None]
    picked = jnp.take_along_axis(perms, positions.reshape(DOM_X, DOM_Y, 8 * BLOCK), axis=-1).reshape(DOM_X, DOM_Y, 8, BLOCK)
    send_index = jnp.where(live_slots, picked, 0).astype(jnp.int32)
    ranks = jnp.arange(E_DEV, dtype=jnp.int32)
    total = ends[..., 7:8]
    rest = ranks - total
    partner_rank = total + rest + 1 - 2 * (rest % 2)
    partner_rank = jnp.where(partner_rank >= E_DEV, ranks, partner_rank)
    partner_rank = jnp.clip(partner_rank, 0, E_DEV - 1).astype(jnp.int32)
    interior_rev = jnp.take_along_axis(perms, partner_rank, axis=-1)
    direction = jnp.minimum(jnp.sum((ranks[..., None] >= ends[..., None, :]).astype(jnp.int32), axis=-1), 7).astype(jnp.int32)
    opposite_table = jnp.array([1, 0, 3, 2, 7, 6, 5, 4], dtype=jnp.int32)
    opposite = opposite_table[direction]
    within = ranks - jnp.take_along_axis(starts, direction, axis=-1)
    boundary_rev = E_DEV + opposite * BLOCK + within
    chosen = jnp.where(ranks < total, boundary_rev, interior_rev).astype(jnp.int32)
    flat_perm = perms.reshape(DOM_X * DOM_Y, E_DEV)
    flat_chosen = chosen.reshape(DOM_X * DOM_Y, E_DEV)
    reverse = jax.vmap(lambda order_ids, entries: jnp.zeros((E_DEV,), jnp.int32).at[order_ids].set(entries))(flat_perm, flat_chosen)
    return (counts, send_index, reverse.reshape(DOM_X, DOM_Y, E_DEV).astype(jnp.int32))


def draw_counts(key, part):
    return boundary_plan(key)[0]


def draw_send_index(key, part):
    return boundary_plan(key)[1]


def draw_reverse(key, part):
    return boundary_plan(key)[2]


def touch_ends(drawn, own_key, least, largest):
    extent = drawn.shape
    place = [jax.random.randint(jax.random.fold_in(own_key, axis), (), 0, extent[axis]) for axis in range(len(extent))]
    drawn = drawn.at[tuple(place)].set(least)
    longest = extent.index(max(extent))
    place[longest] = (place[longest] + 1) % extent[longest]
    return drawn.at[tuple(place)].set(largest)


def block_scale(stream_key, extent, pieces, low, high):
    def one(axis_at, shards_of):
        heights = jax.random.uniform(jax.random.fold_in(jax.random.fold_in(stream_key, 6), axis_at), (shards_of,), jnp.float32, low / len(pieces), high / len(pieces))
        return jnp.repeat(jnp.exp(heights), extent[axis_at] // shards_of).reshape((-1,) + (1,) * (len(extent) - axis_at - 1))

    loudness = one(*pieces[0])
    for cut in pieces[1:]:
        loudness = loudness * one(*cut)
    return loudness


def normal_values(rng, extent, scale, most, pieces=(), kind=jnp.bfloat16):
    values = jax.random.normal(rng, extent, jnp.float32) * scale
    if len(pieces) > 0:
        values = block_scale(rng, extent, pieces, -0.22, 0.18) * values
    return jnp.clip(values, min=-most, max=most).astype(kind)


def setup_inputs(seed: int = 0) -> dict:
    key_list = jax.random.split(jax.random.key(seed), 21)
    return {
        "scalars": normal_values(key_list[0], (DOM_X, DOM_Y, C, E_DEV), 1.0, 6.0, ((0, 16), (1, 2))),
        "tensors": normal_values(key_list[1], (DOM_X, DOM_Y, 9, MUL, E_DEV), 1.0, 6.0, ((0, 16), (1, 2))),
        "vectors": jnp.clip(jax.random.uniform(key_list[2], (DOM_X, DOM_Y, 3, E_DEV), jnp.float32, -1.0, 1.0) * block_scale(key_list[2], (DOM_X, DOM_Y, 3, E_DEV), ((0, 16), (1, 2)), -0.4, 0.0), -1.0, 1.0),
        "species": touch_ends(jax.random.randint(key_list[3], (DOM_X, DOM_Y, E_DEV), 0, 4), jax.random.fold_in(key_list[3], 1), 0, 3).astype(jnp.int32),
        "species_table": normal_values(key_list[4], (C, 4), 0.5, 3.0, (), jnp.float32),
        "reverse": draw_reverse(jax.random.fold_in(key_list[20], 71), 0),
        "send_index": draw_send_index(jax.random.fold_in(key_list[20], 71), 0),
        "counts": draw_counts(jax.random.fold_in(key_list[20], 71), 0),
        "w_query": normal_values(key_list[8], (C, C), C ** -0.5, 0.375),
        "w_key": normal_values(key_list[9], (C, C), C ** -0.5, 0.375),
        "w_value": normal_values(key_list[10], (C, C), C ** -0.5, 0.375),
        "w_output": normal_values(key_list[11], (C, C), C ** -0.5, 0.375),
        "w_invariant": normal_values(key_list[12], (C, 3 * MUL), (3 * MUL) ** -0.5, 0.4375),
        "w_message": normal_values(key_list[13], (C, C), C ** -0.5, 0.375),
        "w_gate": normal_values(key_list[14], (3 * MUL, C), C ** -0.5, 0.375),
        "w_radial": normal_values(key_list[15], (3 * MUL, C), C ** -0.5, 0.375),
        "w_mixing": normal_values(key_list[16], (MUL, MUL), MUL ** -0.5, 0.75),
        "w_expand": normal_values(key_list[17], (FFN, C), C ** -0.5, 0.375),
        "w_reverse": normal_values(key_list[18], (FFN, C), C ** -0.5, 0.375),
        "w_contract": normal_values(key_list[19], (C, FFN), FFN ** -0.5, 0.25),
    }


DIRECTIONS = ((1, 0), (-1, 0), (0, 1), (0, -1), (1, 1), (1, -1), (-1, 1), (-1, -1))

def solid_harmonics(vectors):
    xcoord, ycoord, zcoord = (vectors[0], vectors[1], vectors[2])
    radius_sq = xcoord * xcoord + ycoord * ycoord + zcoord * zcoord
    root_three = math.sqrt(3.0)
    return jnp.stack([jnp.ones_like(xcoord), xcoord, ycoord, zcoord, root_three * xcoord * ycoord, root_three * ycoord * zcoord, 0.5 * (3.0 * zcoord * zcoord - radius_sq), root_three * xcoord * zcoord, 0.5 * root_three * (xcoord * xcoord - ycoord * ycoord)])

def by_degree(rows):
    multiplicity, edge_count = (rows.shape[1], rows.shape[2])
    return jnp.concatenate([rows[0:1], jnp.broadcast_to(rows[1:2], (3, multiplicity, edge_count)), jnp.broadcast_to(rows[2:3], (5, multiplicity, edge_count))], axis=0)

def send_blocks(scalars, tensors, send_index, counts):
    edge_count = scalars.shape[1]
    flatten = send_index.reshape(-1)
    picked = jnp.concatenate([jnp.take(scalars, flatten, axis=1), jnp.take(tensors.reshape(-1, edge_count), flatten, axis=1)], axis=0)
    live_slots = (lax.broadcasted_iota(jnp.int32, send_index.shape, 1) < counts[:, None]).reshape(-1)
    return jnp.where(live_slots[None, :], picked, jnp.zeros_like(picked))

def edge_update(scalars, tensors, vectors, species, reverse, received, species_table, weights):
    w_query, w_key, w_value, w_output, w_invariant, w_message, w_gate, w_radial, w_mixing = weights
    channels, edge_count = scalars.shape
    multiplicity = tensors.shape[1]
    table_scalar = jnp.concatenate([scalars, received[:channels]], axis=1)
    table_tensor = jnp.concatenate([tensors.reshape(9 * multiplicity, edge_count), received[channels:]], axis=1)
    scalar_rev = jnp.take(table_scalar, reverse, axis=1)
    tensor_rev = jnp.take(table_tensor, reverse, axis=1).reshape(9, multiplicity, edge_count)
    species_ids = lax.broadcasted_iota(jnp.int32, (species_table.shape[1], edge_count), 0)
    onehot = (species_ids == species[None, :]).astype(jnp.float32)
    embedding = lax.optimization_barrier(jnp.sum(species_table[:, :, None] * onehot[None, :, :], axis=1))
    embedded = (scalars.astype(jnp.float32) + embedding).astype(jnp.bfloat16)
    queries = jnp.dot(w_query, embedded, preferred_element_type=jnp.float32)
    key_rows = jnp.dot(w_key, scalar_rev, preferred_element_type=jnp.float32)
    values = jnp.dot(w_value, scalar_rev, preferred_element_type=jnp.float32)
    head_size = channels // HEADS
    scores = lax.optimization_barrier(jnp.sum((queries * key_rows).reshape(HEADS, head_size, edge_count), axis=1)) / math.sqrt(head_size)
    attention = jax.nn.sigmoid(scores)
    attended = (attention[:, None, :] * values.reshape(HEADS, head_size, edge_count)).reshape(channels, edge_count).astype(jnp.bfloat16)
    product = tensors.astype(jnp.float32) * tensor_rev.astype(jnp.float32)
    invariant = jnp.concatenate([product[0], lax.optimization_barrier(jnp.sum(product[1:4], axis=0)), lax.optimization_barrier(jnp.sum(product[4:9], axis=0))], axis=0).astype(jnp.bfloat16)
    middle = (embedded.astype(jnp.float32) + jnp.dot(w_output, attended, preferred_element_type=jnp.float32) + jnp.dot(w_invariant, invariant, preferred_element_type=jnp.float32)).astype(jnp.bfloat16)
    message = jnp.dot(w_message, middle, preferred_element_type=jnp.float32).astype(jnp.bfloat16)
    slot_count = received.shape[1]
    target = jnp.where(reverse >= edge_count, reverse - edge_count, slot_count).astype(jnp.int32)
    returned = jnp.zeros((channels, slot_count), jnp.bfloat16).at[:, target].add(message, mode='drop')
    tensor_gate = jax.nn.sigmoid(jnp.dot(w_gate, middle, preferred_element_type=jnp.float32)).reshape(3, multiplicity, edge_count)
    radial = jnp.dot(w_radial, middle, preferred_element_type=jnp.float32).reshape(3, multiplicity, edge_count)
    mixed_rev = jnp.einsum('oi,cie->coe', w_mixing.astype(jnp.float32), tensor_rev.astype(jnp.float32))
    harmonic = solid_harmonics(vectors)
    new_tensors = (tensors.astype(jnp.float32) + by_degree(tensor_gate) * mixed_rev + by_degree(radial) * harmonic[:, None, :]).astype(jnp.bfloat16)
    return (middle, message, returned, new_tensors)

def finish(middle, message, reverse, send_index, counts, returns, w_expand, w_reverse, w_contract):
    channels, edge_count = middle.shape
    local_part = jnp.take(message, jnp.minimum(reverse, edge_count - 1), axis=1).astype(jnp.float32)
    local_part = jnp.where((reverse < edge_count)[None, :], local_part, jnp.float32(0.0))
    live_slots = (lax.broadcasted_iota(jnp.int32, send_index.shape, 1) < counts[:, None]).reshape(-1)
    arrived = jnp.where(live_slots[None, :], returns.astype(jnp.float32), jnp.float32(0.0))
    incoming = (local_part + jnp.zeros((channels, edge_count), jnp.float32).at[:, send_index.reshape(-1)].add(arrived)).astype(jnp.bfloat16)
    hidden = jax.nn.silu(jnp.dot(w_expand, middle, preferred_element_type=jnp.float32) + jnp.dot(w_reverse, incoming, preferred_element_type=jnp.float32)).astype(jnp.bfloat16)
    return (middle.astype(jnp.float32) + jnp.dot(w_contract, hidden, preferred_element_type=jnp.float32)).astype(jnp.bfloat16)

def reference(scalars, tensors, vectors, species, species_table, reverse, send_index, counts, w_query, w_key, w_value, w_output, w_invariant, w_message, w_gate, w_radial, w_mixing, w_expand, w_reverse, w_contract):
    extent_x, extent_y = (scalars.shape[0], scalars.shape[1])
    domains = extent_x * extent_y

    def flatten(array):
        return array.reshape((domains,) + array.shape[2:])

    def grid(array):
        return array.reshape((extent_x, extent_y) + array.shape[1:])
    block_width = send_index.shape[-1]
    outgoing = grid(lax.map(lambda packed: send_blocks(*packed), (flatten(scalars), flatten(tensors), flatten(send_index), flatten(counts))))
    received = jnp.concatenate([jnp.roll(outgoing[..., position * block_width:(position + 1) * block_width], (step_x, step_y), axis=(0, 1)) for position, (step_x, step_y) in enumerate(DIRECTIONS)], axis=-1)
    weights = (w_query, w_key, w_value, w_output, w_invariant, w_message, w_gate, w_radial, w_mixing)
    middle, message, returned, new_tensors = lax.map(lambda packed: edge_update(*packed, species_table, weights), (flatten(scalars), flatten(tensors), flatten(vectors), flatten(species), flatten(reverse), flatten(received)))
    returned = grid(returned)
    returns = jnp.concatenate([jnp.roll(returned[..., position * block_width:(position + 1) * block_width], (-step_x, -step_y), axis=(0, 1)) for position, (step_x, step_y) in enumerate(DIRECTIONS)], axis=-1)
    result = lax.map(lambda packed: finish(*packed, w_expand, w_reverse, w_contract), (middle, message, flatten(reverse), flatten(send_index), flatten(counts), flatten(returns)))
    return (result.reshape(scalars.shape), new_tensors.reshape(tensors.shape))
```

```python
import functools
import math

import jax
import jax.numpy as jnp
from jax import lax
from jax.experimental import pallas as pl
from jax.experimental.pallas import tpu as pltpu
from jax.sharding import PartitionSpec as P

HEADS = 8
DIRECTIONS = ((1, 0), (-1, 0), (0, 1), (0, -1), (1, 1), (1, -1), (-1, 1), (-1, -1))
OPPOSITE = tuple(DIRECTIONS.index((-dx, -dy)) for dx, dy in DIRECTIONS)
EXTRA = 16
BF16 = jnp.bfloat16
F32 = jnp.float32


def plan_groups(gx, gy):
    groups = {}
    for p in (4, 5, 7, 6, 0, 1, 2, 3):
        dx, dy = DIRECTIONS[p]
        pairs = tuple(
            (a * gy + b, ((a + dx) % gx) * gy + (b + dy) % gy)
            for a in range(gx)
            for b in range(gy)
        )
        groups.setdefault(pairs, []).append(p)
    return [(pairs, tuple(members)) for pairs, members in groups.items()]


def mm(a, b):
    return jnp.dot(a, b, preferred_element_type=F32)


def embed(own, table, species):
    picked = table[:, 3:4]
    for j in (2, 1, 0):
        picked = jnp.where(species == j, table[:, j : j + 1], picked)
    return (own.astype(F32) + picked).astype(BF16)


def attend(queries, keys, values):
    channels, width = queries.shape
    size = channels // HEADS
    product = queries * keys
    parts = []
    for h in range(HEADS):
        rows = slice(h * size, (h + 1) * size)
        score = jnp.sum(product[rows], axis=0, keepdims=True) * (1.0 / math.sqrt(size))
        parts.append(jax.nn.sigmoid(score) * values[rows])
    return jnp.concatenate(parts, axis=0).astype(BF16)


def invariants(own, rev):
    product = own.astype(F32) * rev.astype(F32)
    return jnp.concatenate(
        [
            product[0],
            product[1] + product[2] + product[3],
            product[4] + product[5] + product[6] + product[7] + product[8],
        ],
        axis=0,
    ).astype(BF16)


def harmonics(vectors):
    x, y, z = vectors[0:1], vectors[1:2], vectors[2:3]
    r2 = x * x + y * y + z * z
    root = math.sqrt(3.0)
    return (
        None,
        x,
        y,
        z,
        root * x * y,
        root * y * z,
        0.5 * (3.0 * z * z - r2),
        root * x * z,
        0.5 * root * (x * x - y * y),
    )


def update_tensors(own, rev, gate, radial, mixing, vectors):
    m = own.shape[1]
    harmonic = harmonics(vectors)
    for k in range(9):
        degree = 0 if k == 0 else (1 if k < 4 else 2)
        rows = slice(degree * m, (degree + 1) * m)
        mixed = mm(mixing, rev[k])
        tail = radial[rows] if harmonic[k] is None else radial[rows] * harmonic[k]
        yield k, (own[k].astype(F32) + gate[rows] * mixed + tail).astype(BF16)


def feed_forward(middle, incoming, w_expand, w_reverse, w_contract):
    v = mm(w_expand, middle) + mm(w_reverse, incoming)
    hidden = (v * jax.nn.sigmoid(v)).astype(BF16)
    return (middle.astype(F32) + mm(w_contract, hidden)).astype(BF16)


def prepare_kernel(
    groups, scalars, tensors, vectors, species, send_index, counts, own, where, *rest
):
    sends, (s_buf, t_buf, sem) = rest[: len(groups)], rest[len(groups) :]
    copies = [
        pltpu.make_async_copy(scalars.at[0, 0], s_buf, sem.at[0]),
        pltpu.make_async_copy(tensors.at[0, 0], t_buf, sem.at[1]),
    ]
    for copy in copies:
        copy.start()
    channels, edges = s_buf.shape
    block = send_index.shape[-1]
    features = channels + t_buf.shape[0] * t_buf.shape[1]
    lane = lax.broadcasted_iota(jnp.int32, (1, block), 1)
    order = [p for _, members in groups for p in members]
    index = jnp.concatenate(
        [jnp.where(lane < counts[0, 0, p], send_index[0, 0, p : p + 1, :], -1) for p in order],
        axis=1,
    )
    slots = index.shape[1]
    onehot = (lax.broadcasted_iota(jnp.int32, (edges, slots), 0) == index).astype(BF16)
    vec = vectors[0, 0]
    high = vec.astype(BF16)
    left = vec - high.astype(F32)
    mid = left.astype(BF16)
    low = (left - mid.astype(F32)).astype(BF16)
    extra = jnp.concatenate(
        [
            jnp.broadcast_to(species[0].astype(F32), (7, edges)),
            high.astype(F32),
            mid.astype(F32),
            low.astype(F32),
        ],
        axis=0,
    ).astype(BF16)
    extra = mm(extra, onehot)
    where[0:3, :] = extra[7:10] + extra[10:13] + extra[13:16]
    where[3:8, :] = jnp.zeros((5, slots), F32)
    own[features:, :] = jnp.broadcast_to(extra[0:1], (EXTRA, slots)).astype(BF16)
    copies[0].wait()
    own[:channels, :] = mm(s_buf[...], onehot).astype(BF16)
    copies[1].wait()
    own[channels:features, :] = mm(
        t_buf[...].reshape(features - channels, edges), onehot
    ).astype(BF16)
    at = 0
    for send, (_, members) in zip(sends, groups):
        width = len(members) * block
        if width % 128 == 0:
            send[...] = own[:, at : at + width]
        else:
            half = features // 2
            piece = own[:, at : at + width]
            send[:half, :] = jnp.concatenate([piece[:half], piece[half:features]], axis=1)
            send[half:, :] = jnp.concatenate([piece[features:], piece[features:]], axis=1)
        at += width


def interior_kernel(
    scalars,
    tensors,
    vectors,
    species,
    reverse,
    table,
    w_query,
    w_key,
    w_value,
    w_output,
    w_invariant,
    w_message,
    w_gate,
    w_radial,
    w_mixing,
    middle_out,
    message_out,
    tensors_out,
):
    edges = scalars.shape[-1]
    width = reverse.shape[-1]
    channels = scalars.shape[2]
    here = pl.ds(pl.multiple_of(pl.program_id(0) * width, 128), width)
    comps, m = tensors.shape[2:4]
    onehot = (lax.broadcasted_iota(jnp.int32, (edges, width), 0) == reverse[0]).astype(BF16)
    s_rev = mm(scalars[0, 0], onehot).astype(BF16)
    t_rev = (
        mm(tensors[0, 0].reshape(comps * m, edges), onehot).astype(BF16).reshape(comps, m, width)
    )
    embedded = embed(scalars[0, 0, :, here], table[...], species[0])
    attended = attend(mm(w_query[...], embedded), mm(w_key[...], s_rev), mm(w_value[...], s_rev))
    own_t = tensors[0, 0, :, :, here]
    middle = (
        embedded.astype(F32)
        + mm(w_output[...], attended)
        + mm(w_invariant[...], invariants(own_t, t_rev))
    ).astype(BF16)
    middle_out[...] = middle
    message_out[...] = mm(w_message[...], middle).astype(BF16)
    gate = jax.nn.sigmoid(mm(w_gate[...], middle))
    radial = mm(w_radial[...], middle)
    for k, new in update_tensors(own_t, t_rev, gate, radial, w_mixing[...], vectors[0, 0]):
        tensors_out[k] = new


def incoming_kernel(message, middle, reverse, w_expand, w_reverse, w_contract, scalars_out):
    edges = message.shape[1]
    width = reverse.shape[-1]
    onehot = (lax.broadcasted_iota(jnp.int32, (edges, width), 0) == reverse[0]).astype(BF16)
    incoming = mm(message[...], onehot).astype(BF16)
    scalars_out[...] = feed_forward(
        middle[...], incoming, w_expand[...], w_reverse[...], w_contract[...]
    )


def boundary_kernel(groups, block, edges, *refs):
    count = len(groups)
    received, refs = refs[:count], refs[count:]
    (
        own,
        where,
        reverse,
        scalars_in,
        tensors_in,
        table,
        w_query,
        w_key,
        w_value,
        w_output,
        w_invariant,
        w_message,
        w_gate,
        w_radial,
        w_mixing,
        w_expand,
        w_reverse,
        w_contract,
        scalars_out,
        tensors_out,
        s_new,
        t_new,
        far,
    ) = refs
    order = [p for _, members in groups for p in members]
    comps, m = tensors_in.shape[:2]
    channels = scalars_in.shape[0]
    features = channels + comps * m
    slots = own.shape[1]

    @pl.when(pl.program_id(0) == 0)
    def _():
        place = {}
        for g, (_, members) in enumerate(groups):
            for n, p in enumerate(members):
                place[p] = (g, n, len(members))

        def block_of(p):
            g, n, total = place[p]
            if (total * block) % 128 == 0:
                return received[g][:, n * block : (n + 1) * block]
            half = features // 2
            piece = received[g]
            return jnp.concatenate(
                [piece[:half, :block], piece[:half, block:], piece[half:, :block]], axis=0
            )

        per = 128 // block
        for j in range(0, len(order), per):
            far[:, j * block : (j + per) * block] = jnp.concatenate(
                [block_of(OPPOSITE[p]) for p in order[j : j + per]], axis=1
            )
        s_own, s_far = own[:channels, :], far[:channels, :]
        t_own = own[channels:features, :].reshape(comps, m, slots)
        t_far = far[channels:features, :].reshape(comps, m, slots)
        e_own = embed(s_own, table[...], own[features : features + 1, :].astype(F32))
        e_far = embed(s_far, table[...], far[features : features + 1, :].astype(F32))
        shared = mm(w_invariant[...], invariants(t_own, t_far))
        a_own = attend(mm(w_query[...], e_own), mm(w_key[...], s_far), mm(w_value[...], s_far))
        a_far = attend(mm(w_query[...], e_far), mm(w_key[...], s_own), mm(w_value[...], s_own))
        middle = (e_own.astype(F32) + mm(w_output[...], a_own) + shared).astype(BF16)
        middle_far = (e_far.astype(F32) + mm(w_output[...], a_far) + shared).astype(BF16)
        incoming = mm(w_message[...], middle_far).astype(BF16)
        s_new[...] = feed_forward(middle, incoming, w_expand[...], w_reverse[...], w_contract[...])
        gate = jax.nn.sigmoid(mm(w_gate[...], middle))
        radial = mm(w_radial[...], middle)
        for k, new in update_tensors(t_own, t_far, gate, radial, w_mixing[...], where[...]):
            t_new[k * m : (k + 1) * m, :] = new

    target = reverse[0] - edges
    width = target.shape[1]
    rows = lax.broadcasted_iota(jnp.int32, (block, width), 0)
    onehot = jnp.concatenate(
        [(rows + OPPOSITE[p] * block == target).astype(F32) for p in order], axis=0
    ).astype(BF16)
    crosses = target >= 0
    scalars_out[0, 0] = jnp.where(
        crosses, mm(s_new[...], onehot), scalars_in[...].astype(F32)
    ).astype(BF16)
    merged = mm(t_new[...], onehot)
    for k in range(comps):
        tensors_out[0, 0, k] = jnp.where(
            crosses, merged[k * m : (k + 1) * m], tensors_in[k].astype(F32)
        ).astype(BF16)


def whole(*shape):
    return pl.BlockSpec(shape, lambda *_: (0,) * len(shape))


def per_device(gx, gy, *args):
    (
        scalars,
        tensors,
        vectors,
        species,
        table,
        reverse,
        send_index,
        counts,
        w_query,
        w_key,
        w_value,
        w_output,
        w_invariant,
        w_message,
        w_gate,
        w_radial,
        w_mixing,
        w_expand,
        w_reverse,
        w_contract,
    ) = args
    groups = plan_groups(gx, gy)
    _, _, channels, edges = scalars.shape
    comps, m = tensors.shape[2:4]
    features = channels + comps * m
    block = send_index.shape[-1]
    slots = len(DIRECTIONS) * block
    vmem = pl.BlockSpec(memory_space=pltpu.VMEM)
    limit = pltpu.CompilerParams(vmem_limit_bytes=56 * 2**20)

    def send_shape(members):
        width = len(members) * block
        if width % 128 == 0:
            return (features + EXTRA, width)
        return (features // 2 + EXTRA, 2 * width)

    own, where, *sends = pl.pallas_call(
        functools.partial(prepare_kernel, groups),
        in_specs=[
            pl.BlockSpec(memory_space=pl.ANY),
            pl.BlockSpec(memory_space=pl.ANY),
            vmem,
            vmem,
            vmem,
            pl.BlockSpec(memory_space=pltpu.SMEM),
        ],
        out_specs=[vmem] * (2 + len(groups)),
        out_shape=[
            jax.ShapeDtypeStruct((features + EXTRA, slots), BF16),
            jax.ShapeDtypeStruct((8, slots), F32),
        ]
        + [jax.ShapeDtypeStruct(send_shape(members), BF16) for _, members in groups],
        scratch_shapes=[
            pltpu.VMEM((channels, edges), BF16),
            pltpu.VMEM((comps, m, edges), BF16),
            pltpu.SemaphoreType.DMA((2,)),
        ],
        compiler_params=limit,
        name="prepare",
    )(scalars, tensors, vectors, species, send_index, counts)

    received = [
        lax.ppermute(send, ("gx", "gy"), pairs) for send, (pairs, _) in zip(sends, groups)
    ]

    width = 512
    steps = edges // width
    row = pl.BlockSpec((1, 1, width), lambda i: (0, 0, i))
    flat = pl.BlockSpec((channels, width), lambda i: (0, i))
    stack = pl.BlockSpec((comps, m, width), lambda i: (0, 0, i))
    first_weights = (w_query, w_key, w_value, w_output, w_invariant, w_message, w_gate, w_radial, w_mixing)
    last_weights = (w_expand, w_reverse, w_contract)
    middle, message, t_inside = pl.pallas_call(
        interior_kernel,
        grid=(steps,),
        in_specs=[
            whole(*scalars.shape),
            whole(*tensors.shape),
            pl.BlockSpec((1, 1, 3, width), lambda i: (0, 0, 0, i)),
            row,
            row,
            whole(*table.shape),
        ]
        + [whole(*w.shape) for w in first_weights],
        out_specs=[flat, flat, stack],
        out_shape=[
            jax.ShapeDtypeStruct((channels, edges), BF16),
            jax.ShapeDtypeStruct((channels, edges), BF16),
            jax.ShapeDtypeStruct((comps, m, edges), BF16),
        ],
        compiler_params=limit,
        cost_estimate=pl.CostEstimate(
            flops=2 * edges * edges * features, bytes_accessed=4 * edges * features, transcendentals=0
        ),
        name="interior",
    )(scalars, tensors, vectors, species, reverse, table, *first_weights)
    s_inside = pl.pallas_call(
        incoming_kernel,
        grid=(steps,),
        in_specs=[whole(channels, edges), flat, row] + [whole(*w.shape) for w in last_weights],
        out_specs=flat,
        out_shape=jax.ShapeDtypeStruct((channels, edges), BF16),
        compiler_params=limit,
        cost_estimate=pl.CostEstimate(
            flops=4 * edges * edges * channels, bytes_accessed=8 * edges * channels, transcendentals=0
        ),
        name="incoming",
    )(message, middle, reverse, *last_weights)

    return pl.pallas_call(
        functools.partial(boundary_kernel, groups, block, edges),
        grid=(steps,),
        in_specs=[whole(*r.shape) for r in received]
        + [whole(*own.shape), whole(*where.shape), row, flat, stack, whole(*table.shape)]
        + [whole(*w.shape) for w in first_weights + last_weights],
        out_specs=[
            pl.BlockSpec((1, 1, channels, width), lambda i: (0, 0, 0, i)),
            pl.BlockSpec((1, 1, comps, m, width), lambda i: (0, 0, 0, 0, i)),
        ],
        out_shape=[
            jax.ShapeDtypeStruct(scalars.shape, BF16),
            jax.ShapeDtypeStruct(tensors.shape, BF16),
        ],
        scratch_shapes=[
            pltpu.VMEM((channels, slots), BF16),
            pltpu.VMEM((comps * m, slots), BF16),
            pltpu.VMEM((features + EXTRA, slots), BF16),
        ],
        compiler_params=limit,
        cost_estimate=pl.CostEstimate(
            flops=2 * edges * slots * features, bytes_accessed=8 * edges * features, transcendentals=0
        ),
        name="boundary",
    )(*received, own, where, reverse, s_inside, t_inside, table, *first_weights, *last_weights)


def solution(mesh):
    return jax.shard_map(
        functools.partial(per_device, mesh.shape["gx"], mesh.shape["gy"]),
        mesh=mesh,
        in_specs=(
            P("gx", "gy", None, None),
            P("gx", "gy", None, None, None),
            P("gx", "gy", None, None),
            P("gx", "gy", None),
            P(),
            P("gx", "gy", None),
            P("gx", "gy", None, None),
            P("gx", "gy", None),
        )
        + (P(),) * 12,
        out_specs=(P("gx", "gy", None, None), P("gx", "gy", None, None, None)),
        check_vma=False,
    )
```

```python
import functools
import math

import jax
import jax.numpy as jnp
from jax import lax
from jax.experimental import pallas as pl
from jax.experimental.pallas import tpu as pltpu
from jax.sharding import PartitionSpec as P

HEADS = 8
DIRECTIONS = ((1, 0), (-1, 0), (0, 1), (0, -1), (1, 1), (1, -1), (-1, 1), (-1, -1))
OPPOSITE = tuple(DIRECTIONS.index((-dx, -dy)) for dx, dy in DIRECTIONS)
EXTRA = 16
BF16 = jnp.bfloat16
F32 = jnp.float32


def plan_groups(gx, gy):
    groups = {}
    for p in (4, 5, 7, 6, 0, 1, 2, 3):
        dx, dy = DIRECTIONS[p]
        pairs = tuple(
            (a * gy + b, ((a + dx) % gx) * gy + (b + dy) % gy)
            for a in range(gx)
            for b in range(gy)
        )
        groups.setdefault(pairs, []).append(p)
    return [(pairs, tuple(members)) for pairs, members in groups.items()]


def mm(a, b):
    return jnp.dot(a, b, preferred_element_type=F32)


def nt(a, b):
    return lax.dot_general(a, b, (((1,), (1,)), ((), ())), preferred_element_type=F32)


def eye(n):
    rows = lax.broadcasted_iota(jnp.int32, (n, n), 0)
    return (rows == lax.broadcasted_iota(jnp.int32, (n, n), 1)).astype(BF16)


def embed(own, table, species):
    picked = table[:, 3:4]
    for j in (2, 1, 0):
        picked = jnp.where(species == j, table[:, j : j + 1], picked)
    return (own.astype(F32) + picked).astype(BF16)


def attend(queries, keys, values):
    channels, width = queries.shape
    size = channels // HEADS
    product = queries * keys
    parts = []
    for h in range(HEADS):
        rows = slice(h * size, (h + 1) * size)
        score = jnp.sum(product[rows], axis=0, keepdims=True) * (1.0 / math.sqrt(size))
        parts.append(jax.nn.sigmoid(score) * values[rows])
    return jnp.concatenate(parts, axis=0).astype(BF16)


def invariants(own, rev):
    product = [own[k].astype(F32) * rev[k].astype(F32) for k in range(9)]
    return jnp.concatenate(
        [
            product[0],
            product[1] + product[2] + product[3],
            product[4] + product[5] + product[6] + product[7] + product[8],
        ],
        axis=0,
    ).astype(BF16)


def harmonics(vectors):
    x, y, z = vectors[0:1], vectors[1:2], vectors[2:3]
    r2 = x * x + y * y + z * z
    root = math.sqrt(3.0)
    return (
        None,
        x,
        y,
        z,
        root * x * y,
        root * y * z,
        0.5 * (3.0 * z * z - r2),
        root * x * z,
        0.5 * root * (x * x - y * y),
    )


def update_tensors(own, mixed, gate, radial, vectors):
    m = own[0].shape[0]
    harmonic = harmonics(vectors)
    for k in range(9):
        degree = 0 if k == 0 else (1 if k < 4 else 2)
        rows = slice(degree * m, (degree + 1) * m)
        tail = radial[rows] if harmonic[k] is None else radial[rows] * harmonic[k]
        yield k, (own[k].astype(F32) + gate[rows] * mixed[k] + tail).astype(BF16)


def contract(middle, v, w_contract):
    hidden = (v * jax.nn.sigmoid(v)).astype(BF16)
    return (middle.astype(F32) + mm(w_contract, hidden)).astype(BF16)


def prepare_kernel(
    groups, scalars, tensors, vectors, species, reverse, send_index, counts, own, where, rows, *rest
):
    sends, (s_buf, t_buf, sem) = rest[: len(groups)], rest[len(groups) :]
    copies = [
        pltpu.make_async_copy(scalars.at[0, 0], s_buf, sem.at[0]),
        pltpu.make_async_copy(tensors.at[0, 0], t_buf, sem.at[1]),
    ]
    for copy in copies:
        copy.start()
    channels, edges = s_buf.shape
    block = send_index.shape[-1]
    features = channels + t_buf.shape[0] * t_buf.shape[1]
    lane = lax.broadcasted_iota(jnp.int32, (1, block), 1)
    order = [p for _, members in groups for p in members]
    index = jnp.concatenate(
        [jnp.where(lane < counts[0, 0, p], send_index[0, 0, p : p + 1, :], -1) for p in order],
        axis=1,
    )
    slots = index.shape[1]
    onehot = (lax.broadcasted_iota(jnp.int32, (edges, slots), 0) == index).astype(BF16)
    near = jnp.minimum(reverse[0], edges - 1) * 8
    rows[...] = jnp.concatenate(
        [near[:, j * 128 : (j + 1) * 128] for j in range(edges // 128)], axis=0
    )
    vec = jnp.concatenate([vectors[0, j] for j in range(3)], axis=0)
    high = vec.astype(BF16)
    left = vec - high.astype(F32)
    mid = left.astype(BF16)
    low = (left - mid.astype(F32)).astype(BF16)
    extra = jnp.concatenate(
        [
            jnp.broadcast_to(species[0].astype(F32), (7, edges)),
            high.astype(F32),
            mid.astype(F32),
            low.astype(F32),
        ],
        axis=0,
    ).astype(BF16)
    extra = mm(extra, onehot)
    where[0:3, :] = extra[7:10] + extra[10:13] + extra[13:16]
    where[3:8, :] = jnp.zeros((5, slots), F32)
    own[features:, :] = jnp.broadcast_to(extra[0:1], (EXTRA, slots)).astype(BF16)
    copies[0].wait()
    own[:channels, :] = mm(s_buf[...], onehot).astype(BF16)
    copies[1].wait()
    own[channels:features, :] = mm(
        t_buf[...].reshape(features - channels, edges), onehot
    ).astype(BF16)
    at = 0
    for send, (_, members) in zip(sends, groups):
        width = len(members) * block
        if width % 128 == 0:
            send[...] = own[:, at : at + width]
        else:
            half = features // 2
            piece = own[:, at : at + width]
            send[:half, :] = jnp.concatenate([piece[:half], piece[half:features]], axis=1)
            send[half:, :] = jnp.concatenate([piece[features:], piece[features:]], axis=1)
        at += width


def copy_rows(table, rows, first, gathered, width):
    per = rows.shape[1]

    def body(i, _):
        for u in range(per):
            source = pl.ds(pl.multiple_of(rows[first + i, u], 8), 8)
            gathered[pl.ds(pl.multiple_of(i * (per * 8) + u * 8, 8), 8), :] = table[source, :]
        return 0

    lax.fori_loop(0, width // per, body, 0)


def interior_kernel(
    scalars,
    tensors,
    vectors,
    species,
    rows,
    table,
    w_query,
    w_key,
    w_value,
    w_output,
    w_invariant,
    w_message,
    w_gate,
    w_radial,
    w_mixing,
    middle_out,
    message_out,
    tensors_out,
    edge_rows,
    gathered,
    pair_mix,
    w_shared,
):
    edges = scalars.shape[-1]
    width = species.shape[-1]
    channels = scalars.shape[2]
    comps, m = tensors.shape[2:4]
    step = pl.program_id(0)
    here = pl.ds(pl.multiple_of(step * width, 128), width)
    pairs = [(k, k + 1) for k in range(0, comps - 1, 2)] + [(comps - 2, comps - 1)]

    @pl.when(step == 0)
    def _():
        unit = eye(256)
        half = eye(128)
        mixing = w_mixing[...].astype(F32)
        zero = jnp.zeros((m, m), F32)
        pair_mix[...] = jnp.concatenate(
            [
                half.astype(F32),
                jnp.concatenate([mixing, zero], axis=1),
                jnp.concatenate([zero, mixing], axis=1),
            ],
            axis=0,
        ).astype(BF16)
        w_shared[...] = nt(unit, w_invariant[...]).astype(BF16)
        for at in range(0, edges, 256):
            tile = slice(at, at + 256)
            pieces = [
                scalars[0, 0, c : c + 128, tile] for c in range(0, channels, 128)
            ] + [tensors[0, 0, k : k + 2, :, tile].reshape(2 * m, 256) for k, _ in pairs]
            for j, piece in enumerate(pieces):
                edge_rows[pl.ds(at * 8 + j, 256, stride=8), :] = nt(unit, piece)

    copy_rows(edge_rows, rows, step * (width // rows.shape[1]), gathered, width)

    def feature(j):
        return gathered[pl.ds(j, width, stride=8), :].astype(BF16)

    lead = channels // 128
    s_rev = jnp.concatenate([feature(j) for j in range(lead)], axis=1)
    t_rev, mixed = {}, {}
    for j, (first, second) in enumerate(pairs):
        both = nt(pair_mix[...], feature(lead + j))
        t_rev[first], t_rev[second] = both[:m], both[m : 2 * m]
        mixed[first], mixed[second] = both[2 * m : 3 * m], both[3 * m :]
    embedded = embed(scalars[0, 0, :, here], jnp.transpose(table[...]), species[0])
    attended = attend(mm(w_query[...], embedded), nt(w_key[...], s_rev), nt(w_value[...], s_rev))
    own_t = [tensors[0, 0, k, :, here] for k in range(comps)]
    middle = (
        embedded.astype(F32)
        + mm(w_output[...], attended)
        + mm(w_shared[...], invariants(own_t, t_rev))
    ).astype(BF16)
    middle_out[...] = middle
    message_out[...] = mm(w_message[...], middle).astype(BF16)
    gate = jax.nn.sigmoid(mm(w_gate[...], middle))
    radial = mm(w_radial[...], middle)
    vec = jnp.concatenate([vectors[0, j] for j in range(3)], axis=0)
    for k, new in update_tensors(own_t, mixed, gate, radial, vec):
        tensors_out[k] = new


def incoming_kernel(
    message, middle, rows, w_expand, w_reverse, w_contract, scalars_out, edge_rows, gathered
):
    channels, edges = message.shape
    width = middle.shape[1]
    step = pl.program_id(0)

    @pl.when(step == 0)
    def _():
        unit = eye(256)
        for at in range(0, edges, 256):
            for j in range(channels // 128):
                piece = message[j * 128 : (j + 1) * 128, at : at + 256]
                edge_rows[pl.ds(at * 8 + j, 256, stride=8), :] = nt(unit, piece)

    copy_rows(edge_rows, rows, step * (width // rows.shape[1]), gathered, width)
    incoming = jnp.concatenate(
        [
            gathered[pl.ds(j, width, stride=8), :].astype(BF16)
            for j in range(channels // 128)
        ],
        axis=1,
    )
    v = mm(w_expand[...], middle[...]) + nt(w_reverse[...], incoming)
    scalars_out[...] = contract(middle[...], v, w_contract[...])


def boundary_kernel(groups, block, edges, *refs):
    count = len(groups)
    received, refs = refs[:count], refs[count:]
    (
        own,
        where,
        reverse,
        scalars_in,
        tensors_in,
        table,
        w_query,
        w_key,
        w_value,
        w_output,
        w_invariant,
        w_message,
        w_gate,
        w_radial,
        w_mixing,
        w_expand,
        w_reverse,
        w_contract,
        scalars_out,
        tensors_out,
        s_new,
        t_new,
        far,
    ) = refs
    order = [p for _, members in groups for p in members]
    comps, m = tensors_in.shape[:2]
    channels = scalars_in.shape[0]
    features = channels + comps * m
    slots = own.shape[1]

    @pl.when(pl.program_id(0) == 0)
    def _():
        place = {}
        for g, (_, members) in enumerate(groups):
            for n, p in enumerate(members):
                place[p] = (g, n, len(members))

        def block_of(p):
            g, n, total = place[p]
            if (total * block) % 128 == 0:
                return received[g][:, n * block : (n + 1) * block]
            half = features // 2
            piece = received[g]
            return jnp.concatenate(
                [piece[:half, :block], piece[:half, block:], piece[half:, :block]], axis=0
            )

        per = 128 // block
        for j in range(0, len(order), per):
            far[:, j * block : (j + per) * block] = jnp.concatenate(
                [block_of(OPPOSITE[p]) for p in order[j : j + per]], axis=1
            )
        s_own, s_far = own[:channels, :], far[:channels, :]
        t_own = [own[channels + k * m : channels + (k + 1) * m, :] for k in range(comps)]
        t_far = [far[channels + k * m : channels + (k + 1) * m, :] for k in range(comps)]
        columns = jnp.transpose(table[...])
        e_own = embed(s_own, columns, own[features : features + 1, :].astype(F32))
        e_far = embed(s_far, columns, far[features : features + 1, :].astype(F32))
        w_shared = nt(eye(channels), w_invariant[...]).astype(BF16)
        shared = mm(w_shared, invariants(t_own, t_far))
        a_own = attend(mm(w_query[...], e_own), mm(w_key[...], s_far), mm(w_value[...], s_far))
        a_far = attend(mm(w_query[...], e_far), mm(w_key[...], s_own), mm(w_value[...], s_own))
        middle = (e_own.astype(F32) + mm(w_output[...], a_own) + shared).astype(BF16)
        middle_far = (e_far.astype(F32) + mm(w_output[...], a_far) + shared).astype(BF16)
        incoming = mm(w_message[...], middle_far).astype(BF16)
        v = mm(w_expand[...], middle) + mm(w_reverse[...], incoming)
        s_new[...] = contract(middle, v, w_contract[...])
        gate = jax.nn.sigmoid(mm(w_gate[...], middle))
        radial = mm(w_radial[...], middle)
        mixed = [mm(w_mixing[...], t_far[k]) for k in range(comps)]
        for k, new in update_tensors(t_own, mixed, gate, radial, where[...]):
            t_new[k * m : (k + 1) * m, :] = new

    target = reverse[0] - edges
    width = target.shape[1]
    rows = lax.broadcasted_iota(jnp.int32, (block, width), 0)
    onehot = jnp.concatenate(
        [(rows + OPPOSITE[p] * block == target).astype(F32) for p in order], axis=0
    ).astype(BF16)
    crosses = target >= 0
    scalars_out[0, 0] = jnp.where(
        crosses, mm(s_new[...], onehot), scalars_in[...].astype(F32)
    ).astype(BF16)
    merged = mm(t_new[...], onehot)
    for k in range(comps):
        tensors_out[0, 0, k] = jnp.where(
            crosses, merged[k * m : (k + 1) * m], tensors_in[k].astype(F32)
        ).astype(BF16)


def whole(*shape):
    return pl.BlockSpec(shape, lambda *_: (0,) * len(shape))


def per_device(gx, gy, *args):
    (
        scalars,
        tensors,
        vectors,
        species,
        table,
        reverse,
        send_index,
        counts,
        w_query,
        w_key,
        w_value,
        w_output,
        w_invariant,
        w_message,
        w_gate,
        w_radial,
        w_mixing,
        w_expand,
        w_reverse,
        w_contract,
    ) = args
    groups = plan_groups(gx, gy)
    vectors = jnp.transpose(vectors, (0, 2, 1, 3))
    table = jnp.transpose(table)
    w_invariant = jnp.transpose(w_invariant)
    _, _, channels, edges = scalars.shape
    comps, m = tensors.shape[2:4]
    features = channels + comps * m
    block = send_index.shape[-1]
    slots = len(DIRECTIONS) * block
    vmem = pl.BlockSpec(memory_space=pltpu.VMEM)

    def limit(mebibytes):
        return pltpu.CompilerParams(vmem_limit_bytes=mebibytes * 2**20)


    def send_shape(members):
        width = len(members) * block
        if width % 128 == 0:
            return (features + EXTRA, width)
        return (features // 2 + EXTRA, 2 * width)

    own, where, rows, *sends = pl.pallas_call(
        functools.partial(prepare_kernel, groups),
        in_specs=[
            pl.BlockSpec(memory_space=pl.ANY),
            pl.BlockSpec(memory_space=pl.ANY),
            vmem,
            vmem,
            vmem,
            vmem,
            pl.BlockSpec(memory_space=pltpu.SMEM),
        ],
        out_specs=[vmem] * (3 + len(groups)),
        out_shape=[
            jax.ShapeDtypeStruct((features + EXTRA, slots), BF16),
            jax.ShapeDtypeStruct((8, slots), F32),
            jax.ShapeDtypeStruct((edges // 128, 128), jnp.int32),
        ]
        + [jax.ShapeDtypeStruct(send_shape(members), BF16) for _, members in groups],
        scratch_shapes=[
            pltpu.VMEM((channels, edges), BF16),
            pltpu.VMEM((comps, m, edges), BF16),
            pltpu.SemaphoreType.DMA((2,)),
        ],
        compiler_params=limit(24),
        name="prepare",
    )(scalars, tensors, vectors, species, reverse, send_index, counts)

    received = [None] * len(sends)

    def exchange(chosen):
        for g in chosen:
            received[g] = lax.ppermute(sends[g], ("gx", "gy"), groups[g][0])

    early = range(2)
    late = range(2, len(sends))
    exchange(early)
    width = 512
    steps = edges // width
    row = pl.BlockSpec((1, 1, width), lambda i: (0, 0, i))
    flat = pl.BlockSpec((channels, width), lambda i: (0, i))
    stack = pl.BlockSpec((comps, m, width), lambda i: (0, 0, i))
    first_weights = (w_query, w_key, w_value, w_output, w_invariant, w_message, w_gate, w_radial, w_mixing)
    last_weights = (w_expand, w_reverse, w_contract)
    middle, message, t_inside = pl.pallas_call(
        interior_kernel,
        grid=(steps,),
        in_specs=[
            whole(*scalars.shape),
            whole(*tensors.shape),
            pl.BlockSpec((1, 3, 1, width), lambda i: (0, 0, 0, i)),
            row,
            pl.BlockSpec(memory_space=pltpu.SMEM),
            whole(*table.shape),
        ]
        + [whole(*w.shape) for w in first_weights],
        out_specs=[flat, flat, stack],
        out_shape=[
            jax.ShapeDtypeStruct((channels, edges), BF16),
            jax.ShapeDtypeStruct((channels, edges), BF16),
            jax.ShapeDtypeStruct((comps, m, edges), BF16),
        ],
        scratch_shapes=[
            pltpu.VMEM((edges * 8, 128), F32),
            pltpu.VMEM((width * 8, 128), F32),
            pltpu.VMEM((256, 128), BF16),
            pltpu.VMEM((channels, w_invariant.shape[0]), BF16),
        ],
        compiler_params=limit(36),
        cost_estimate=pl.CostEstimate(
            flops=2 * edges * edges * features, bytes_accessed=4 * edges * features, transcendentals=0
        ),
        name="interior",
    )(scalars, tensors, vectors, species, rows, table, *first_weights)
    *held, middle = lax.optimization_barrier((*[sends[g] for g in late], middle))
    for g, send in zip(late, held):
        sends[g] = send
    exchange(late)
    s_inside = pl.pallas_call(
        incoming_kernel,
        grid=(steps,),
        in_specs=[whole(channels, edges), flat, pl.BlockSpec(memory_space=pltpu.SMEM)]
        + [whole(*w.shape) for w in last_weights],
        out_specs=flat,
        out_shape=jax.ShapeDtypeStruct((channels, edges), BF16),
        scratch_shapes=[
            pltpu.VMEM((edges * 8, 128), F32),
            pltpu.VMEM((width * 8, 128), F32),
        ],
        compiler_params=limit(24),
        cost_estimate=pl.CostEstimate(
            flops=4 * edges * edges * channels, bytes_accessed=8 * edges * channels, transcendentals=0
        ),
        name="incoming",
    )(message, middle, rows, *last_weights)

    return pl.pallas_call(
        functools.partial(boundary_kernel, groups, block, edges),
        grid=(steps,),
        in_specs=[whole(*r.shape) for r in received]
        + [whole(*own.shape), whole(*where.shape), row, flat, stack, whole(*table.shape)]
        + [whole(*w.shape) for w in first_weights + last_weights],
        out_specs=[
            pl.BlockSpec((1, 1, channels, width), lambda i: (0, 0, 0, i)),
            pl.BlockSpec((1, 1, comps, m, width), lambda i: (0, 0, 0, 0, i)),
        ],
        out_shape=[
            jax.ShapeDtypeStruct(scalars.shape, BF16),
            jax.ShapeDtypeStruct(tensors.shape, BF16),
        ],
        scratch_shapes=[
            pltpu.VMEM((channels, slots), BF16),
            pltpu.VMEM((comps * m, slots), BF16),
            pltpu.VMEM((features + EXTRA, slots), BF16),
        ],
        compiler_params=limit(26),
        cost_estimate=pl.CostEstimate(
            flops=2 * edges * slots * features, bytes_accessed=8 * edges * features, transcendentals=0
        ),
        name="boundary",
    )(*received, own, where, reverse, s_inside, t_inside, table, *first_weights, *last_weights)


def solution(mesh):
    return jax.shard_map(
        functools.partial(per_device, mesh.shape["gx"], mesh.shape["gy"]),
        mesh=mesh,
        in_specs=(
            P("gx", "gy", None, None),
            P("gx", "gy", None, None, None),
            P("gx", "gy", None, None),
            P("gx", "gy", None),
            P(),
            P("gx", "gy", None),
            P("gx", "gy", None, None),
            P("gx", "gy", None),
        )
        + (P(),) * 12,
        out_specs=(P("gx", "gy", None, None), P("gx", "gy", None, None, None)),
        check_vma=False,
    )
```

```python
import functools
import math

import jax
import jax.numpy as jnp
from jax import lax
from jax.experimental import pallas as pl
from jax.experimental.pallas import tpu as pltpu
from jax.sharding import PartitionSpec as P


HEADS = 8
DIRECTIONS = ((1, 0), (-1, 0), (0, 1), (0, -1), (1, 1), (1, -1), (-1, 1), (-1, -1))
OPPOSITE = tuple(DIRECTIONS.index((-dx, -dy)) for dx, dy in DIRECTIONS)
EXTRA = 16
BF16 = jnp.bfloat16
F32 = jnp.float32


def ring(gx, gy, dx, dy):
    return tuple(
        (a * gy + b, ((a + dx) % gx) * gy + (b + dy) % gy) for a in range(gx) for b in range(gy)
    )


class Plan:
    def __init__(self, gx, gy):
        self.paired = gx % 2 == 0 and gy == 2
        if self.paired:
            self.orders = ((4, 5, 7, 6, 0, 1, 2, 3), (7, 6, 4, 5, 1, 0, 2, 3))
            self.arrays = ((("wide", 0), ("fold", 4)), (("wide", 2), ("fold", 5)), (("wide", 6),))
            self.facing = (
                (3, 0, 0), (3, 0, 1), (4, 0, 0), (4, 0, 1), (0, 1, 0), (1, 1, 0), (2, 0, 1), (2, 0, 0),
            )
            self.parts = self.arrays + self.arrays[:2]
            even = [(a, a + 1 - 2 * (a % 2)) for a in range(gx)]
            odd = [(a, (a - 1 + 2 * (a % 2)) % gx) for a in range(gx)]
            self.swaps = [
                tuple((a * gy + b, c * gy + b) for a, c in pairs for b in range(gy))
                for pairs in (even, odd)
            ]
            self.across = ring(gx, gy, 0, 1)
        else:
            groups = {}
            for p in (4, 5, 7, 6, 0, 1, 2, 3):
                groups.setdefault(ring(gx, gy, *DIRECTIONS[p]), []).append(p)
            order, self.arrays, place = [], (), {}
            for g, members in enumerate(groups.values()):
                parts = ()
                rest = members
                while rest:
                    taken = 2 if len(rest) > 1 else 1
                    for n, p in enumerate(rest[:taken]):
                        place[p] = (g, len(parts), n)
                    parts += (("wide" if taken == 2 else "fold", len(order)),)
                    order += rest[:taken]
                    rest = rest[taken:]
                self.arrays += (parts,)
            self.orders = (tuple(order),) * 2
            self.parts = self.arrays
            self.facing = tuple(place[OPPOSITE[p]] for p in order)
            self.pairs = list(groups)

    def part_rows(self, kind, features):
        return features + EXTRA if kind == "wide" else features // 2 + EXTRA

    def offset(self, parts, number, features):
        return sum(self.part_rows(kind, features) for kind, _ in parts[:number])

    def rows(self, parts, features):
        return self.offset(parts, len(parts), features)


def pick(odd, pair):
    return pair[0] if pair[0] == pair[1] else jnp.where(odd, pair[1], pair[0])


def mm(a, b):
    return jnp.dot(a, b, preferred_element_type=F32)


def nt(a, b):
    return lax.dot_general(a, b, (((1,), (1,)), ((), ())), preferred_element_type=F32)


def eye(n):
    rows = lax.broadcasted_iota(jnp.int32, (n, n), 0)
    return (rows == lax.broadcasted_iota(jnp.int32, (n, n), 1)).astype(BF16)


def embed(own, table, species):
    picked = table[:, 3:4]
    for j in (2, 1, 0):
        picked = jnp.where(species == j, table[:, j : j + 1], picked)
    return (own.astype(F32) + picked).astype(BF16)


def attend(queries, keys, values):
    channels, _ = queries.shape
    size = channels // HEADS
    product = queries * keys
    parts = []
    for h in range(HEADS):
        rows = slice(h * size, (h + 1) * size)
        score = jnp.sum(product[rows], axis=0, keepdims=True) * (1.0 / math.sqrt(size))
        parts.append(jax.nn.sigmoid(score) * values[rows])
    return jnp.concatenate(parts, axis=0).astype(BF16)


def invariants(own, rev):
    product = [own[k].astype(F32) * rev[k].astype(F32) for k in range(9)]
    return jnp.concatenate(
        [
            product[0],
            product[1] + product[2] + product[3],
            product[4] + product[5] + product[6] + product[7] + product[8],
        ],
        axis=0,
    ).astype(BF16)


def harmonics(vectors):
    x, y, z = vectors[0:1], vectors[1:2], vectors[2:3]
    r2 = x * x + y * y + z * z
    root = math.sqrt(3.0)
    return (
        None,
        x,
        y,
        z,
        root * x * y,
        root * y * z,
        0.5 * (3.0 * z * z - r2),
        root * x * z,
        0.5 * root * (x * x - y * y),
    )


def update_tensors(own, mixed, gate, radial, vectors):
    m = own[0].shape[0]
    harmonic = harmonics(vectors)
    for k in range(9):
        degree = 0 if k == 0 else (1 if k < 4 else 2)
        rows = slice(degree * m, (degree + 1) * m)
        tail = radial[rows] if harmonic[k] is None else radial[rows] * harmonic[k]
        yield k, (own[k].astype(F32) + gate[rows] * mixed[k] + tail).astype(BF16)


def contract(middle, v, w_contract):
    hidden = (v * jax.nn.sigmoid(v)).astype(BF16)
    return (middle.astype(F32) + mm(w_contract, hidden)).astype(BF16)


def fetch(sources, buffers, sem):
    copies = [
        pltpu.make_async_copy(source, buffer, sem.at[n])
        for n, (source, buffer) in enumerate(zip(sources, buffers))
    ]
    for copy in copies:
        copy.start()
    return copies


def prepare_kernel(plan, *refs):
    inputs, own, where, rows, refs = refs[:7], refs[7], refs[8], refs[9], refs[10:]
    sends, buffers, sem = refs[: len(plan.arrays)], refs[len(plan.arrays) : -1], refs[-1]
    copies = fetch(inputs, buffers, sem)
    send_index, counts, species, vectors, reverse, scalars, tensors = buffers
    channels, edges = scalars.shape[2:]
    comps, m = tensors.shape[2:4]
    block = send_index.shape[-1]
    features = channels + comps * m
    odd = lax.rem(lax.axis_index("gx"), 2) == 1
    lane = lax.broadcasted_iota(jnp.int32, (1, block), 1)
    for copy in copies[:5]:
        copy.wait()

    def live(p):
        return jnp.where(lane < counts[0, 0, p], send_index[0, 0, p : p + 1, :], -1)

    index = jnp.concatenate(
        [
            live(p) if p == q else jnp.where(odd, live(q), live(p))
            for p, q in zip(*plan.orders)
        ],
        axis=1,
    )
    slots = index.shape[1]
    onehot = (lax.broadcasted_iota(jnp.int32, (edges, slots), 0) == index).astype(BF16)
    near = jnp.minimum(reverse[0], edges - 1) * 8
    rows[...] = jnp.concatenate(
        [near[:, j * 128 : (j + 1) * 128] for j in range(edges // 128)], axis=0
    )
    vec = jnp.concatenate([vectors[0, j] for j in range(3)], axis=0)
    high = vec.astype(BF16)
    left = vec - high.astype(F32)
    mid = left.astype(BF16)
    low = (left - mid.astype(F32)).astype(BF16)
    extra = jnp.concatenate(
        [
            jnp.broadcast_to(species[0].astype(F32), (7, edges)),
            high.astype(F32),
            mid.astype(F32),
            low.astype(F32),
        ],
        axis=0,
    ).astype(BF16)
    extra = mm(extra, onehot)
    where[0:3, :] = extra[7:10] + extra[10:13] + extra[13:16]
    where[3:8, :] = jnp.zeros((5, slots), F32)
    own[features:, :] = jnp.broadcast_to(extra[0:1], (EXTRA, slots)).astype(BF16)
    copies[5].wait()
    own[:channels, :] = mm(scalars[0, 0], onehot).astype(BF16)
    copies[6].wait()
    own[channels:features, :] = mm(tensors[0, 0].reshape(comps * m, edges), onehot).astype(BF16)
    half = features // 2
    for send, parts in zip(sends, plan.arrays):
        at = 0
        for kind, j in parts:
            if kind == "wide":
                send[at : at + features + EXTRA, :] = own[:, j * block : (j + 2) * block]
            else:
                piece = own[:, j * block : (j + 1) * block]
                send[at : at + half, :] = jnp.concatenate(
                    [piece[:half], piece[half:features]], axis=1
                )
                send[at + half : at + half + EXTRA, :] = jnp.concatenate(
                    [piece[features:], piece[features:]], axis=1
                )
            at += plan.part_rows(kind, features)


def copy_rows(table, rows, first, gathered, width):
    per = rows.shape[1]

    def body(i, _):
        for u in range(per):
            source = pl.ds(pl.multiple_of(rows[first + i, u], 8), 8)
            gathered[pl.ds(pl.multiple_of(i * (per * 8) + u * 8, 8), 8), :] = table[source, :]
        return 0

    lax.fori_loop(0, width // per, body, 0)


def interior_kernel(rows, *refs):
    inputs, refs = refs[:14], refs[14:]
    middle_out, message_out, tensors_out, edge_rows, gathered, pair_mix, w_shared, *refs = refs
    buffers, sem = refs[:-1], refs[-1]
    (
        scalars,
        tensors,
        w_mixing,
        w_invariant,
        vectors,
        species,
        table,
        w_query,
        w_key,
        w_value,
        w_output,
        w_message,
        w_gate,
        w_radial,
    ) = buffers
    edges = scalars.shape[-1]
    width = middle_out.shape[-1]
    channels = scalars.shape[2]
    comps, m = tensors.shape[2:4]
    step = pl.program_id(0)
    here = pl.ds(pl.multiple_of(step * width, 128), width)
    pairs = [(k, k + 1) for k in range(0, comps - 1, 2)] + [(comps - 2, comps - 1)]

    @pl.when(step == 0)
    def _():
        copies = fetch(inputs, buffers, sem)
        unit = eye(256)
        half = eye(128)
        for copy in copies:
            copy.wait()
        mixing = w_mixing[...].astype(F32)
        zero = jnp.zeros((m, m), F32)
        pair_mix[...] = jnp.concatenate(
            [
                half.astype(F32),
                jnp.concatenate([mixing, zero], axis=1),
                jnp.concatenate([zero, mixing], axis=1),
            ],
            axis=0,
        ).astype(BF16)
        w_shared[...] = nt(unit, w_invariant[...]).astype(BF16)
        for at in range(0, edges, 256):
            tile = slice(at, at + 256)
            pieces = [scalars[0, 0, c : c + 256, tile] for c in range(0, channels, 256)]
            n = 0
            while n < len(pairs):
                taken = 2 if n + 2 < len(pairs) else 1
                k = pairs[n][0]
                pieces.append(tensors[0, 0, k : k + 2 * taken, :, tile].reshape(-1, 256))
                n += taken
            j = 0
            for piece in pieces:
                turned = nt(unit, piece)
                for c in range(0, piece.shape[0], 128):
                    edge_rows[pl.ds(at * 8 + j, 256, stride=8), :] = turned[:, c : c + 128]
                    j += 1

    copy_rows(edge_rows, rows, step * (width // rows.shape[1]), gathered, width)

    def feature(j):
        return gathered[pl.ds(j, width, stride=8), :].astype(BF16)

    lead = channels // 128
    s_rev = jnp.concatenate([feature(j) for j in range(lead)], axis=1)
    t_rev, mixed = {}, {}
    for j, (first, second) in enumerate(pairs):
        both = nt(pair_mix[...], feature(lead + j))
        t_rev[first], t_rev[second] = both[:m], both[m : 2 * m]
        mixed[first], mixed[second] = both[2 * m : 3 * m], both[3 * m :]
    embedded = embed(scalars[0, 0, :, here], jnp.transpose(table[...]), species[0, :, here])
    attended = attend(mm(w_query[...], embedded), nt(w_key[...], s_rev), nt(w_value[...], s_rev))
    own_t = [tensors[0, 0, k, :, here] for k in range(comps)]
    middle = (
        embedded.astype(F32)
        + mm(w_output[...], attended)
        + mm(w_shared[...], invariants(own_t, t_rev))
    ).astype(BF16)
    middle_out[...] = middle
    message_out[...] = mm(w_message[...], middle).astype(BF16)
    gate = jax.nn.sigmoid(mm(w_gate[...], middle))
    radial = mm(w_radial[...], middle)
    vec = jnp.concatenate([vectors[0, j, :, here] for j in range(3)], axis=0)
    for k, new in update_tensors(own_t, mixed, gate, radial, vec):
        tensors_out[k] = new


def incoming_kernel(message, middle, rows, *refs):
    inputs, (scalars_out, edge_rows, gathered, *buffers, sem) = refs[:3], refs[3:]
    w_expand, w_reverse, w_contract = buffers
    channels, edges = message.shape
    width = middle.shape[1]
    step = pl.program_id(0)

    @pl.when(step == 0)
    def _():
        copies = fetch(inputs, buffers, sem)
        unit = eye(256)
        for at in range(0, edges, 256):
            for first in range(0, channels, 256):
                turned = nt(unit, message[first : first + 256, at : at + 256])
                for c in range(0, 256, 128):
                    row = at * 8 + (first + c) // 128
                    edge_rows[pl.ds(row, 256, stride=8), :] = turned[:, c : c + 128]
        for copy in copies:
            copy.wait()

    copy_rows(edge_rows, rows, step * (width // rows.shape[1]), gathered, width)
    incoming = jnp.concatenate(
        [
            gathered[pl.ds(j, width, stride=8), :].astype(BF16)
            for j in range(channels // 128)
        ],
        axis=1,
    )
    v = mm(w_expand[...], middle[...]) + nt(w_reverse[...], incoming)
    scalars_out[...] = contract(middle[...], v, w_contract[...])


def boundary_kernel(plan, block, edges, *refs):
    count = len(plan.parts)
    received, refs = refs[:count], refs[count:]
    (
        own,
        where,
        reverse,
        scalars_in,
        tensors_in,
        table,
        w_query,
        w_key,
        w_value,
        w_output,
        w_invariant,
        w_message,
        w_gate,
        w_radial,
        w_mixing,
        w_expand,
        w_reverse,
        w_contract,
        scalars_out,
        tensors_out,
        s_new,
        t_new,
        far,
    ) = refs
    odd = lax.rem(lax.axis_index("gx"), 2) == 1
    comps, m = tensors_in.shape[:2]
    channels = scalars_in.shape[0]
    features = channels + comps * m

    @pl.when(pl.program_id(0) == 0)
    def _():
        def block_of(g, part, n):
            kind, _ = plan.parts[g][part]
            at = plan.offset(plan.parts[g], part, features)
            if kind == "wide":
                return received[g][at : at + features + EXTRA, n * block : (n + 1) * block]
            half = features // 2
            upper = received[g][at : at + half, :]
            extra = received[g][at + half : at + half + EXTRA, :block]
            return jnp.concatenate([upper[:, :block], upper[:, block:], extra], axis=0)

        for j in range(0, len(plan.facing), 2):
            to = slice(j * block, (j + 2) * block)
            (g, part, n), second = plan.facing[j : j + 2]
            if n == 0 and second == (g, part, 1):
                at = plan.offset(plan.parts[g], part, features)
                far[:, to] = received[g][at : at + features + EXTRA, :]
            else:
                far[:, to] = jnp.concatenate([block_of(g, part, n), block_of(*second)], axis=1)
        s_own, s_far = own[:channels, :], far[:channels, :]
        t_own = [own[channels + k * m : channels + (k + 1) * m, :] for k in range(comps)]
        t_far = [far[channels + k * m : channels + (k + 1) * m, :] for k in range(comps)]
        columns = jnp.transpose(table[...])
        e_own = embed(s_own, columns, own[features : features + 1, :].astype(F32))
        e_far = embed(s_far, columns, far[features : features + 1, :].astype(F32))
        w_shared = nt(eye(channels), w_invariant[...]).astype(BF16)
        shared = mm(w_shared, invariants(t_own, t_far))
        a_own = attend(mm(w_query[...], e_own), mm(w_key[...], s_far), mm(w_value[...], s_far))
        a_far = attend(mm(w_query[...], e_far), mm(w_key[...], s_own), mm(w_value[...], s_own))
        middle = (e_own.astype(F32) + mm(w_output[...], a_own) + shared).astype(BF16)
        middle_far = (e_far.astype(F32) + mm(w_output[...], a_far) + shared).astype(BF16)
        incoming = mm(w_message[...], middle_far).astype(BF16)
        v = mm(w_expand[...], middle) + mm(w_reverse[...], incoming)
        s_new[...] = contract(middle, v, w_contract[...])
        gate = jax.nn.sigmoid(mm(w_gate[...], middle))
        radial = mm(w_radial[...], middle)
        mixed = [mm(w_mixing[...], t_far[k]) for k in range(comps)]
        for k, new in update_tensors(t_own, mixed, gate, radial, where[...]):
            t_new[k * m : (k + 1) * m, :] = new

    target = reverse[0] - edges
    width = target.shape[1]
    rows = lax.broadcasted_iota(jnp.int32, (block, width), 0)
    onehot = jnp.concatenate(
        [
            (rows + pick(odd, (OPPOSITE[p], OPPOSITE[q])) * block == target).astype(F32)
            for p, q in zip(*plan.orders)
        ],
        axis=0,
    ).astype(BF16)
    crosses = target >= 0
    scalars_out[0, 0] = jnp.where(
        crosses, mm(s_new[...], onehot), scalars_in[...].astype(F32)
    ).astype(BF16)
    merged = mm(t_new[...], onehot)
    for k in range(comps):
        tensors_out[0, 0, k] = jnp.where(
            crosses, merged[k * m : (k + 1) * m], tensors_in[k].astype(F32)
        ).astype(BF16)


def resident(*arrays):
    return [pltpu.with_memory_space_constraint(x, pltpu.HBM) for x in arrays]


def whole(*shape):
    return pl.BlockSpec(shape, lambda *_: (0,) * len(shape))


def per_device(gx, gy, *args):
    (
        scalars,
        tensors,
        vectors,
        species,
        table,
        reverse,
        send_index,
        counts,
        w_query,
        w_key,
        w_value,
        w_output,
        w_invariant,
        w_message,
        w_gate,
        w_radial,
        w_mixing,
        w_expand,
        w_reverse,
        w_contract,
    ) = args
    plan = Plan(gx, gy)
    vectors = jnp.transpose(vectors, (0, 2, 1, 3))
    table = jnp.transpose(table)
    w_invariant = jnp.transpose(w_invariant)
    _, _, channels, edges = scalars.shape
    comps, m = tensors.shape[2:4]
    features = channels + comps * m
    block = send_index.shape[-1]
    slots = len(DIRECTIONS) * block
    vmem = pl.BlockSpec(memory_space=pltpu.VMEM)

    def limit(mebibytes):
        return pltpu.CompilerParams(vmem_limit_bytes=mebibytes * 2**20)


    hbm = pl.BlockSpec(memory_space=pltpu.HBM)

    def buffers(*arrays):
        return [pltpu.VMEM(x.shape, x.dtype) for x in arrays] + [
            pltpu.SemaphoreType.DMA((len(arrays),))
        ]

    prepared = (send_index, counts, species, vectors, reverse, scalars, tensors)
    prepared_buffers = buffers(*prepared)
    prepared_buffers[1] = pltpu.SMEM(counts.shape, counts.dtype)
    own, where, rows, *sends = pl.pallas_call(
        functools.partial(prepare_kernel, plan),
        in_specs=[hbm] * len(prepared),
        out_specs=[vmem] * (3 + len(plan.arrays)),
        out_shape=[
            jax.ShapeDtypeStruct((features + EXTRA, slots), BF16),
            jax.ShapeDtypeStruct((8, slots), F32),
            jax.ShapeDtypeStruct((edges // 128, 128), jnp.int32),
        ]
        + [
            jax.ShapeDtypeStruct((plan.rows(parts, features), 2 * block), BF16)
            for parts in plan.arrays
        ],
        scratch_shapes=prepared_buffers,
        compiler_params=limit(24),
        name="prepare",
    )(*resident(*prepared))

    def exchange(x, pairs):
        return lax.ppermute(x, ("gx", "gy"), pairs)

    if plan.paired:
        received = [
            exchange(sends[0], plan.swaps[0]),
            exchange(sends[1], plan.swaps[1]),
            exchange(sends[2], plan.across),
        ]
    else:
        received = [exchange(x, pairs) for x, pairs in zip(sends, plan.pairs)]

    width = 512
    steps = edges // width
    row = pl.BlockSpec((1, 1, width), lambda i: (0, 0, i))
    flat = pl.BlockSpec((channels, width), lambda i: (0, i))
    stack = pl.BlockSpec((comps, m, width), lambda i: (0, 0, i))
    first_weights = (w_query, w_key, w_value, w_output, w_invariant, w_message, w_gate, w_radial, w_mixing)
    last_weights = (w_expand, w_reverse, w_contract)
    inside = (
        scalars, tensors, w_mixing, w_invariant, vectors, species, table,
        w_query, w_key, w_value, w_output, w_message, w_gate, w_radial,
    )
    middle, message, t_inside = pl.pallas_call(
        interior_kernel,
        grid=(steps,),
        in_specs=[pl.BlockSpec(memory_space=pltpu.SMEM)] + [hbm] * len(inside),
        out_specs=[flat, flat, stack],
        out_shape=[
            jax.ShapeDtypeStruct((channels, edges), BF16),
            jax.ShapeDtypeStruct((channels, edges), BF16),
            jax.ShapeDtypeStruct((comps, m, edges), BF16),
        ],
        scratch_shapes=[
            pltpu.VMEM((edges * 8, 128), F32),
            pltpu.VMEM((width * 8, 128), F32),
            pltpu.VMEM((256, 128), BF16),
            pltpu.VMEM((channels, w_invariant.shape[0]), BF16),
        ]
        + buffers(*inside),
        compiler_params=limit(36),
        cost_estimate=pl.CostEstimate(
            flops=2 * edges * edges * features, bytes_accessed=4 * edges * features, transcendentals=0
        ),
        name="interior",
    )(rows, *resident(*inside))
    if plan.paired:
        first, middle = lax.optimization_barrier((received[0], middle))
        received[0] = first
        received.append(exchange(first, plan.across))
    s_inside = pl.pallas_call(
        incoming_kernel,
        grid=(steps,),
        in_specs=[whole(channels, edges), flat, pl.BlockSpec(memory_space=pltpu.SMEM)]
        + [hbm] * len(last_weights),
        out_specs=flat,
        out_shape=jax.ShapeDtypeStruct((channels, edges), BF16),
        scratch_shapes=[
            pltpu.VMEM((edges * 8, 128), F32),
            pltpu.VMEM((width * 8, 128), F32),
        ]
        + buffers(*last_weights),
        compiler_params=limit(24),
        cost_estimate=pl.CostEstimate(
            flops=4 * edges * edges * channels, bytes_accessed=8 * edges * channels, transcendentals=0
        ),
        name="incoming",
    )(message, middle, rows, *resident(*last_weights))
    if plan.paired:
        second, s_inside = lax.optimization_barrier((received[1], s_inside))
        received[1] = second
        received.append(exchange(second, plan.across))

    return pl.pallas_call(
        functools.partial(boundary_kernel, plan, block, edges),
        grid=(steps,),
        in_specs=[whole(*r.shape) for r in received]
        + [whole(*own.shape), whole(*where.shape), row, flat, stack, whole(*table.shape)]
        + [whole(*w.shape) for w in first_weights + last_weights],
        out_specs=[
            pl.BlockSpec((1, 1, channels, width), lambda i: (0, 0, 0, i)),
            pl.BlockSpec((1, 1, comps, m, width), lambda i: (0, 0, 0, 0, i)),
        ],
        out_shape=[
            jax.ShapeDtypeStruct(scalars.shape, BF16),
            jax.ShapeDtypeStruct(tensors.shape, BF16),
        ],
        scratch_shapes=[
            pltpu.VMEM((channels, slots), BF16),
            pltpu.VMEM((comps * m, slots), BF16),
            pltpu.VMEM((features + EXTRA, slots), BF16),
        ],
        compiler_params=limit(26),
        cost_estimate=pl.CostEstimate(
            flops=2 * edges * slots * features, bytes_accessed=8 * edges * features, transcendentals=0
        ),
        name="boundary",
    )(*received, own, where, reverse, s_inside, t_inside, table, *first_weights, *last_weights)


def solution(mesh):
    gx, gy = mesh.shape["gx"], mesh.shape["gy"]

    def body(*args):
        return per_device(gx, gy, *args)

    step = jax.shard_map(
        body,
        mesh=mesh,
        in_specs=(
            P("gx", "gy", None, None),
            P("gx", "gy", None, None, None),
            P("gx", "gy", None, None),
            P("gx", "gy", None),
            P(),
            P("gx", "gy", None),
            P("gx", "gy", None, None),
            P("gx", "gy", None),
        )
        + (P(),) * 12,
        out_specs=(P("gx", "gy", None, None), P("gx", "gy", None, None, None)),
        check_vma=False,
    )
    if not Plan(gx, gy).paired:
        return step
    return step
```

```python
import functools
import math

import jax
import jax.numpy as jnp
from jax import lax
from jax.experimental import pallas as pl
from jax.experimental.pallas import tpu as pltpu
from jax.sharding import PartitionSpec as P


HEADS = 8
DIRECTIONS = ((1, 0), (-1, 0), (0, 1), (0, -1), (1, 1), (1, -1), (-1, 1), (-1, -1))
OPPOSITE = tuple(DIRECTIONS.index((-dx, -dy)) for dx, dy in DIRECTIONS)
EXTRA = 16
BF16 = jnp.bfloat16
F32 = jnp.float32


def ring(gx, gy, dx, dy):
    return tuple(
        (a * gy + b, ((a + dx) % gx) * gy + (b + dy) % gy) for a in range(gx) for b in range(gy)
    )


class Plan:
    def __init__(self, gx, gy):
        self.paired = gx % 2 == 0 and gy == 2
        if self.paired:
            self.orders = ((4, 5, 7, 6, 0, 1, 2, 3), (7, 6, 4, 5, 1, 0, 2, 3))
            self.arrays = ((("wide", 0), ("fold", 4)), (("wide", 2), ("fold", 5)), (("wide", 6),))
            self.facing = (
                (3, 0, 0), (3, 0, 1), (4, 0, 0), (4, 0, 1), (0, 1, 0), (1, 1, 0), (2, 0, 1), (2, 0, 0),
            )
            self.parts = self.arrays + self.arrays[:2]
            even = [(a, a + 1 - 2 * (a % 2)) for a in range(gx)]
            odd = [(a, (a - 1 + 2 * (a % 2)) % gx) for a in range(gx)]
            self.swaps = [
                tuple((a * gy + b, c * gy + b) for a, c in pairs for b in range(gy))
                for pairs in (even, odd)
            ]
            self.across = ring(gx, gy, 0, 1)
        else:
            groups = {}
            for p in (4, 5, 7, 6, 0, 1, 2, 3):
                groups.setdefault(ring(gx, gy, *DIRECTIONS[p]), []).append(p)
            order, self.arrays, place = [], (), {}
            for g, members in enumerate(groups.values()):
                parts = ()
                rest = members
                while rest:
                    taken = 2 if len(rest) > 1 else 1
                    for n, p in enumerate(rest[:taken]):
                        place[p] = (g, len(parts), n)
                    parts += (("wide" if taken == 2 else "fold", len(order)),)
                    order += rest[:taken]
                    rest = rest[taken:]
                self.arrays += (parts,)
            self.orders = (tuple(order),) * 2
            self.parts = self.arrays
            self.facing = tuple(place[OPPOSITE[p]] for p in order)
            self.pairs = list(groups)

    def part_rows(self, kind, features):
        return features + EXTRA if kind == "wide" else features // 2 + EXTRA

    def offset(self, parts, number, features):
        return sum(self.part_rows(kind, features) for kind, _ in parts[:number])

    def rows(self, parts, features):
        return self.offset(parts, len(parts), features)


def pick(odd, pair):
    return pair[0] if pair[0] == pair[1] else jnp.where(odd, pair[1], pair[0])


def mm(a, b):
    return jnp.dot(a, b, preferred_element_type=F32)


def nt(a, b):
    return lax.dot_general(a, b, (((1,), (1,)), ((), ())), preferred_element_type=F32)


def eye(n):
    rows = lax.broadcasted_iota(jnp.int32, (n, n), 0)
    return (rows == lax.broadcasted_iota(jnp.int32, (n, n), 1)).astype(BF16)


def embed(own, table, species):
    picked = table[:, 3:4]
    for j in (2, 1, 0):
        picked = jnp.where(species == j, table[:, j : j + 1], picked)
    return (own.astype(F32) + picked).astype(BF16)


def attend(queries, keys, values):
    channels, _ = queries.shape
    size = channels // HEADS
    product = queries * keys
    parts = []
    for h in range(HEADS):
        rows = slice(h * size, (h + 1) * size)
        score = jnp.sum(product[rows], axis=0, keepdims=True) * (1.0 / math.sqrt(size))
        parts.append(jax.nn.sigmoid(score) * values[rows])
    return jnp.concatenate(parts, axis=0).astype(BF16)


def invariants(own, rev):
    product = [own[k].astype(F32) * rev[k].astype(F32) for k in range(9)]
    return jnp.concatenate(
        [
            product[0],
            product[1] + product[2] + product[3],
            product[4] + product[5] + product[6] + product[7] + product[8],
        ],
        axis=0,
    ).astype(BF16)


def harmonics(vectors):
    x, y, z = vectors[0:1], vectors[1:2], vectors[2:3]
    r2 = x * x + y * y + z * z
    root = math.sqrt(3.0)
    return (
        None,
        x,
        y,
        z,
        root * x * y,
        root * y * z,
        0.5 * (3.0 * z * z - r2),
        root * x * z,
        0.5 * root * (x * x - y * y),
    )


def update_tensors(own, mixed, gate, radial, vectors):
    m = own[0].shape[0]
    harmonic = harmonics(vectors)
    for k in range(9):
        degree = 0 if k == 0 else (1 if k < 4 else 2)
        rows = slice(degree * m, (degree + 1) * m)
        tail = radial[rows] if harmonic[k] is None else radial[rows] * harmonic[k]
        yield k, (own[k].astype(F32) + gate[rows] * mixed[k] + tail).astype(BF16)


def contract(middle, v, w_contract):
    hidden = (v * jax.nn.sigmoid(v)).astype(BF16)
    return (middle.astype(F32) + mm(w_contract, hidden)).astype(BF16)


def fetch(sources, buffers, sem):
    pieces = []
    waiting = list(sources)
    for buffer in buffers:
        at = 0
        while at < buffer.shape[0]:
            source = waiting.pop(0)
            part = buffer if source.shape == buffer.shape else buffer.at[pl.ds(at, source.shape[0])]
            pieces.append((source, part))
            at += source.shape[0]
    copies = [pltpu.make_async_copy(*piece, sem.at[n]) for n, piece in enumerate(pieces)]
    for copy in copies:
        copy.start()
    return copies


def prepare_kernel(plan, *refs):
    inputs, own, where, rows, refs = refs[:7], refs[7], refs[8], refs[9], refs[10:]
    sends, buffers, sem = refs[: len(plan.arrays)], refs[len(plan.arrays) : -1], refs[-1]
    copies = fetch(inputs, buffers, sem)
    send_index, counts, species, vectors, reverse, scalars, tensors = buffers
    channels, edges = scalars.shape[2:]
    comps, m = tensors.shape[2:4]
    block = send_index.shape[-1]
    features = channels + comps * m
    odd = lax.rem(lax.axis_index("gx"), 2) == 1
    lane = lax.broadcasted_iota(jnp.int32, (1, block), 1)
    for copy in copies[:5]:
        copy.wait()

    def live(p):
        return jnp.where(lane < counts[0, 0, p], send_index[0, 0, p : p + 1, :], -1)

    index = jnp.concatenate(
        [
            live(p) if p == q else jnp.where(odd, live(q), live(p))
            for p, q in zip(*plan.orders)
        ],
        axis=1,
    )
    slots = index.shape[1]
    onehot = (lax.broadcasted_iota(jnp.int32, (edges, slots), 0) == index).astype(BF16)
    near = jnp.minimum(reverse[0], edges - 1) * 8
    rows[...] = jnp.concatenate(
        [near[:, j * 128 : (j + 1) * 128] for j in range(edges // 128)], axis=0
    )
    vec = jnp.concatenate([vectors[0, j] for j in range(3)], axis=0)
    high = vec.astype(BF16)
    left = vec - high.astype(F32)
    mid = left.astype(BF16)
    low = (left - mid.astype(F32)).astype(BF16)
    extra = jnp.concatenate(
        [
            jnp.broadcast_to(species[0].astype(F32), (7, edges)),
            high.astype(F32),
            mid.astype(F32),
            low.astype(F32),
        ],
        axis=0,
    ).astype(BF16)
    extra = mm(extra, onehot)
    where[0:3, :] = extra[7:10] + extra[10:13] + extra[13:16]
    where[3:8, :] = jnp.zeros((5, slots), F32)
    own[features:, :] = jnp.broadcast_to(extra[0:1], (EXTRA, slots)).astype(BF16)
    copies[5].wait()
    own[:channels, :] = mm(scalars[0, 0], onehot).astype(BF16)
    copies[6].wait()
    own[channels:features, :] = mm(tensors[0, 0].reshape(comps * m, edges), onehot).astype(BF16)
    half = features // 2
    for send, parts in zip(sends, plan.arrays):
        at = 0
        for kind, j in parts:
            if kind == "wide":
                send[at : at + features + EXTRA, :] = own[:, j * block : (j + 2) * block]
            else:
                piece = own[:, j * block : (j + 1) * block]
                send[at : at + half, :] = jnp.concatenate(
                    [piece[:half], piece[half:features]], axis=1
                )
                send[at + half : at + half + EXTRA, :] = jnp.concatenate(
                    [piece[features:], piece[features:]], axis=1
                )
            at += plan.part_rows(kind, features)


def copy_rows(step, table, rows, gathered):
    per = rows.shape[1]
    width = gathered.shape[0] // 8
    for t in range(rows.shape[0] * per // width):

        @pl.when(step == t)
        def _(first=t * width):
            for e in range(width):
                n = first + e
                source = pl.ds(pl.multiple_of(rows[n // per, n % per], 8), 8)
                gathered[e * 8 : e * 8 + 8, :] = table[source, :]


def interior_kernel(rows, *refs):
    inputs, refs = refs[:14], refs[14:]
    middle_out, message_out, tensors_out, edge_rows, gathered, pair_mix, w_shared, *refs = refs
    buffers, sem = refs[:-1], refs[-1]
    (
        scalars,
        tensors,
        w_mixing,
        w_invariant,
        vectors,
        species,
        table,
        w_query,
        w_output,
        w_rev,
        w_mid,
    ) = buffers
    edges = scalars.shape[-1]
    width = middle_out.shape[-1]
    channels = scalars.shape[2]
    comps, m = tensors.shape[2:4]
    step = pl.program_id(0)
    here = pl.ds(pl.multiple_of(step * width, 128), width)
    pairs = [(k, k + 1) for k in range(0, comps - 1, 2)] + [(comps - 2, comps - 1)]

    @pl.when(step == 0)
    def _():
        copies = fetch(inputs, buffers, sem)
        unit = eye(256)
        half = eye(128)

        def turn(at, j, piece):
            turned = nt(unit, piece)
            for c in range(0, piece.shape[0], 128):
                edge_rows[pl.ds(at * 8 + j + c // 128, 256, stride=8), :] = turned[:, c : c + 128]

        copies[0].wait()
        for at in range(0, edges, 256):
            for c in range(0, channels, 256):
                turn(at, c // 128, scalars[0, 0, c : c + 256, at : at + 256])
        copies[1].wait()
        for at in range(0, edges, 256):
            n = 0
            while n < len(pairs):
                taken = 2 if n + 2 < len(pairs) else 1
                k = pairs[n][0]
                piece = tensors[0, 0, k : k + 2 * taken, :, at : at + 256].reshape(-1, 256)
                turn(at, channels // 128 + n, piece)
                n += taken
        for copy in copies[2:]:
            copy.wait()
        mixing = w_mixing[...].astype(F32)
        zero = jnp.zeros((m, m), F32)
        pair_mix[...] = jnp.concatenate(
            [
                half.astype(F32),
                jnp.concatenate([mixing, zero], axis=1),
                jnp.concatenate([zero, mixing], axis=1),
            ],
            axis=0,
        ).astype(BF16)
        w_shared[...] = nt(unit, w_invariant[...]).astype(BF16)

    copy_rows(step, edge_rows, rows, gathered)

    def feature(j):
        return gathered[pl.ds(j, width, stride=8), :].astype(BF16)

    lead = channels // 128
    s_rev = jnp.concatenate([feature(j) for j in range(lead)], axis=1)
    t_rev, mixed = {}, {}
    for j, (first, second) in enumerate(pairs):
        both = nt(pair_mix[...], feature(lead + j))
        t_rev[first], t_rev[second] = both[:m], both[m : 2 * m]
        mixed[first], mixed[second] = both[2 * m : 3 * m], both[3 * m :]
    embedded = embed(scalars[0, 0, :, here], jnp.transpose(table[...]), species[0, :, here])
    both = nt(w_rev[...], s_rev)
    attended = attend(mm(w_query[...], embedded), both[:channels], both[channels:])
    own_t = [tensors[0, 0, k, :, here] for k in range(comps)]
    middle = (
        embedded.astype(F32)
        + mm(w_output[...], attended)
        + mm(w_shared[...], invariants(own_t, t_rev))
    ).astype(BF16)
    middle_out[...] = middle
    spread = mm(w_mid[...], middle)
    message_out[...] = spread[:channels].astype(BF16)
    gate = jax.nn.sigmoid(spread[channels : channels + 3 * m])
    radial = spread[channels + 3 * m :]
    vec = jnp.concatenate([vectors[0, j, :, here] for j in range(3)], axis=0)
    for k, new in update_tensors(own_t, mixed, gate, radial, vec):
        tensors_out[k] = new


def incoming_kernel(message, middle, rows, *refs):
    inputs, (scalars_out, edge_rows, gathered, *buffers, sem) = refs[:3], refs[3:]
    w_expand, w_reverse, w_contract = buffers
    channels, edges = message.shape
    width = middle.shape[1]
    step = pl.program_id(0)

    @pl.when(step == 0)
    def _():
        copies = fetch(inputs, buffers, sem)
        unit = eye(256)
        for at in range(0, edges, 256):
            for first in range(0, channels, 256):
                turned = nt(unit, message[first : first + 256, at : at + 256])
                for c in range(0, 256, 128):
                    row = at * 8 + (first + c) // 128
                    edge_rows[pl.ds(row, 256, stride=8), :] = turned[:, c : c + 128]
        for copy in copies:
            copy.wait()

    copy_rows(step, edge_rows, rows, gathered)
    incoming = jnp.concatenate(
        [
            gathered[pl.ds(j, width, stride=8), :].astype(BF16)
            for j in range(channels // 128)
        ],
        axis=1,
    )
    v = mm(w_expand[...], middle[...]) + nt(w_reverse[...], incoming)
    scalars_out[...] = contract(middle[...], v, w_contract[...])


def boundary_kernel(plan, block, edges, *refs):
    count = len(plan.parts)
    received, refs = refs[:count], refs[count:]
    (
        own,
        where,
        reverse,
        scalars_in,
        tensors_in,
        table,
        w_query,
        w_key,
        w_value,
        w_output,
        w_invariant,
        w_message,
        w_gate,
        w_radial,
        w_mixing,
        w_expand,
        w_reverse,
        w_contract,
        scalars_out,
        tensors_out,
        s_new,
        t_new,
        far,
    ) = refs
    odd = lax.rem(lax.axis_index("gx"), 2) == 1
    comps, m = tensors_in.shape[:2]
    channels = scalars_in.shape[0]
    features = channels + comps * m

    @pl.when(pl.program_id(0) == 0)
    def _():
        def block_of(g, part, n):
            kind, _ = plan.parts[g][part]
            at = plan.offset(plan.parts[g], part, features)
            if kind == "wide":
                return received[g][at : at + features + EXTRA, n * block : (n + 1) * block]
            half = features // 2
            upper = received[g][at : at + half, :]
            extra = received[g][at + half : at + half + EXTRA, :block]
            return jnp.concatenate([upper[:, :block], upper[:, block:], extra], axis=0)

        for j in range(0, len(plan.facing), 2):
            to = slice(j * block, (j + 2) * block)
            (g, part, n), second = plan.facing[j : j + 2]
            if n == 0 and second == (g, part, 1):
                at = plan.offset(plan.parts[g], part, features)
                far[:, to] = received[g][at : at + features + EXTRA, :]
            else:
                far[:, to] = jnp.concatenate([block_of(g, part, n), block_of(*second)], axis=1)
        s_own, s_far = own[:channels, :], far[:channels, :]
        t_own = [own[channels + k * m : channels + (k + 1) * m, :] for k in range(comps)]
        t_far = [far[channels + k * m : channels + (k + 1) * m, :] for k in range(comps)]
        columns = jnp.transpose(table[...])
        e_own = embed(s_own, columns, own[features : features + 1, :].astype(F32))
        e_far = embed(s_far, columns, far[features : features + 1, :].astype(F32))
        w_shared = nt(eye(channels), w_invariant[...]).astype(BF16)
        shared = mm(w_shared, invariants(t_own, t_far))
        a_own = attend(mm(w_query[...], e_own), mm(w_key[...], s_far), mm(w_value[...], s_far))
        a_far = attend(mm(w_query[...], e_far), mm(w_key[...], s_own), mm(w_value[...], s_own))
        middle = (e_own.astype(F32) + mm(w_output[...], a_own) + shared).astype(BF16)
        middle_far = (e_far.astype(F32) + mm(w_output[...], a_far) + shared).astype(BF16)
        incoming = mm(w_message[...], middle_far).astype(BF16)
        v = mm(w_expand[...], middle) + mm(w_reverse[...], incoming)
        s_new[...] = contract(middle, v, w_contract[...])
        gate = jax.nn.sigmoid(mm(w_gate[...], middle))
        radial = mm(w_radial[...], middle)
        mixed = [mm(w_mixing[...], t_far[k]) for k in range(comps)]
        for k, new in update_tensors(t_own, mixed, gate, radial, where[...]):
            t_new[k * m : (k + 1) * m, :] = new

    target = reverse[0] - edges
    width = target.shape[1]
    rows = lax.broadcasted_iota(jnp.int32, (block, width), 0)
    onehot = jnp.concatenate(
        [
            (rows + pick(odd, (OPPOSITE[p], OPPOSITE[q])) * block == target).astype(F32)
            for p, q in zip(*plan.orders)
        ],
        axis=0,
    ).astype(BF16)
    crosses = target >= 0
    scalars_out[0, 0] = jnp.where(
        crosses, mm(s_new[...], onehot), scalars_in[...].astype(F32)
    ).astype(BF16)
    merged = mm(t_new[...], onehot)
    for k in range(comps):
        tensors_out[0, 0, k] = jnp.where(
            crosses, merged[k * m : (k + 1) * m], tensors_in[k].astype(F32)
        ).astype(BF16)


def resident(*arrays):
    return [pltpu.with_memory_space_constraint(x, pltpu.HBM) for x in arrays]


def whole(*shape):
    return pl.BlockSpec(shape, lambda *_: (0,) * len(shape))


def per_device(gx, gy, *args):
    (
        scalars,
        tensors,
        vectors,
        species,
        table,
        reverse,
        send_index,
        counts,
        w_query,
        w_key,
        w_value,
        w_output,
        w_invariant,
        w_message,
        w_gate,
        w_radial,
        w_mixing,
        w_expand,
        w_reverse,
        w_contract,
    ) = args
    plan = Plan(gx, gy)
    vectors = jnp.transpose(vectors, (0, 2, 1, 3))
    table = jnp.transpose(table)
    w_invariant = jnp.transpose(w_invariant)
    _, _, channels, edges = scalars.shape
    comps, m = tensors.shape[2:4]
    features = channels + comps * m
    block = send_index.shape[-1]
    slots = len(DIRECTIONS) * block
    vmem = pl.BlockSpec(memory_space=pltpu.VMEM)

    def limit(mebibytes):
        return pltpu.CompilerParams(vmem_limit_bytes=mebibytes * 2**20)


    hbm = pl.BlockSpec(memory_space=pltpu.HBM)

    def buffers(*arrays):
        return [pltpu.VMEM(x.shape, x.dtype) for x in arrays] + [
            pltpu.SemaphoreType.DMA((len(arrays),))
        ]

    prepared = (send_index, counts, species, vectors, reverse, scalars, tensors)
    prepared_buffers = buffers(*prepared)
    prepared_buffers[1] = pltpu.SMEM(counts.shape, counts.dtype)
    own, where, rows, *sends = pl.pallas_call(
        functools.partial(prepare_kernel, plan),
        in_specs=[hbm] * len(prepared),
        out_specs=[vmem] * (3 + len(plan.arrays)),
        out_shape=[
            jax.ShapeDtypeStruct((features + EXTRA, slots), BF16),
            jax.ShapeDtypeStruct((8, slots), F32),
            jax.ShapeDtypeStruct((edges // 128, 128), jnp.int32),
        ]
        + [
            jax.ShapeDtypeStruct((plan.rows(parts, features), 2 * block), BF16)
            for parts in plan.arrays
        ],
        scratch_shapes=prepared_buffers,
        compiler_params=limit(24),
        name="prepare",
    )(*resident(*prepared))

    def exchange(x, pairs):
        return lax.ppermute(x, ("gx", "gy"), pairs)

    if plan.paired:
        received = [exchange(sends[0], plan.swaps[0]), exchange(sends[1], plan.swaps[1]), None]
    else:
        received = [exchange(x, pairs) for x, pairs in zip(sends, plan.pairs)]

    width = 1024 if edges % 1024 == 0 else edges
    steps = edges // width
    row = pl.BlockSpec((1, 1, width), lambda i: (0, 0, i))
    flat = pl.BlockSpec((channels, width), lambda i: (0, i))
    stack = pl.BlockSpec((comps, m, width), lambda i: (0, 0, i))
    first_weights = (w_query, w_key, w_value, w_output, w_invariant, w_message, w_gate, w_radial, w_mixing)
    last_weights = (w_expand, w_reverse, w_contract)
    inside = (
        scalars, tensors, w_mixing, w_invariant, vectors, species, table,
        w_query, w_output, w_key, w_value, w_message, w_gate, w_radial,
    )
    stacked = [pltpu.VMEM((2 * channels, channels), BF16), pltpu.VMEM((channels + 6 * m, channels), BF16)]
    middle, message, t_inside = pl.pallas_call(
        interior_kernel,
        grid=(steps,),
        in_specs=[pl.BlockSpec(memory_space=pltpu.SMEM)] + [hbm] * len(inside),
        out_specs=[flat, flat, stack],
        out_shape=[
            jax.ShapeDtypeStruct((channels, edges), BF16),
            jax.ShapeDtypeStruct((channels, edges), BF16),
            jax.ShapeDtypeStruct((comps, m, edges), BF16),
        ],
        scratch_shapes=[
            pltpu.VMEM((edges * 8, 128), F32),
            pltpu.VMEM((width * 8, 128), F32),
            pltpu.VMEM((256, 128), BF16),
            pltpu.VMEM((channels, w_invariant.shape[0]), BF16),
        ]
        + buffers(*inside)[:9]
        + stacked
        + [pltpu.SemaphoreType.DMA((len(inside),))],
        compiler_params=limit(36),
        cost_estimate=pl.CostEstimate(
            flops=2 * edges * edges * features, bytes_accessed=4 * edges * features, transcendentals=0
        ),
        name="interior",
    )(rows, *resident(*inside))
    if plan.paired:
        first, own_side, middle = lax.optimization_barrier((received[0], sends[2], middle))
        received[0] = first
        received[2] = exchange(own_side, plan.across)
        received.append(exchange(first, plan.across))
    s_inside = pl.pallas_call(
        incoming_kernel,
        grid=(steps,),
        in_specs=[whole(channels, edges), flat, pl.BlockSpec(memory_space=pltpu.SMEM)]
        + [hbm] * len(last_weights),
        out_specs=flat,
        out_shape=jax.ShapeDtypeStruct((channels, edges), BF16),
        scratch_shapes=[
            pltpu.VMEM((edges * 8, 128), F32),
            pltpu.VMEM((width * 8, 128), F32),
        ]
        + buffers(*last_weights),
        compiler_params=limit(24),
        cost_estimate=pl.CostEstimate(
            flops=4 * edges * edges * channels, bytes_accessed=8 * edges * channels, transcendentals=0
        ),
        name="incoming",
    )(message, middle, rows, *resident(*last_weights))
    if plan.paired:
        second, s_inside = lax.optimization_barrier((received[1], s_inside))
        received[1] = second
        received.append(exchange(second, plan.across))

    return pl.pallas_call(
        functools.partial(boundary_kernel, plan, block, edges),
        grid=(steps,),
        in_specs=[whole(*r.shape) for r in received]
        + [whole(*own.shape), whole(*where.shape), row, flat, stack, whole(*table.shape)]
        + [whole(*w.shape) for w in first_weights + last_weights],
        out_specs=[
            pl.BlockSpec((1, 1, channels, width), lambda i: (0, 0, 0, i)),
            pl.BlockSpec((1, 1, comps, m, width), lambda i: (0, 0, 0, 0, i)),
        ],
        out_shape=[
            jax.ShapeDtypeStruct(scalars.shape, BF16),
            jax.ShapeDtypeStruct(tensors.shape, BF16),
        ],
        scratch_shapes=[
            pltpu.VMEM((channels, slots), BF16),
            pltpu.VMEM((comps * m, slots), BF16),
            pltpu.VMEM((features + EXTRA, slots), BF16),
        ],
        compiler_params=limit(26),
        cost_estimate=pl.CostEstimate(
            flops=2 * edges * slots * features, bytes_accessed=8 * edges * features, transcendentals=0
        ),
        name="boundary",
    )(*received, own, where, reverse, s_inside, t_inside, table, *first_weights, *last_weights)


def solution(mesh):
    gx, gy = mesh.shape["gx"], mesh.shape["gy"]

    def body(*args):
        return per_device(gx, gy, *args)

    step = jax.shard_map(
        body,
        mesh=mesh,
        in_specs=(
            P("gx", "gy", None, None),
            P("gx", "gy", None, None, None),
            P("gx", "gy", None, None),
            P("gx", "gy", None),
            P(),
            P("gx", "gy", None),
            P("gx", "gy", None, None),
            P("gx", "gy", None),
        )
        + (P(),) * 12,
        out_specs=(P("gx", "gy", None, None), P("gx", "gy", None, None, None)),
        check_vma=False,
    )
    if not Plan(gx, gy).paired:
        return step
    return step
```

```python
import functools
import math

import jax
import jax.numpy as jnp
from jax import lax
from jax.experimental import pallas as pl
from jax.experimental.pallas import tpu as pltpu
from jax.sharding import PartitionSpec as P


HEADS = 8
DIRECTIONS = ((1, 0), (-1, 0), (0, 1), (0, -1), (1, 1), (1, -1), (-1, 1), (-1, -1))
OPPOSITE = tuple(DIRECTIONS.index((-dx, -dy)) for dx, dy in DIRECTIONS)
EXTRA = 16
BF16 = jnp.bfloat16
F32 = jnp.float32


def ring(gx, gy, dx, dy):
    return tuple(
        (a * gy + b, ((a + dx) % gx) * gy + (b + dy) % gy) for a in range(gx) for b in range(gy)
    )


class Plan:
    def __init__(self, gx, gy):
        self.paired = gx % 2 == 0 and gy == 2
        if self.paired:
            self.orders = ((4, 5, 7, 6, 0, 1, 2, 3), (7, 6, 4, 5, 1, 0, 2, 3))
            self.arrays = ((("wide", 0), ("fold", 4)), (("wide", 2), ("fold", 5)), (("wide", 6),))
            self.facing = (
                (3, 0, 0), (3, 0, 1), (4, 0, 0), (4, 0, 1), (0, 1, 0), (1, 1, 0), (2, 0, 1), (2, 0, 0),
            )
            self.parts = self.arrays + self.arrays[:2]
            even = [(a, a + 1 - 2 * (a % 2)) for a in range(gx)]
            odd = [(a, (a - 1 + 2 * (a % 2)) % gx) for a in range(gx)]
            self.swaps = [
                tuple((a * gy + b, c * gy + b) for a, c in pairs for b in range(gy))
                for pairs in (even, odd)
            ]
            self.across = ring(gx, gy, 0, 1)
        else:
            groups = {}
            for p in (4, 5, 7, 6, 0, 1, 2, 3):
                groups.setdefault(ring(gx, gy, *DIRECTIONS[p]), []).append(p)
            order, self.arrays, place = [], (), {}
            for g, members in enumerate(groups.values()):
                parts = ()
                rest = members
                while rest:
                    taken = 2 if len(rest) > 1 else 1
                    for n, p in enumerate(rest[:taken]):
                        place[p] = (g, len(parts), n)
                    parts += (("wide" if taken == 2 else "fold", len(order)),)
                    order += rest[:taken]
                    rest = rest[taken:]
                self.arrays += (parts,)
            self.orders = (tuple(order),) * 2
            self.parts = self.arrays
            self.facing = tuple(place[OPPOSITE[p]] for p in order)
            self.pairs = list(groups)

    def part_rows(self, kind, features):
        return features + EXTRA if kind == "wide" else features // 2 + EXTRA

    def offset(self, parts, number, features):
        return sum(self.part_rows(kind, features) for kind, _ in parts[:number])

    def rows(self, parts, features):
        return self.offset(parts, len(parts), features)


def pick(odd, pair):
    return pair[0] if pair[0] == pair[1] else jnp.where(odd, pair[1], pair[0])


def mm(a, b):
    return jnp.dot(a, b, preferred_element_type=F32)


def nt(a, b):
    return lax.dot_general(a, b, (((1,), (1,)), ((), ())), preferred_element_type=F32)


def eye(n):
    rows = lax.broadcasted_iota(jnp.int32, (n, n), 0)
    return (rows == lax.broadcasted_iota(jnp.int32, (n, n), 1)).astype(BF16)


def embed(own, table, species):
    picked = table[:, 3:4]
    for j in (2, 1, 0):
        picked = jnp.where(species == j, table[:, j : j + 1], picked)
    return (own.astype(F32) + picked).astype(BF16)


def attend(queries, keys, values):
    channels, _ = queries.shape
    size = channels // HEADS
    product = queries * keys
    parts = []
    for h in range(HEADS):
        rows = slice(h * size, (h + 1) * size)
        score = jnp.sum(product[rows], axis=0, keepdims=True) * (1.0 / math.sqrt(size))
        parts.append(jax.nn.sigmoid(score) * values[rows])
    return jnp.concatenate(parts, axis=0).astype(BF16)


def invariants(own, rev):
    product = [own[k].astype(F32) * rev[k].astype(F32) for k in range(9)]
    return jnp.concatenate(
        [
            product[0],
            product[1] + product[2] + product[3],
            product[4] + product[5] + product[6] + product[7] + product[8],
        ],
        axis=0,
    ).astype(BF16)


def harmonics(vectors):
    x, y, z = vectors[0:1], vectors[1:2], vectors[2:3]
    r2 = x * x + y * y + z * z
    root = math.sqrt(3.0)
    return (
        None,
        x,
        y,
        z,
        root * x * y,
        root * y * z,
        0.5 * (3.0 * z * z - r2),
        root * x * z,
        0.5 * root * (x * x - y * y),
    )


def update_tensors(own, mixed, gate, radial, vectors):
    m = own[0].shape[0]
    harmonic = harmonics(vectors)
    for k in range(9):
        degree = 0 if k == 0 else (1 if k < 4 else 2)
        rows = slice(degree * m, (degree + 1) * m)
        tail = radial[rows] if harmonic[k] is None else radial[rows] * harmonic[k]
        yield k, (own[k].astype(F32) + gate[rows] * mixed[k] + tail).astype(BF16)


def contract(middle, v, w_contract):
    hidden = (v * jax.nn.sigmoid(v)).astype(BF16)
    return (middle.astype(F32) + mm(w_contract, hidden)).astype(BF16)


def fetch(sources, buffers, sem):
    pieces = []
    waiting = list(sources)
    for buffer in buffers:
        at = 0
        while at < buffer.shape[0]:
            source = waiting.pop(0)
            part = buffer if source.shape == buffer.shape else buffer.at[pl.ds(at, source.shape[0])]
            pieces.append((source, part))
            at += source.shape[0]
    copies = [pltpu.make_async_copy(*piece, sem.at[n]) for n, piece in enumerate(pieces)]
    for copy in copies:
        copy.start()
    return copies


def prepare_kernel(plan, *refs):
    inputs, own, where, rows, refs = refs[:7], refs[7], refs[8], refs[9], refs[10:]
    sends, buffers, sem = refs[: len(plan.arrays)], refs[len(plan.arrays) : -1], refs[-1]
    onehot, *buffers = buffers
    copies = fetch(inputs, buffers, sem)
    send_index, counts, species, vectors, reverse, scalars, tensors = buffers
    channels, edges = scalars.shape[2:]
    comps, m = tensors.shape[2:4]
    block = send_index.shape[-1]
    features = channels + comps * m
    odd = lax.rem(lax.axis_index("gx"), 2) == 1
    lane = lax.broadcasted_iota(jnp.int32, (1, block), 1)
    for copy in copies[:5]:
        copy.wait()

    def live(p):
        return jnp.where(lane < counts[0, 0, p], send_index[0, 0, p : p + 1, :], -1)

    index = jnp.concatenate(
        [
            live(p) if p == q else jnp.where(odd, live(q), live(p))
            for p, q in zip(*plan.orders)
        ],
        axis=1,
    )
    slots = index.shape[1]
    onehot[...] = (lax.broadcasted_iota(jnp.int32, (edges, slots), 0) == index).astype(BF16)
    near = jnp.minimum(reverse[0], edges - 1) * 8
    rows[...] = jnp.concatenate(
        [near[:, j * 128 : (j + 1) * 128] for j in range(edges // 128)], axis=0
    )
    vec = jnp.concatenate([vectors[0, j] for j in range(3)], axis=0)
    high = vec.astype(BF16)
    left = vec - high.astype(F32)
    mid = left.astype(BF16)
    low = (left - mid.astype(F32)).astype(BF16)
    extra = jnp.concatenate(
        [
            jnp.broadcast_to(species[0].astype(F32), (7, edges)),
            high.astype(F32),
            mid.astype(F32),
            low.astype(F32),
        ],
        axis=0,
    ).astype(BF16)
    extra = mm(extra, onehot[...])
    where[0:3, :] = extra[7:10] + extra[10:13] + extra[13:16]
    where[3:8, :] = jnp.zeros((5, slots), F32)
    own[features:, :] = jnp.broadcast_to(extra[0:1], (EXTRA, slots)).astype(BF16)
    copies[5].wait()
    own[:channels, :] = mm(scalars[0, 0], onehot[...]).astype(BF16)
    copies[6].wait()
    own[channels:features, :] = mm(
        tensors[0, 0].reshape(comps * m, edges), onehot[...]
    ).astype(BF16)
    half = features // 2
    for send, parts in zip(sends, plan.arrays):
        at = 0
        for kind, j in parts:
            if kind == "wide":
                send[at : at + features + EXTRA, :] = own[:, j * block : (j + 2) * block]
            else:
                piece = own[:, j * block : (j + 1) * block]
                send[at : at + half, :] = jnp.concatenate(
                    [piece[:half], piece[half:features]], axis=1
                )
                send[at + half : at + half + EXTRA, :] = jnp.concatenate(
                    [piece[features:], piece[features:]], axis=1
                )
            at += plan.part_rows(kind, features)


def copy_rows(step, table, rows, gathered):
    per = rows.shape[1]
    width = gathered.shape[0] // 8
    for t in range(rows.shape[0] * per // width):

        @pl.when(step == t)
        def _(first=t * width):
            for e in range(width):
                n = first + e
                source = pl.ds(pl.multiple_of(rows[n // per, n % per], 8), 8)
                gathered[e * 8 : e * 8 + 8, :] = table[source, :]


def interior_kernel(rows, *refs):
    inputs, refs = refs[:14], refs[14:]
    middle_out, message_out, tensors_out, edge_rows, gathered, pair_mix, w_shared, *refs = refs
    buffers, sem = refs[:-1], refs[-1]
    (
        scalars,
        tensors,
        w_mixing,
        w_invariant,
        vectors,
        species,
        table,
        w_query,
        w_output,
        w_rev,
        w_mid,
    ) = buffers
    edges = scalars.shape[-1]
    width = gathered.shape[0] // 8
    channels = scalars.shape[2]
    comps, m = tensors.shape[2:4]
    step = pl.program_id(0)
    here = pl.ds(pl.multiple_of(step * width, 128), width)
    pairs = [(k, k + 1) for k in range(0, comps - 1, 2)] + [(comps - 2, comps - 1)]

    @pl.when(step == 0)
    def _():
        copies = fetch(inputs, buffers, sem)
        unit = eye(256)
        half = eye(128)

        def turn(at, j, piece):
            turned = nt(unit, piece)
            for c in range(0, piece.shape[0], 128):
                edge_rows[pl.ds(at * 8 + j + c // 128, 256, stride=8), :] = turned[:, c : c + 128]

        copies[0].wait()
        for at in range(0, edges, 256):
            for c in range(0, channels, 256):
                turn(at, c // 128, scalars[0, 0, c : c + 256, at : at + 256])
        copies[1].wait()
        for at in range(0, edges, 256):
            n = 0
            while n < len(pairs):
                taken = 2 if n + 2 < len(pairs) else 1
                k = pairs[n][0]
                piece = tensors[0, 0, k : k + 2 * taken, :, at : at + 256].reshape(-1, 256)
                turn(at, channels // 128 + n, piece)
                n += taken
        for copy in copies[2:]:
            copy.wait()
        mixing = w_mixing[...].astype(F32)
        zero = jnp.zeros((m, m), F32)
        pair_mix[...] = jnp.concatenate(
            [
                half.astype(F32),
                jnp.concatenate([mixing, zero], axis=1),
                jnp.concatenate([zero, mixing], axis=1),
            ],
            axis=0,
        ).astype(BF16)
        w_shared[...] = nt(unit, w_invariant[...]).astype(BF16)

    copy_rows(step, edge_rows, rows, gathered)

    def feature(j):
        return gathered[pl.ds(j, width, stride=8), :].astype(BF16)

    lead = channels // 128
    s_rev = jnp.concatenate([feature(j) for j in range(lead)], axis=1)
    t_rev, mixed = {}, {}
    for j, (first, second) in enumerate(pairs):
        both = nt(pair_mix[...], feature(lead + j))
        t_rev[first], t_rev[second] = both[:m], both[m : 2 * m]
        mixed[first], mixed[second] = both[2 * m : 3 * m], both[3 * m :]
    embedded = embed(scalars[0, 0, :, here], jnp.transpose(table[...]), species[0, :, here])
    both = nt(w_rev[...], s_rev)
    attended = attend(mm(w_query[...], embedded), both[:channels], both[channels:])
    own_t = [tensors[0, 0, k, :, here] for k in range(comps)]
    middle = (
        embedded.astype(F32)
        + mm(w_output[...], attended)
        + mm(w_shared[...], invariants(own_t, t_rev))
    ).astype(BF16)
    middle_out[:, here] = middle
    spread = mm(w_mid[...], middle)
    message_out[:, here] = spread[:channels].astype(BF16)
    gate = jax.nn.sigmoid(spread[channels : channels + 3 * m])
    radial = spread[channels + 3 * m :]
    vec = jnp.concatenate([vectors[0, j, :, here] for j in range(3)], axis=0)
    for k, new in update_tensors(own_t, mixed, gate, radial, vec):
        tensors_out[k, :, here] = new


def incoming_kernel(plan, block, message, middle, rows, *refs):
    inputs, (scalars_out, merge, edge_rows, gathered, *buffers, sem) = refs[:4], refs[4:]
    reverse, w_expand, w_reverse, w_contract = buffers
    channels, edges = message.shape
    width = gathered.shape[0] // 8
    step = pl.program_id(0)
    here = pl.ds(pl.multiple_of(step * width, 128), width)

    @pl.when(step == 0)
    def _():
        copies = fetch(inputs, buffers, sem)
        unit = eye(256)
        for at in range(0, edges, 256):
            for first in range(0, channels, 256):
                turned = nt(unit, message[first : first + 256, at : at + 256])
                for c in range(0, 256, 128):
                    row = at * 8 + (first + c) // 128
                    edge_rows[pl.ds(row, 256, stride=8), :] = turned[:, c : c + 128]
        for copy in copies:
            copy.wait()

    copy_rows(step, edge_rows, rows, gathered)
    incoming = jnp.concatenate(
        [
            gathered[pl.ds(j, width, stride=8), :].astype(BF16)
            for j in range(channels // 128)
        ],
        axis=1,
    )
    v = mm(w_expand[...], middle[:, here]) + nt(w_reverse[...], incoming)
    scalars_out[:, here] = contract(middle[:, here], v, w_contract[...])
    target = reverse[0, :, here] - edges
    odd = lax.rem(lax.axis_index("gx"), 2) == 1
    at = lax.broadcasted_iota(jnp.int32, (block, width), 0)
    for j, (p, q) in enumerate(zip(*plan.orders)):
        merge[j * block : (j + 1) * block, here] = (
            at + pick(odd, (OPPOSITE[p], OPPOSITE[q])) * block == target
        ).astype(BF16)


def boundary_kernel(plan, block, edges, *refs):
    count = len(plan.parts)
    received, refs = refs[:count], refs[count:]
    (
        own,
        where,
        merge,
        reverse,
        scalars_in,
        tensors_in,
        table,
        w_query,
        w_key,
        w_value,
        w_output,
        w_invariant,
        w_message,
        w_gate,
        w_radial,
        w_mixing,
        w_expand,
        w_reverse,
        w_contract,
        scalars_out,
        tensors_out,
        s_new,
        t_new,
        far,
    ) = refs
    comps, m = tensors_in.shape[:2]
    channels = scalars_in.shape[0]
    features = channels + comps * m
    slots = own.shape[1]

    @pl.when(pl.program_id(0) == 0)
    def _():
        def block_of(g, part, n):
            kind, _ = plan.parts[g][part]
            at = plan.offset(plan.parts[g], part, features)
            if kind == "wide":
                return received[g][at : at + features + EXTRA, n * block : (n + 1) * block]
            half = features // 2
            upper = received[g][at : at + half, :]
            extra = received[g][at + half : at + half + EXTRA, :block]
            return jnp.concatenate([upper[:, :block], upper[:, block:], extra], axis=0)

        for j in range(0, len(plan.facing), 2):
            to = slice(j * block, (j + 2) * block)
            (g, part, n), second = plan.facing[j : j + 2]
            if n == 0 and second == (g, part, 1):
                at = plan.offset(plan.parts[g], part, features)
                far[:, to] = received[g][at : at + features + EXTRA, :]
            else:
                far[:, to] = jnp.concatenate([block_of(g, part, n), block_of(*second)], axis=1)
        s_own, s_far = own[:channels, :], far[:channels, :]
        t_own = [own[channels + k * m : channels + (k + 1) * m, :] for k in range(comps)]
        t_far = [far[channels + k * m : channels + (k + 1) * m, :] for k in range(comps)]
        columns = jnp.transpose(table[...])
        e_own = embed(s_own, columns, own[features : features + 1, :].astype(F32))
        e_far = embed(s_far, columns, far[features : features + 1, :].astype(F32))
        w_shared = nt(eye(channels), w_invariant[...]).astype(BF16)
        shared = mm(w_shared, invariants(t_own, t_far))
        embedded = jnp.concatenate([e_own, e_far], axis=1)
        w_rev = jnp.concatenate([w_key[...], w_value[...]], axis=0)
        both = mm(w_rev, jnp.concatenate([s_far, s_own], axis=1))
        attended = attend(mm(w_query[...], embedded), both[:channels], both[channels:])
        middles = (
            embedded.astype(F32)
            + mm(w_output[...], attended)
            + jnp.concatenate([shared, shared], axis=1)
        ).astype(BF16)
        middle = middles[:, :slots]
        incoming = mm(w_message[...], middles[:, slots:]).astype(BF16)
        w_mid = jnp.concatenate([w_expand[...], w_gate[...], w_radial[...]], axis=0)
        spread = mm(w_mid, middle)
        hidden = w_expand.shape[0]
        v = spread[:hidden] + mm(w_reverse[...], incoming)
        s_new[...] = contract(middle, v, w_contract[...])
        gate = jax.nn.sigmoid(spread[hidden : hidden + 3 * m])
        radial = spread[hidden + 3 * m :]
        mixed = [mm(w_mixing[...], t_far[k]) for k in range(comps)]
        for k, new in update_tensors(t_own, mixed, gate, radial, where[...]):
            t_new[k * m : (k + 1) * m, :] = new

    width = scalars_out.shape[-1]
    here = pl.ds(pl.multiple_of(pl.program_id(0) * width, 128), width)
    onehot = merge[:, here]
    crosses = jnp.broadcast_to((reverse[0, :, here] >= edges).astype(F32), (m, width))
    crosses = crosses.astype(BF16) > 0

    def merged(new, old):
        return jnp.where(crosses, new.astype(BF16), old)

    s_all = mm(s_new[...], onehot)
    for c in range(0, channels, m):
        scalars_out[0, 0, c : c + m] = merged(s_all[c : c + m], scalars_in[c : c + m, here])
    t_all = mm(t_new[...], onehot)
    for k in range(comps):
        tensors_out[0, 0, k] = merged(t_all[k * m : (k + 1) * m], tensors_in[k, :, here])


def resident(*arrays):
    return [pltpu.with_memory_space_constraint(x, pltpu.HBM) for x in arrays]


def whole(*shape):
    return pl.BlockSpec(shape, lambda *_: (0,) * len(shape))


def per_device(gx, gy, *args):
    (
        scalars,
        tensors,
        vectors,
        species,
        table,
        reverse,
        send_index,
        counts,
        w_query,
        w_key,
        w_value,
        w_output,
        w_invariant,
        w_message,
        w_gate,
        w_radial,
        w_mixing,
        w_expand,
        w_reverse,
        w_contract,
    ) = args
    plan = Plan(gx, gy)
    vectors = jnp.transpose(vectors, (0, 2, 1, 3))
    table = jnp.transpose(table)
    w_invariant = jnp.transpose(w_invariant)
    _, _, channels, edges = scalars.shape
    comps, m = tensors.shape[2:4]
    features = channels + comps * m
    block = send_index.shape[-1]
    slots = len(DIRECTIONS) * block
    vmem = pl.BlockSpec(memory_space=pltpu.VMEM)

    def limit(mebibytes):
        return pltpu.CompilerParams(vmem_limit_bytes=mebibytes * 2**20)


    hbm = pl.BlockSpec(memory_space=pltpu.HBM)

    def buffers(*arrays):
        return [pltpu.VMEM(x.shape, x.dtype) for x in arrays] + [
            pltpu.SemaphoreType.DMA((len(arrays),))
        ]

    prepared = (send_index, counts, species, vectors, reverse, scalars, tensors)
    prepared_buffers = buffers(*prepared)
    prepared_buffers[1] = pltpu.SMEM(counts.shape, counts.dtype)
    prepared_buffers.insert(0, pltpu.VMEM((edges, slots), BF16))
    own, where, rows, *sends = pl.pallas_call(
        functools.partial(prepare_kernel, plan),
        in_specs=[hbm] * len(prepared),
        out_specs=[vmem] * (3 + len(plan.arrays)),
        out_shape=[
            jax.ShapeDtypeStruct((features + EXTRA, slots), BF16),
            jax.ShapeDtypeStruct((8, slots), F32),
            jax.ShapeDtypeStruct((edges // 128, 128), jnp.int32),
        ]
        + [
            jax.ShapeDtypeStruct((plan.rows(parts, features), 2 * block), BF16)
            for parts in plan.arrays
        ],
        scratch_shapes=prepared_buffers,
        compiler_params=limit(24),
        name="prepare",
    )(*resident(*prepared))

    def exchange(x, pairs):
        return lax.ppermute(x, ("gx", "gy"), pairs)

    if plan.paired:
        received = [exchange(sends[0], plan.swaps[0]), exchange(sends[1], plan.swaps[1]), None]
    else:
        received = [exchange(x, pairs) for x, pairs in zip(sends, plan.pairs)]

    width = 1024 if edges % 1024 == 0 else edges
    steps = edges // width
    flat = whole(channels, edges)
    first_weights = (w_query, w_key, w_value, w_output, w_invariant, w_message, w_gate, w_radial, w_mixing)
    last_weights = (w_expand, w_reverse, w_contract)
    inside = (
        scalars, tensors, w_mixing, w_invariant, vectors, species, table,
        w_query, w_output, w_key, w_value, w_message, w_gate, w_radial,
    )
    stacked = [pltpu.VMEM((2 * channels, channels), BF16), pltpu.VMEM((channels + 6 * m, channels), BF16)]
    middle, message, t_inside = pl.pallas_call(
        interior_kernel,
        grid=(steps,),
        in_specs=[pl.BlockSpec(memory_space=pltpu.SMEM)] + [hbm] * len(inside),
        out_specs=[flat, flat, whole(comps, m, edges)],
        out_shape=[
            jax.ShapeDtypeStruct((channels, edges), BF16),
            jax.ShapeDtypeStruct((channels, edges), BF16),
            jax.ShapeDtypeStruct((comps, m, edges), BF16),
        ],
        scratch_shapes=[
            pltpu.VMEM((edges * 8, 128), F32),
            pltpu.VMEM((width * 8, 128), F32),
            pltpu.VMEM((256, 128), BF16),
            pltpu.VMEM((channels, w_invariant.shape[0]), BF16),
        ]
        + buffers(*inside)[:9]
        + stacked
        + [pltpu.SemaphoreType.DMA((len(inside),))],
        compiler_params=limit(36),
        cost_estimate=pl.CostEstimate(
            flops=2 * edges * edges * features, bytes_accessed=4 * edges * features, transcendentals=0
        ),
        name="interior",
    )(rows, *resident(*inside))
    last_weights = (w_expand, w_reverse, w_contract)
    brought = (reverse, *last_weights)
    s_inside, merge = pl.pallas_call(
        functools.partial(incoming_kernel, plan, block),
        grid=(steps,),
        in_specs=[whole(channels, edges), flat, pl.BlockSpec(memory_space=pltpu.SMEM)]
        + [hbm] * len(brought),
        out_specs=[flat, whole(slots, edges)],
        out_shape=[
            jax.ShapeDtypeStruct((channels, edges), BF16),
            jax.ShapeDtypeStruct((slots, edges), BF16),
        ],
        scratch_shapes=[
            pltpu.VMEM((edges * 8, 128), F32),
            pltpu.VMEM((width * 8, 128), F32),
        ]
        + buffers(*brought),
        compiler_params=limit(24),
        cost_estimate=pl.CostEstimate(
            flops=4 * edges * edges * channels, bytes_accessed=8 * edges * channels, transcendentals=0
        ),
        name="incoming",
    )(message, middle, rows, *resident(*brought))
    if plan.paired:
        held = lax.optimization_barrier((received[0], received[1], sends[2], s_inside))
        received[0], received[1], own_side, s_inside = held
        received[2] = exchange(own_side, plan.across)
        received.append(exchange(received[0], plan.across))
        received.append(exchange(received[1], plan.across))

    return pl.pallas_call(
        functools.partial(boundary_kernel, plan, block, edges),
        grid=(steps,),
        in_specs=[whole(*r.shape) for r in received]
        + [whole(*own.shape), whole(*where.shape), whole(slots, edges)]
        + [whole(*reverse.shape), flat, whole(comps, m, edges), whole(*table.shape)]
        + [whole(*w.shape) for w in first_weights + last_weights],
        out_specs=[
            pl.BlockSpec((1, 1, channels, width), lambda i: (0, 0, 0, i)),
            pl.BlockSpec((1, 1, comps, m, width), lambda i: (0, 0, 0, 0, i)),
        ],
        out_shape=[
            jax.ShapeDtypeStruct(scalars.shape, BF16),
            jax.ShapeDtypeStruct(tensors.shape, BF16),
        ],
        scratch_shapes=[
            pltpu.VMEM((channels, slots), BF16),
            pltpu.VMEM((comps * m, slots), BF16),
            pltpu.VMEM((features + EXTRA, slots), BF16),
        ],
        compiler_params=limit(26),
        cost_estimate=pl.CostEstimate(
            flops=2 * edges * slots * features, bytes_accessed=8 * edges * features, transcendentals=0
        ),
        name="boundary",
    )(*received, own, where, merge, reverse, s_inside, t_inside, table, *first_weights, *last_weights)


def solution(mesh):
    gx, gy = mesh.shape["gx"], mesh.shape["gy"]

    def body(*args):
        return per_device(gx, gy, *args)

    step = jax.shard_map(
        body,
        mesh=mesh,
        in_specs=(
            P("gx", "gy", None, None),
            P("gx", "gy", None, None, None),
            P("gx", "gy", None, None),
            P("gx", "gy", None),
            P(),
            P("gx", "gy", None),
            P("gx", "gy", None, None),
            P("gx", "gy", None),
        )
        + (P(),) * 12,
        out_specs=(P("gx", "gy", None, None), P("gx", "gy", None, None, None)),
        check_vma=False,
    )
    if not Plan(gx, gy).paired:
        return step
    return step
```

```python
import functools
import math

import jax
import jax.numpy as jnp
from jax import lax
from jax.experimental import pallas as pl
from jax.experimental.pallas import tpu as pltpu
from jax.sharding import PartitionSpec as P


HEADS = 8
DIRECTIONS = ((1, 0), (-1, 0), (0, 1), (0, -1), (1, 1), (1, -1), (-1, 1), (-1, -1))
OPPOSITE = tuple(DIRECTIONS.index((-dx, -dy)) for dx, dy in DIRECTIONS)
EXTRA = 16
BF16 = jnp.bfloat16
F32 = jnp.float32


def ring(gx, gy, dx, dy):
    return tuple(
        (a * gy + b, ((a + dx) % gx) * gy + (b + dy) % gy) for a in range(gx) for b in range(gy)
    )


class Plan:
    def __init__(self, gx, gy):
        self.paired = gx % 2 == 0 and gy == 2
        if self.paired:
            self.orders = ((4, 5, 7, 6, 0, 1, 2, 3), (7, 6, 4, 5, 1, 0, 2, 3))
            self.arrays = ((("wide", 0), ("fold", 4)), (("wide", 2), ("fold", 5)), (("wide", 6),))
            self.facing = (
                (3, 0, 0), (3, 0, 1), (4, 0, 0), (4, 0, 1), (0, 1, 0), (1, 1, 0), (2, 0, 1), (2, 0, 0),
            )
            self.parts = self.arrays + self.arrays[:2]
            even = [(a, a + 1 - 2 * (a % 2)) for a in range(gx)]
            odd = [(a, (a - 1 + 2 * (a % 2)) % gx) for a in range(gx)]
            self.swaps = [
                tuple((a * gy + b, c * gy + b) for a, c in pairs for b in range(gy))
                for pairs in (even, odd)
            ]
            self.across = ring(gx, gy, 0, 1)
        else:
            groups = {}
            for p in (4, 5, 7, 6, 0, 1, 2, 3):
                groups.setdefault(ring(gx, gy, *DIRECTIONS[p]), []).append(p)
            order, self.arrays, place = [], (), {}
            for g, members in enumerate(groups.values()):
                parts = ()
                rest = members
                while rest:
                    taken = 2 if len(rest) > 1 else 1
                    for n, p in enumerate(rest[:taken]):
                        place[p] = (g, len(parts), n)
                    parts += (("wide" if taken == 2 else "fold", len(order)),)
                    order += rest[:taken]
                    rest = rest[taken:]
                self.arrays += (parts,)
            self.orders = (tuple(order),) * 2
            self.parts = self.arrays
            self.facing = tuple(place[OPPOSITE[p]] for p in order)
            self.pairs = list(groups)

    def part_rows(self, kind, features):
        return features + EXTRA if kind == "wide" else features // 2 + EXTRA

    def offset(self, parts, number, features):
        return sum(self.part_rows(kind, features) for kind, _ in parts[:number])

    def rows(self, parts, features):
        return self.offset(parts, len(parts), features)


def pick(odd, pair):
    return pair[0] if pair[0] == pair[1] else jnp.where(odd, pair[1], pair[0])


def mm(a, b):
    return jnp.dot(a, b, preferred_element_type=F32)


def nt(a, b):
    return lax.dot_general(a, b, (((1,), (1,)), ((), ())), preferred_element_type=F32)


def eye(n):
    rows = lax.broadcasted_iota(jnp.int32, (n, n), 0)
    return (rows == lax.broadcasted_iota(jnp.int32, (n, n), 1)).astype(BF16)


def embed(own, table, species):
    picked = table[:, 3:4]
    for j in (2, 1, 0):
        picked = jnp.where(species == j, table[:, j : j + 1], picked)
    return (own.astype(F32) + picked).astype(BF16)


def attend(queries, keys, values):
    channels, _ = queries.shape
    size = channels // HEADS
    product = queries * keys
    parts = []
    for h in range(HEADS):
        rows = slice(h * size, (h + 1) * size)
        score = jnp.sum(product[rows], axis=0, keepdims=True) * (1.0 / math.sqrt(size))
        parts.append(jax.nn.sigmoid(score) * values[rows])
    return jnp.concatenate(parts, axis=0).astype(BF16)


def invariants(own, rev):
    product = [own[k].astype(F32) * rev[k].astype(F32) for k in range(9)]
    return jnp.concatenate(
        [
            product[0],
            product[1] + product[2] + product[3],
            product[4] + product[5] + product[6] + product[7] + product[8],
        ],
        axis=0,
    ).astype(BF16)


def harmonics(vectors):
    x, y, z = vectors[0:1], vectors[1:2], vectors[2:3]
    r2 = x * x + y * y + z * z
    root = math.sqrt(3.0)
    return (
        None,
        x,
        y,
        z,
        root * x * y,
        root * y * z,
        0.5 * (3.0 * z * z - r2),
        root * x * z,
        0.5 * root * (x * x - y * y),
    )


def update_tensors(own, mixed, gate, radial, vectors):
    m = own[0].shape[0]
    harmonic = harmonics(vectors)
    for k in range(9):
        degree = 0 if k == 0 else (1 if k < 4 else 2)
        rows = slice(degree * m, (degree + 1) * m)
        tail = radial[rows] if harmonic[k] is None else radial[rows] * harmonic[k]
        yield k, (own[k].astype(F32) + gate[rows] * mixed[k] + tail).astype(BF16)


def contract(middle, v, w_contract):
    hidden = (v * jax.nn.sigmoid(v)).astype(BF16)
    return (middle.astype(F32) + mm(w_contract, hidden)).astype(BF16)


def fetch(sources, buffers, sem):
    pieces = []
    waiting = list(sources)
    for buffer in buffers:
        at = 0
        while at < buffer.shape[0]:
            source = waiting.pop(0)
            part = buffer if source.shape == buffer.shape else buffer.at[pl.ds(at, source.shape[0])]
            pieces.append((source, part))
            at += source.shape[0]
    copies = [pltpu.make_async_copy(*piece, sem.at[n]) for n, piece in enumerate(pieces)]
    for copy in copies:
        copy.start()
    return copies


def prepare_kernel(plan, *refs):
    inputs, (own, where, rows, scalars, tensors), refs = refs[:7], refs[7:12], refs[12:]
    sends, (onehot, *buffers, sem) = refs[: len(plan.arrays)], refs[len(plan.arrays) :]
    copies = fetch(inputs, (*buffers, scalars, tensors), sem)
    send_index, counts, species, vectors, reverse = buffers
    channels, edges = scalars.shape[2:]
    comps, m = tensors.shape[2:4]
    block = send_index.shape[-1]
    features = channels + comps * m
    odd = lax.rem(lax.axis_index("gx"), 2) == 1
    lane = lax.broadcasted_iota(jnp.int32, (1, block), 1)
    for copy in copies[:5]:
        copy.wait()

    def live(p):
        return jnp.where(lane < counts[0, 0, p], send_index[0, 0, p : p + 1, :], -1)

    index = jnp.concatenate(
        [
            live(p) if p == q else jnp.where(odd, live(q), live(p))
            for p, q in zip(*plan.orders)
        ],
        axis=1,
    )
    slots = index.shape[1]
    onehot[...] = (lax.broadcasted_iota(jnp.int32, (edges, slots), 0) == index).astype(BF16)
    near = jnp.minimum(reverse[0], edges - 1) * 8
    rows[...] = jnp.concatenate(
        [near[:, j * 128 : (j + 1) * 128] for j in range(edges // 128)], axis=0
    )
    vec = jnp.concatenate([vectors[0, j] for j in range(3)], axis=0)
    high = vec.astype(BF16)
    left = vec - high.astype(F32)
    mid = left.astype(BF16)
    low = (left - mid.astype(F32)).astype(BF16)
    extra = jnp.concatenate(
        [
            jnp.broadcast_to(species[0].astype(F32), (7, edges)),
            high.astype(F32),
            mid.astype(F32),
            low.astype(F32),
        ],
        axis=0,
    ).astype(BF16)
    extra = mm(extra, onehot[...])
    where[0:3, :] = extra[7:10] + extra[10:13] + extra[13:16]
    where[3:8, :] = jnp.zeros((5, slots), F32)
    own[features:, :] = jnp.broadcast_to(extra[0:1], (EXTRA, slots)).astype(BF16)
    copies[5].wait()
    own[:channels, :] = mm(scalars[0, 0], onehot[...]).astype(BF16)
    copies[6].wait()
    own[channels:features, :] = mm(
        tensors[0, 0].reshape(comps * m, edges), onehot[...]
    ).astype(BF16)
    half = features // 2
    for send, parts in zip(sends, plan.arrays):
        at = 0
        for kind, j in parts:
            if kind == "wide":
                send[at : at + features + EXTRA, :] = own[:, j * block : (j + 2) * block]
            else:
                piece = own[:, j * block : (j + 1) * block]
                send[at : at + half, :] = jnp.concatenate(
                    [piece[:half], piece[half:features]], axis=1
                )
                send[at + half : at + half + EXTRA, :] = jnp.concatenate(
                    [piece[features:], piece[features:]], axis=1
                )
            at += plan.part_rows(kind, features)


def copy_rows(step, table, rows, gathered):
    per = rows.shape[1]
    width = gathered.shape[0] // 8
    for t in range(rows.shape[0] * per // width):

        @pl.when(step == t)
        def _(first=t * width):
            for e in range(width):
                n = first + e
                source = pl.ds(pl.multiple_of(rows[n // per, n % per], 8), 8)
                gathered[e * 8 : e * 8 + 8, :] = table[source, :]


def interior_kernel(rows, scalars, tensors, *refs):
    inputs, refs = refs[:12], refs[12:]
    middle_out, message_out, tensors_out, edge_rows, gathered, pair_mix, w_shared, *refs = refs
    buffers, sem = refs[:-1], refs[-1]
    (
        w_mixing,
        w_invariant,
        vectors,
        species,
        table,
        w_query,
        w_output,
        w_rev,
        w_mid,
    ) = buffers
    edges = scalars.shape[-1]
    width = gathered.shape[0] // 8
    channels = scalars.shape[2]
    comps, m = tensors.shape[2:4]
    step = pl.program_id(0)
    here = pl.ds(pl.multiple_of(step * width, 128), width)
    pairs = [(k, k + 1) for k in range(0, comps - 1, 2)] + [(comps - 2, comps - 1)]

    @pl.when(step == 0)
    def _():
        copies = fetch(inputs, buffers, sem)
        unit = eye(256)
        half = eye(128)

        def turn(at, j, piece):
            turned = nt(unit, piece)
            for c in range(0, piece.shape[0], 128):
                edge_rows[pl.ds(at * 8 + j + c // 128, 256, stride=8), :] = turned[:, c : c + 128]

        for at in range(0, edges, 256):
            for c in range(0, channels, 256):
                turn(at, c // 128, scalars[0, 0, c : c + 256, at : at + 256])
        for at in range(0, edges, 256):
            n = 0
            while n < len(pairs):
                taken = 2 if n + 2 < len(pairs) else 1
                k = pairs[n][0]
                piece = tensors[0, 0, k : k + 2 * taken, :, at : at + 256].reshape(-1, 256)
                turn(at, channels // 128 + n, piece)
                n += taken
        for copy in copies:
            copy.wait()
        mixing = w_mixing[...].astype(F32)
        zero = jnp.zeros((m, m), F32)
        pair_mix[...] = jnp.concatenate(
            [
                half.astype(F32),
                jnp.concatenate([mixing, zero], axis=1),
                jnp.concatenate([zero, mixing], axis=1),
            ],
            axis=0,
        ).astype(BF16)
        w_shared[...] = nt(unit, w_invariant[...]).astype(BF16)

    copy_rows(step, edge_rows, rows, gathered)

    def feature(j):
        return gathered[pl.ds(j, width, stride=8), :].astype(BF16)

    lead = channels // 128
    s_rev = jnp.concatenate([feature(j) for j in range(lead)], axis=1)
    t_rev, mixed = {}, {}
    for j, (first, second) in enumerate(pairs):
        both = nt(pair_mix[...], feature(lead + j))
        t_rev[first], t_rev[second] = both[:m], both[m : 2 * m]
        mixed[first], mixed[second] = both[2 * m : 3 * m], both[3 * m :]
    embedded = embed(scalars[0, 0, :, here], jnp.transpose(table[...]), species[0, :, here])
    both = nt(w_rev[...], s_rev)
    attended = attend(mm(w_query[...], embedded), both[:channels], both[channels:])
    own_t = [tensors[0, 0, k, :, here] for k in range(comps)]
    middle = (
        embedded.astype(F32)
        + mm(w_output[...], attended)
        + mm(w_shared[...], invariants(own_t, t_rev))
    ).astype(BF16)
    middle_out[:, here] = middle
    spread = mm(w_mid[...], middle)
    message_out[:, here] = spread[:channels].astype(BF16)
    gate = jax.nn.sigmoid(spread[channels : channels + 3 * m])
    radial = spread[channels + 3 * m :]
    vec = jnp.concatenate([vectors[0, j, :, here] for j in range(3)], axis=0)
    for k, new in update_tensors(own_t, mixed, gate, radial, vec):
        tensors_out[k, :, here] = new


def incoming_kernel(plan, block, message, middle, rows, *refs):
    inputs, (scalars_out, merge, edge_rows, gathered, *buffers, sem) = refs[:4], refs[4:]
    reverse, w_expand, w_reverse, w_contract = buffers
    channels, edges = message.shape
    width = gathered.shape[0] // 8
    step = pl.program_id(0)
    here = pl.ds(pl.multiple_of(step * width, 128), width)

    @pl.when(step == 0)
    def _():
        copies = fetch(inputs, buffers, sem)
        unit = eye(256)
        for at in range(0, edges, 256):
            for first in range(0, channels, 256):
                turned = nt(unit, message[first : first + 256, at : at + 256])
                for c in range(0, 256, 128):
                    row = at * 8 + (first + c) // 128
                    edge_rows[pl.ds(row, 256, stride=8), :] = turned[:, c : c + 128]
        for copy in copies:
            copy.wait()

    copy_rows(step, edge_rows, rows, gathered)
    incoming = jnp.concatenate(
        [
            gathered[pl.ds(j, width, stride=8), :].astype(BF16)
            for j in range(channels // 128)
        ],
        axis=1,
    )
    v = mm(w_expand[...], middle[:, here]) + nt(w_reverse[...], incoming)
    scalars_out[:, here] = contract(middle[:, here], v, w_contract[...])
    target = reverse[0, :, here] - edges
    odd = lax.rem(lax.axis_index("gx"), 2) == 1
    at = lax.broadcasted_iota(jnp.int32, (block, width), 0)
    for j, (p, q) in enumerate(zip(*plan.orders)):
        merge[j * block : (j + 1) * block, here] = (
            at + pick(odd, (OPPOSITE[p], OPPOSITE[q])) * block == target
        ).astype(BF16)


def boundary_kernel(plan, block, edges, *refs):
    count = len(plan.parts)
    received, refs = refs[:count], refs[count:]
    (
        own,
        where,
        merge,
        reverse,
        scalars_in,
        tensors_in,
        table,
        w_query,
        w_key,
        w_value,
        w_output,
        w_invariant,
        w_message,
        w_gate,
        w_radial,
        w_mixing,
        w_expand,
        w_reverse,
        w_contract,
        scalars_out,
        tensors_out,
        s_new,
        t_new,
        far,
    ) = refs
    comps, m = tensors_in.shape[:2]
    channels = scalars_in.shape[0]
    features = channels + comps * m
    slots = own.shape[1]

    @pl.when(pl.program_id(0) == 0)
    def _():
        def block_of(g, part, n):
            kind, _ = plan.parts[g][part]
            at = plan.offset(plan.parts[g], part, features)
            if kind == "wide":
                return received[g][at : at + features + EXTRA, n * block : (n + 1) * block]
            half = features // 2
            upper = received[g][at : at + half, :]
            extra = received[g][at + half : at + half + EXTRA, :block]
            return jnp.concatenate([upper[:, :block], upper[:, block:], extra], axis=0)

        for j in range(0, len(plan.facing), 2):
            to = slice(j * block, (j + 2) * block)
            (g, part, n), second = plan.facing[j : j + 2]
            if n == 0 and second == (g, part, 1):
                at = plan.offset(plan.parts[g], part, features)
                far[:, to] = received[g][at : at + features + EXTRA, :]
            else:
                far[:, to] = jnp.concatenate([block_of(g, part, n), block_of(*second)], axis=1)
        s_own, s_far = own[:channels, :], far[:channels, :]
        t_own = [own[channels + k * m : channels + (k + 1) * m, :] for k in range(comps)]
        t_far = [far[channels + k * m : channels + (k + 1) * m, :] for k in range(comps)]
        columns = jnp.transpose(table[...])
        e_own = embed(s_own, columns, own[features : features + 1, :].astype(F32))
        e_far = embed(s_far, columns, far[features : features + 1, :].astype(F32))
        w_shared = nt(eye(channels), w_invariant[...]).astype(BF16)
        shared = mm(w_shared, invariants(t_own, t_far))
        embedded = jnp.concatenate([e_own, e_far], axis=1)
        w_rev = jnp.concatenate([w_key[...], w_value[...]], axis=0)
        both = mm(w_rev, jnp.concatenate([s_far, s_own], axis=1))
        attended = attend(mm(w_query[...], embedded), both[:channels], both[channels:])
        middles = (
            embedded.astype(F32)
            + mm(w_output[...], attended)
            + jnp.concatenate([shared, shared], axis=1)
        ).astype(BF16)
        middle = middles[:, :slots]
        incoming = mm(w_message[...], middles[:, slots:]).astype(BF16)
        w_mid = jnp.concatenate([w_expand[...], w_gate[...], w_radial[...]], axis=0)
        spread = mm(w_mid, middle)
        hidden = w_expand.shape[0]
        v = spread[:hidden] + mm(w_reverse[...], incoming)
        s_new[...] = contract(middle, v, w_contract[...])
        gate = jax.nn.sigmoid(spread[hidden : hidden + 3 * m])
        radial = spread[hidden + 3 * m :]
        mixed = [mm(w_mixing[...], t_far[k]) for k in range(comps)]
        for k, new in update_tensors(t_own, mixed, gate, radial, where[...]):
            t_new[k * m : (k + 1) * m, :] = new

    width = scalars_out.shape[-1]
    here = pl.ds(pl.multiple_of(pl.program_id(0) * width, 128), width)
    onehot = merge[:, here]
    crosses = jnp.broadcast_to((reverse[0, :, here] >= edges).astype(F32), (m, width))
    crosses = crosses.astype(BF16) > 0

    def merged(new, old):
        return jnp.where(crosses, new.astype(BF16), old)

    s_all = mm(s_new[...], onehot)
    for c in range(0, channels, m):
        scalars_out[0, 0, c : c + m] = merged(s_all[c : c + m], scalars_in[c : c + m, here])
    t_all = mm(t_new[...], onehot)
    for k in range(comps):
        tensors_out[0, 0, k] = merged(t_all[k * m : (k + 1) * m], tensors_in[k, :, here])


def resident(*arrays):
    return [pltpu.with_memory_space_constraint(x, pltpu.HBM) for x in arrays]


def whole(*shape):
    return pl.BlockSpec(shape, lambda *_: (0,) * len(shape))


def per_device(gx, gy, *args):
    (
        scalars,
        tensors,
        vectors,
        species,
        table,
        reverse,
        send_index,
        counts,
        w_query,
        w_key,
        w_value,
        w_output,
        w_invariant,
        w_message,
        w_gate,
        w_radial,
        w_mixing,
        w_expand,
        w_reverse,
        w_contract,
    ) = args
    plan = Plan(gx, gy)
    vectors = jnp.transpose(vectors, (0, 2, 1, 3))
    table = jnp.transpose(table)
    w_invariant = jnp.transpose(w_invariant)
    _, _, channels, edges = scalars.shape
    comps, m = tensors.shape[2:4]
    features = channels + comps * m
    block = send_index.shape[-1]
    slots = len(DIRECTIONS) * block
    vmem = pl.BlockSpec(memory_space=pltpu.VMEM)

    def limit(mebibytes):
        return pltpu.CompilerParams(vmem_limit_bytes=mebibytes * 2**20)


    hbm = pl.BlockSpec(memory_space=pltpu.HBM)

    def buffers(*arrays):
        return [pltpu.VMEM(x.shape, x.dtype) for x in arrays] + [
            pltpu.SemaphoreType.DMA((len(arrays),))
        ]

    prepared = (send_index, counts, species, vectors, reverse, scalars, tensors)
    prepared_buffers = buffers(*prepared)
    del prepared_buffers[5:7]
    prepared_buffers[1] = pltpu.SMEM(counts.shape, counts.dtype)
    prepared_buffers.insert(0, pltpu.VMEM((edges, slots), BF16))
    own, where, rows, scalars, tensors, *sends = pl.pallas_call(
        functools.partial(prepare_kernel, plan),
        in_specs=[hbm] * len(prepared),
        out_specs=[vmem] * (5 + len(plan.arrays)),
        out_shape=[
            jax.ShapeDtypeStruct((features + EXTRA, slots), BF16),
            jax.ShapeDtypeStruct((8, slots), F32),
            jax.ShapeDtypeStruct((edges // 128, 128), jnp.int32),
            jax.ShapeDtypeStruct(scalars.shape, BF16),
            jax.ShapeDtypeStruct(tensors.shape, BF16),
        ]
        + [
            jax.ShapeDtypeStruct((plan.rows(parts, features), 2 * block), BF16)
            for parts in plan.arrays
        ],
        scratch_shapes=prepared_buffers,
        compiler_params=limit(24),
        name="prepare",
    )(*resident(*prepared))

    def exchange(x, pairs):
        return lax.ppermute(x, ("gx", "gy"), pairs)

    if plan.paired:
        received = [
            exchange(sends[0], plan.swaps[0]),
            exchange(sends[1], plan.swaps[1]),
            exchange(sends[2], plan.across),
        ]
    else:
        received = [exchange(x, pairs) for x, pairs in zip(sends, plan.pairs)]

    width = 1024 if edges % 1024 == 0 else edges
    steps = edges // width
    flat = whole(channels, edges)
    first_weights = (w_query, w_key, w_value, w_output, w_invariant, w_message, w_gate, w_radial, w_mixing)
    last_weights = (w_expand, w_reverse, w_contract)
    inside = (
        w_mixing, w_invariant, vectors, species, table,
        w_query, w_output, w_key, w_value, w_message, w_gate, w_radial,
    )
    stacked = [pltpu.VMEM((2 * channels, channels), BF16), pltpu.VMEM((channels + 6 * m, channels), BF16)]
    middle, message, t_inside = pl.pallas_call(
        interior_kernel,
        grid=(steps,),
        in_specs=[pl.BlockSpec(memory_space=pltpu.SMEM)]
        + [whole(*scalars.shape), whole(*tensors.shape)]
        + [hbm] * len(inside),
        out_specs=[flat, flat, whole(comps, m, edges)],
        out_shape=[
            jax.ShapeDtypeStruct((channels, edges), BF16),
            jax.ShapeDtypeStruct((channels, edges), BF16),
            jax.ShapeDtypeStruct((comps, m, edges), BF16),
        ],
        scratch_shapes=[
            pltpu.VMEM((edges * 8, 128), F32),
            pltpu.VMEM((width * 8, 128), F32),
            pltpu.VMEM((256, 128), BF16),
            pltpu.VMEM((channels, w_invariant.shape[0]), BF16),
        ]
        + buffers(*inside)[:7]
        + stacked
        + [pltpu.SemaphoreType.DMA((len(inside),))],
        compiler_params=limit(36),
        cost_estimate=pl.CostEstimate(
            flops=2 * edges * edges * features, bytes_accessed=4 * edges * features, transcendentals=0
        ),
        name="interior",
    )(rows, scalars, tensors, *resident(*inside))
    last_weights = (w_expand, w_reverse, w_contract)
    brought = (reverse, *last_weights)
    s_inside, merge = pl.pallas_call(
        functools.partial(incoming_kernel, plan, block),
        grid=(steps,),
        in_specs=[whole(channels, edges), flat, pl.BlockSpec(memory_space=pltpu.SMEM)]
        + [hbm] * len(brought),
        out_specs=[flat, whole(slots, edges)],
        out_shape=[
            jax.ShapeDtypeStruct((channels, edges), BF16),
            jax.ShapeDtypeStruct((slots, edges), BF16),
        ],
        scratch_shapes=[
            pltpu.VMEM((edges * 8, 128), F32),
            pltpu.VMEM((width * 8, 128), F32),
        ]
        + buffers(*brought),
        compiler_params=limit(24),
        cost_estimate=pl.CostEstimate(
            flops=4 * edges * edges * channels, bytes_accessed=8 * edges * channels, transcendentals=0
        ),
        name="incoming",
    )(message, middle, rows, *resident(*brought))
    if plan.paired:
        held = lax.optimization_barrier((received[0], received[1], s_inside))
        received[0], received[1], s_inside = held
        received.append(exchange(received[0], plan.across))
        received.append(exchange(received[1], plan.across))

    return pl.pallas_call(
        functools.partial(boundary_kernel, plan, block, edges),
        grid=(steps,),
        in_specs=[whole(*r.shape) for r in received]
        + [whole(*own.shape), whole(*where.shape), whole(slots, edges)]
        + [whole(*reverse.shape), flat, whole(comps, m, edges), whole(*table.shape)]
        + [whole(*w.shape) for w in first_weights + last_weights],
        out_specs=[
            pl.BlockSpec((1, 1, channels, width), lambda i: (0, 0, 0, i)),
            pl.BlockSpec((1, 1, comps, m, width), lambda i: (0, 0, 0, 0, i)),
        ],
        out_shape=[
            jax.ShapeDtypeStruct(scalars.shape, BF16),
            jax.ShapeDtypeStruct(tensors.shape, BF16),
        ],
        scratch_shapes=[
            pltpu.VMEM((channels, slots), BF16),
            pltpu.VMEM((comps * m, slots), BF16),
            pltpu.VMEM((features + EXTRA, slots), BF16),
        ],
        compiler_params=limit(26),
        cost_estimate=pl.CostEstimate(
            flops=2 * edges * slots * features, bytes_accessed=8 * edges * features, transcendentals=0
        ),
        name="boundary",
    )(*received, own, where, merge, reverse, s_inside, t_inside, table, *first_weights, *last_weights)


def solution(mesh):
    gx, gy = mesh.shape["gx"], mesh.shape["gy"]

    def body(*args):
        return per_device(gx, gy, *args)

    step = jax.shard_map(
        body,
        mesh=mesh,
        in_specs=(
            P("gx", "gy", None, None),
            P("gx", "gy", None, None, None),
            P("gx", "gy", None, None),
            P("gx", "gy", None),
            P(),
            P("gx", "gy", None),
            P("gx", "gy", None, None),
            P("gx", "gy", None),
        )
        + (P(),) * 12,
        out_specs=(P("gx", "gy", None, None), P("gx", "gy", None, None, None)),
        check_vma=False,
    )
    if not Plan(gx, gy).paired:
        return step
    return step
```

```python
import functools
import math

import jax
import jax.numpy as jnp
from jax import lax
from jax.experimental import pallas as pl
from jax.experimental.pallas import tpu as pltpu
from jax.sharding import PartitionSpec as P


HEADS = 8
DIRECTIONS = ((1, 0), (-1, 0), (0, 1), (0, -1), (1, 1), (1, -1), (-1, 1), (-1, -1))
OPPOSITE = tuple(DIRECTIONS.index((-dx, -dy)) for dx, dy in DIRECTIONS)
EXTRA = 16
BF16 = jnp.bfloat16
F32 = jnp.float32


def ring(gx, gy, dx, dy):
    return tuple(
        (a * gy + b, ((a + dx) % gx) * gy + (b + dy) % gy) for a in range(gx) for b in range(gy)
    )


class Plan:
    def __init__(self, gx, gy):
        self.paired = gx % 2 == 0 and gy == 2
        if self.paired:
            self.orders = ((4, 5, 7, 6, 0, 1, 2, 3), (7, 6, 4, 5, 1, 0, 2, 3))
            self.arrays = ((("wide", 0), ("fold", 4)), (("wide", 2), ("fold", 5)), (("wide", 6),))
            self.facing = (
                (3, 0, 0), (3, 0, 1), (4, 0, 0), (4, 0, 1), (0, 1, 0), (1, 1, 0), (2, 0, 1), (2, 0, 0),
            )
            self.parts = self.arrays + self.arrays[:2]
            even = [(a, a + 1 - 2 * (a % 2)) for a in range(gx)]
            odd = [(a, (a - 1 + 2 * (a % 2)) % gx) for a in range(gx)]
            self.swaps = [
                tuple((a * gy + b, c * gy + b) for a, c in pairs for b in range(gy))
                for pairs in (even, odd)
            ]
            self.across = ring(gx, gy, 0, 1)
        else:
            groups = {}
            for p in (4, 5, 7, 6, 0, 1, 2, 3):
                groups.setdefault(ring(gx, gy, *DIRECTIONS[p]), []).append(p)
            order, self.arrays, place = [], (), {}
            for g, members in enumerate(groups.values()):
                parts = ()
                rest = members
                while rest:
                    taken = 2 if len(rest) > 1 else 1
                    for n, p in enumerate(rest[:taken]):
                        place[p] = (g, len(parts), n)
                    parts += (("wide" if taken == 2 else "fold", len(order)),)
                    order += rest[:taken]
                    rest = rest[taken:]
                self.arrays += (parts,)
            self.orders = (tuple(order),) * 2
            self.parts = self.arrays
            self.facing = tuple(place[OPPOSITE[p]] for p in order)
            self.pairs = list(groups)

    def part_rows(self, kind, features):
        return features + EXTRA if kind == "wide" else features // 2 + EXTRA

    def offset(self, parts, number, features):
        return sum(self.part_rows(kind, features) for kind, _ in parts[:number])

    def rows(self, parts, features):
        return self.offset(parts, len(parts), features)


def pick(odd, pair):
    return pair[0] if pair[0] == pair[1] else jnp.where(odd, pair[1], pair[0])


def mm(a, b):
    return jnp.dot(a, b, preferred_element_type=F32)


def nt(a, b):
    return lax.dot_general(a, b, (((1,), (1,)), ((), ())), preferred_element_type=F32)


def eye(n):
    rows = lax.broadcasted_iota(jnp.int32, (n, n), 0)
    return (rows == lax.broadcasted_iota(jnp.int32, (n, n), 1)).astype(BF16)


def embed(own, table, species):
    picked = table[:, 3:4]
    for j in (2, 1, 0):
        picked = jnp.where(species == j, table[:, j : j + 1], picked)
    return (own.astype(F32) + picked).astype(BF16)


def attend(queries, keys, values):
    channels, _ = queries.shape
    size = channels // HEADS
    product = queries * keys
    parts = []
    for h in range(HEADS):
        rows = slice(h * size, (h + 1) * size)
        score = jnp.sum(product[rows], axis=0, keepdims=True) * (1.0 / math.sqrt(size))
        parts.append(jax.nn.sigmoid(score) * values[rows])
    return jnp.concatenate(parts, axis=0).astype(BF16)


def invariants(own, rev):
    product = [own[k].astype(F32) * rev[k].astype(F32) for k in range(9)]
    return jnp.concatenate(
        [
            product[0],
            product[1] + product[2] + product[3],
            product[4] + product[5] + product[6] + product[7] + product[8],
        ],
        axis=0,
    ).astype(BF16)


def harmonics(vectors):
    x, y, z = vectors[0:1], vectors[1:2], vectors[2:3]
    r2 = x * x + y * y + z * z
    root = math.sqrt(3.0)
    return (
        None,
        x,
        y,
        z,
        root * x * y,
        root * y * z,
        0.5 * (3.0 * z * z - r2),
        root * x * z,
        0.5 * root * (x * x - y * y),
    )


def update_tensors(own, mixed, gate, radial, vectors):
    m = own[0].shape[0]
    harmonic = harmonics(vectors)
    for k in range(9):
        degree = 0 if k == 0 else (1 if k < 4 else 2)
        rows = slice(degree * m, (degree + 1) * m)
        tail = radial[rows] if harmonic[k] is None else radial[rows] * harmonic[k]
        yield k, (own[k].astype(F32) + gate[rows] * mixed[k] + tail).astype(BF16)


def contract(middle, v, w_contract):
    hidden = (v * jax.nn.sigmoid(v)).astype(BF16)
    return (middle.astype(F32) + mm(w_contract, hidden)).astype(BF16)


def fetch(sources, buffers, sem):
    pieces = []
    waiting = list(sources)
    for buffer in buffers:
        at = 0
        while at < buffer.shape[0]:
            source = waiting.pop(0)
            part = buffer if source.shape == buffer.shape else buffer.at[pl.ds(at, source.shape[0])]
            pieces.append((source, part))
            at += source.shape[0]
    copies = [pltpu.make_async_copy(*piece, sem.at[n]) for n, piece in enumerate(pieces)]
    for copy in copies:
        copy.start()
    return copies


def prepare_kernel(plan, *refs):
    inputs, (own, where, rows, scalars, tensors), refs = refs[:7], refs[7:12], refs[12:]
    sends, (onehot, *buffers, sem) = refs[: len(plan.arrays)], refs[len(plan.arrays) :]
    copies = fetch(inputs, (*buffers, scalars, tensors), sem)
    send_index, counts, species, vectors, reverse = buffers
    channels, edges = scalars.shape[2:]
    comps, m = tensors.shape[2:4]
    block = send_index.shape[-1]
    features = channels + comps * m
    odd = lax.rem(lax.axis_index("gx"), 2) == 1
    lane = lax.broadcasted_iota(jnp.int32, (1, block), 1)
    for copy in copies[:5]:
        copy.wait()

    def live(p):
        return jnp.where(lane < counts[0, 0, p], send_index[0, 0, p : p + 1, :], -1)

    index = jnp.concatenate(
        [
            live(p) if p == q else jnp.where(odd, live(q), live(p))
            for p, q in zip(*plan.orders)
        ],
        axis=1,
    )
    slots = index.shape[1]
    onehot[...] = (lax.broadcasted_iota(jnp.int32, (edges, slots), 0) == index).astype(BF16)
    near = jnp.minimum(reverse[0], edges - 1) * 8
    rows[...] = jnp.concatenate(
        [near[:, j * 128 : (j + 1) * 128] for j in range(edges // 128)], axis=0
    )
    vec = jnp.concatenate([vectors[0, j] for j in range(3)], axis=0)
    high = vec.astype(BF16)
    left = vec - high.astype(F32)
    mid = left.astype(BF16)
    low = (left - mid.astype(F32)).astype(BF16)
    extra = jnp.concatenate(
        [
            jnp.broadcast_to(species[0].astype(F32), (7, edges)),
            high.astype(F32),
            mid.astype(F32),
            low.astype(F32),
        ],
        axis=0,
    ).astype(BF16)
    extra = mm(extra, onehot[...])
    where[0:3, :] = extra[7:10] + extra[10:13] + extra[13:16]
    where[3:8, :] = jnp.zeros((5, slots), F32)
    own[features:, :] = jnp.broadcast_to(extra[0:1], (EXTRA, slots)).astype(BF16)
    copies[5].wait()
    own[:channels, :] = mm(scalars[0, 0], onehot[...]).astype(BF16)
    copies[6].wait()
    own[channels:features, :] = mm(
        tensors[0, 0].reshape(comps * m, edges), onehot[...]
    ).astype(BF16)
    half = features // 2
    for send, parts in zip(sends, plan.arrays):
        at = 0
        for kind, j in parts:
            if kind == "wide":
                send[at : at + features + EXTRA, :] = own[:, j * block : (j + 2) * block]
            else:
                piece = own[:, j * block : (j + 1) * block]
                send[at : at + half, :] = jnp.concatenate(
                    [piece[:half], piece[half:features]], axis=1
                )
                send[at + half : at + half + EXTRA, :] = jnp.concatenate(
                    [piece[features:], piece[features:]], axis=1
                )
            at += plan.part_rows(kind, features)


def copy_rows(step, table, rows, gathered):
    per = rows.shape[1]
    width = gathered.shape[0] // 8
    for t in range(rows.shape[0] * per // width):

        @pl.when(step == t)
        def _(first=t * width):
            for e in range(width):
                n = first + e
                source = pl.ds(pl.multiple_of(rows[n // per, n % per], 8), 8)
                gathered[e * 8 : e * 8 + 8, :] = table[source, :]


def interior_kernel(rows, scalars, tensors, *refs):
    inputs, refs = refs[:12], refs[12:]
    middle_out, message_out, tensors_out, edge_rows, gathered, pair_mix, w_shared, *refs = refs
    buffers, sem = refs[:-1], refs[-1]
    (
        w_mixing,
        w_invariant,
        vectors,
        species,
        table,
        w_query,
        w_output,
        w_rev,
        w_mid,
    ) = buffers
    edges = scalars.shape[-1]
    width = gathered.shape[0] // 8
    channels = scalars.shape[2]
    comps, m = tensors.shape[2:4]
    step = pl.program_id(0)
    here = pl.ds(pl.multiple_of(step * width, 128), width)
    pairs = [(k, k + 1) for k in range(0, comps - 1, 2)] + [(comps - 2, comps - 1)]

    @pl.when(step == 0)
    def _():
        copies = fetch(inputs, buffers, sem)
        unit = eye(256)
        half = eye(128)

        def turn(at, j, piece):
            turned = nt(unit, piece)
            for c in range(0, piece.shape[0], 128):
                edge_rows[pl.ds(at * 8 + j + c // 128, 256, stride=8), :] = turned[:, c : c + 128]

        for at in range(0, edges, 256):
            for c in range(0, channels, 256):
                turn(at, c // 128, scalars[0, 0, c : c + 256, at : at + 256])
        for at in range(0, edges, 256):
            n = 0
            while n < len(pairs):
                taken = 2 if n + 2 < len(pairs) else 1
                k = pairs[n][0]
                piece = tensors[0, 0, k : k + 2 * taken, :, at : at + 256].reshape(-1, 256)
                turn(at, channels // 128 + n, piece)
                n += taken
        for copy in copies:
            copy.wait()
        mixing = w_mixing[...].astype(F32)
        zero = jnp.zeros((m, m), F32)
        pair_mix[...] = jnp.concatenate(
            [
                half.astype(F32),
                jnp.concatenate([mixing, zero], axis=1),
                jnp.concatenate([zero, mixing], axis=1),
            ],
            axis=0,
        ).astype(BF16)
        w_shared[...] = nt(unit, w_invariant[...]).astype(BF16)

    copy_rows(step, edge_rows, rows, gathered)

    def feature(j):
        return gathered[pl.ds(j, width, stride=8), :].astype(BF16)

    lead = channels // 128
    s_rev = jnp.concatenate([feature(j) for j in range(lead)], axis=1)
    t_rev, mixed = {}, {}
    for j, (first, second) in enumerate(pairs):
        both = nt(pair_mix[...], feature(lead + j))
        t_rev[first], t_rev[second] = both[:m], both[m : 2 * m]
        mixed[first], mixed[second] = both[2 * m : 3 * m], both[3 * m :]
    embedded = embed(scalars[0, 0, :, here], jnp.transpose(table[...]), species[0, :, here])
    both = nt(w_rev[...], s_rev)
    attended = attend(mm(w_query[...], embedded), both[:channels], both[channels:])
    own_t = [tensors[0, 0, k, :, here] for k in range(comps)]
    middle = (
        embedded.astype(F32)
        + mm(w_output[...], attended)
        + mm(w_shared[...], invariants(own_t, t_rev))
    ).astype(BF16)
    middle_out[:, here] = middle
    spread = mm(w_mid[...], middle)
    message_out[:, here] = spread[:channels].astype(BF16)
    gate = jax.nn.sigmoid(spread[channels : channels + 3 * m])
    radial = spread[channels + 3 * m :]
    vec = jnp.concatenate([vectors[0, j, :, here] for j in range(3)], axis=0)
    for k, new in update_tensors(own_t, mixed, gate, radial, vec):
        tensors_out[k, :, here] = new


def incoming_kernel(plan, block, message, middle, rows, *refs):
    inputs, (scalars_out, merge, edge_rows, gathered, *buffers, sem) = refs[:4], refs[4:]
    reverse, w_expand, w_reverse, w_contract = buffers
    channels, edges = message.shape
    width = gathered.shape[0] // 8
    step = pl.program_id(0)
    here = pl.ds(pl.multiple_of(step * width, 128), width)

    @pl.when(step == 0)
    def _():
        copies = fetch(inputs, buffers, sem)
        unit = eye(256)
        for at in range(0, edges, 256):
            for first in range(0, channels, 256):
                turned = nt(unit, message[first : first + 256, at : at + 256])
                for c in range(0, 256, 128):
                    row = at * 8 + (first + c) // 128
                    edge_rows[pl.ds(row, 256, stride=8), :] = turned[:, c : c + 128]
        for copy in copies:
            copy.wait()

    copy_rows(step, edge_rows, rows, gathered)
    incoming = jnp.concatenate(
        [
            gathered[pl.ds(j, width, stride=8), :].astype(BF16)
            for j in range(channels // 128)
        ],
        axis=1,
    )
    v = mm(w_expand[...], middle[:, here]) + nt(w_reverse[...], incoming)
    scalars_out[:, here] = contract(middle[:, here], v, w_contract[...])
    target = reverse[0, :, here] - edges
    odd = lax.rem(lax.axis_index("gx"), 2) == 1
    at = lax.broadcasted_iota(jnp.int32, (block, width), 0)
    for j, (p, q) in enumerate(zip(*plan.orders)):
        merge[j * block : (j + 1) * block, here] = (
            at + pick(odd, (OPPOSITE[p], OPPOSITE[q])) * block == target
        ).astype(BF16)


def settle(plan, block, positions, base, received, own, where, table, weights, far, s_new, t_new):
    (
        w_query,
        w_key,
        w_value,
        w_output,
        w_invariant,
        w_message,
        w_gate,
        w_radial,
        w_mixing,
        w_expand,
        w_reverse,
        w_contract,
    ) = weights
    m = w_mixing.shape[0]
    channels = w_query.shape[0]
    comps = t_new.shape[0] // m
    features = channels + comps * m
    columns = slice(positions[0] * block, (positions[-1] + 1) * block)
    slots = len(positions) * block

    def block_of(g, part, n):
        kind, _ = plan.parts[g][part]
        at = plan.offset(plan.parts[g], part, features)
        if kind == "wide":
            return received[g - base][at : at + features + EXTRA, n * block : (n + 1) * block]
        half = features // 2
        upper = received[g - base][at : at + half, :]
        extra = received[g - base][at + half : at + half + EXTRA, :block]
        return jnp.concatenate([upper[:, :block], upper[:, block:], extra], axis=0)

    for j in range(0, len(positions), 2):
        to = slice(j * block, (j + 2) * block)
        (g, part, n), second = (plan.facing[p] for p in positions[j : j + 2])
        if n == 0 and second == (g, part, 1):
            at = plan.offset(plan.parts[g], part, features)
            far[:, to] = received[g - base][at : at + features + EXTRA, :]
        else:
            far[:, to] = jnp.concatenate([block_of(g, part, n), block_of(*second)], axis=1)
    s_own, s_far = own[:channels, columns], far[:channels, :]
    t_own = [own[channels + k * m : channels + (k + 1) * m, columns] for k in range(comps)]
    t_far = [far[channels + k * m : channels + (k + 1) * m, :] for k in range(comps)]
    picks = jnp.transpose(table[...])
    e_own = embed(s_own, picks, own[features : features + 1, columns].astype(F32))
    e_far = embed(s_far, picks, far[features : features + 1, :].astype(F32))
    w_shared = nt(eye(channels), w_invariant[...]).astype(BF16)
    shared = mm(w_shared, invariants(t_own, t_far))
    embedded = jnp.concatenate([e_own, e_far], axis=1)
    w_rev = jnp.concatenate([w_key[...], w_value[...]], axis=0)
    both = mm(w_rev, jnp.concatenate([s_far, s_own], axis=1))
    attended = attend(mm(w_query[...], embedded), both[:channels], both[channels:])
    middles = (
        embedded.astype(F32)
        + mm(w_output[...], attended)
        + jnp.concatenate([shared, shared], axis=1)
    ).astype(BF16)
    middle = middles[:, :slots]
    incoming = mm(w_message[...], middles[:, slots:]).astype(BF16)
    w_mid = jnp.concatenate([w_expand[...], w_gate[...], w_radial[...]], axis=0)
    spread = mm(w_mid, middle)
    hidden = w_expand.shape[0]
    v = spread[:hidden] + mm(w_reverse[...], incoming)
    s_new[...] = contract(middle, v, w_contract[...])
    gate = jax.nn.sigmoid(spread[hidden : hidden + 3 * m])
    radial = spread[hidden + 3 * m :]
    mixed = [mm(w_mixing[...], t_far[k]) for k in range(comps)]
    for k, new in update_tensors(t_own, mixed, gate, radial, where[:, columns]):
        t_new[k * m : (k + 1) * m, :] = new


def near_kernel(plan, block, positions, *refs):
    received, (own, where, table, *refs) = refs[:3], refs[3:]
    weights, (s_new, t_new, far) = refs[:12], refs[12:]
    settle(plan, block, positions, 0, received, own, where, table, weights, far, s_new, t_new)


def boundary_kernel(plan, block, positions, base, count, done, edges, *refs):
    received, refs = refs[:count], refs[count:]
    settled, (own, where, merge, reverse, scalars_in, tensors_in, table, *refs) = (
        refs[:done],
        refs[done:],
    )
    weights, (scalars_out, tensors_out, s_new, t_new, far) = refs[:12], refs[12:]
    comps, m = tensors_in.shape[:2]
    channels = scalars_in.shape[0]

    @pl.when(pl.program_id(0) == 0)
    def _():
        settle(
            plan, block, positions, base, received, own, where, table, weights, far, s_new, t_new
        )

    width = scalars_out.shape[-1]
    here = pl.ds(pl.multiple_of(pl.program_id(0) * width, 128), width)
    first = len(positions) * block
    crosses = jnp.broadcast_to((reverse[0, :, here] >= edges).astype(F32), (m, width))
    crosses = crosses.astype(BF16) > 0

    def spread(new, n):
        total = mm(new[...], merge[:first, here])
        if done:
            total = total + mm(settled[n][...], merge[first:, here])
        return total

    def merged(new, old):
        return jnp.where(crosses, new.astype(BF16), old)

    s_all = spread(s_new, 0)
    for c in range(0, channels, m):
        scalars_out[0, 0, c : c + m] = merged(s_all[c : c + m], scalars_in[c : c + m, here])
    t_all = spread(t_new, 1)
    for k in range(comps):
        tensors_out[0, 0, k] = merged(t_all[k * m : (k + 1) * m], tensors_in[k, :, here])


def resident(*arrays):
    return [pltpu.with_memory_space_constraint(x, pltpu.HBM) for x in arrays]


def whole(*shape):
    return pl.BlockSpec(shape, lambda *_: (0,) * len(shape))


def per_device(gx, gy, *args):
    (
        scalars,
        tensors,
        vectors,
        species,
        table,
        reverse,
        send_index,
        counts,
        w_query,
        w_key,
        w_value,
        w_output,
        w_invariant,
        w_message,
        w_gate,
        w_radial,
        w_mixing,
        w_expand,
        w_reverse,
        w_contract,
    ) = args
    plan = Plan(gx, gy)
    vectors = jnp.transpose(vectors, (0, 2, 1, 3))
    table = jnp.transpose(table)
    w_invariant = jnp.transpose(w_invariant)
    _, _, channels, edges = scalars.shape
    comps, m = tensors.shape[2:4]
    features = channels + comps * m
    block = send_index.shape[-1]
    slots = len(DIRECTIONS) * block
    vmem = pl.BlockSpec(memory_space=pltpu.VMEM)

    def limit(mebibytes):
        return pltpu.CompilerParams(vmem_limit_bytes=mebibytes * 2**20)


    hbm = pl.BlockSpec(memory_space=pltpu.HBM)

    def buffers(*arrays):
        return [pltpu.VMEM(x.shape, x.dtype) for x in arrays] + [
            pltpu.SemaphoreType.DMA((len(arrays),))
        ]

    prepared = (send_index, counts, species, vectors, reverse, scalars, tensors)
    prepared_buffers = buffers(*prepared)
    del prepared_buffers[5:7]
    prepared_buffers[1] = pltpu.SMEM(counts.shape, counts.dtype)
    prepared_buffers.insert(0, pltpu.VMEM((edges, slots), BF16))
    own, where, rows, scalars, tensors, *sends = pl.pallas_call(
        functools.partial(prepare_kernel, plan),
        in_specs=[hbm] * len(prepared),
        out_specs=[vmem] * (5 + len(plan.arrays)),
        out_shape=[
            jax.ShapeDtypeStruct((features + EXTRA, slots), BF16),
            jax.ShapeDtypeStruct((8, slots), F32),
            jax.ShapeDtypeStruct((edges // 128, 128), jnp.int32),
            jax.ShapeDtypeStruct(scalars.shape, BF16),
            jax.ShapeDtypeStruct(tensors.shape, BF16),
        ]
        + [
            jax.ShapeDtypeStruct((plan.rows(parts, features), 2 * block), BF16)
            for parts in plan.arrays
        ],
        scratch_shapes=prepared_buffers,
        compiler_params=limit(24),
        name="prepare",
    )(*resident(*prepared))

    def exchange(x, pairs):
        return lax.ppermute(x, ("gx", "gy"), pairs)

    if plan.paired:
        received = [
            exchange(sends[0], plan.swaps[0]),
            exchange(sends[1], plan.swaps[1]),
            exchange(sends[2], plan.across),
        ]
    else:
        received = [exchange(x, pairs) for x, pairs in zip(sends, plan.pairs)]

    width = 1024 if edges % 1024 == 0 else edges
    steps = edges // width
    flat = whole(channels, edges)
    first_weights = (w_query, w_key, w_value, w_output, w_invariant, w_message, w_gate, w_radial, w_mixing)
    last_weights = (w_expand, w_reverse, w_contract)
    inside = (
        w_mixing, w_invariant, vectors, species, table,
        w_query, w_output, w_key, w_value, w_message, w_gate, w_radial,
    )
    stacked = [pltpu.VMEM((2 * channels, channels), BF16), pltpu.VMEM((channels + 6 * m, channels), BF16)]
    middle, message, t_inside = pl.pallas_call(
        interior_kernel,
        grid=(steps,),
        in_specs=[pl.BlockSpec(memory_space=pltpu.SMEM)]
        + [whole(*scalars.shape), whole(*tensors.shape)]
        + [hbm] * len(inside),
        out_specs=[flat, flat, whole(comps, m, edges)],
        out_shape=[
            jax.ShapeDtypeStruct((channels, edges), BF16),
            jax.ShapeDtypeStruct((channels, edges), BF16),
            jax.ShapeDtypeStruct((comps, m, edges), BF16),
        ],
        scratch_shapes=[
            pltpu.VMEM((edges * 8, 128), F32),
            pltpu.VMEM((width * 8, 128), F32),
            pltpu.VMEM((256, 128), BF16),
            pltpu.VMEM((channels, w_invariant.shape[0]), BF16),
        ]
        + buffers(*inside)[:7]
        + stacked
        + [pltpu.SemaphoreType.DMA((len(inside),))],
        compiler_params=limit(36),
        cost_estimate=pl.CostEstimate(
            flops=2 * edges * edges * features, bytes_accessed=4 * edges * features, transcendentals=0
        ),
        name="interior",
    )(rows, scalars, tensors, *resident(*inside))
    last_weights = (w_expand, w_reverse, w_contract)
    brought = (reverse, *last_weights)
    s_inside, merge = pl.pallas_call(
        functools.partial(incoming_kernel, plan, block),
        grid=(steps,),
        in_specs=[whole(channels, edges), flat, pl.BlockSpec(memory_space=pltpu.SMEM)]
        + [hbm] * len(brought),
        out_specs=[flat, whole(slots, edges)],
        out_shape=[
            jax.ShapeDtypeStruct((channels, edges), BF16),
            jax.ShapeDtypeStruct((slots, edges), BF16),
        ],
        scratch_shapes=[
            pltpu.VMEM((edges * 8, 128), F32),
            pltpu.VMEM((width * 8, 128), F32),
        ]
        + buffers(*brought),
        compiler_params=limit(24),
        cost_estimate=pl.CostEstimate(
            flops=4 * edges * edges * channels, bytes_accessed=8 * edges * channels, transcendentals=0
        ),
        name="incoming",
    )(message, middle, rows, *resident(*brought))
    if plan.paired:
        held = lax.optimization_barrier((received[0], received[1], s_inside))
        received[0], received[1], s_inside = held
        relayed = [exchange(received[0], plan.across), exchange(received[1], plan.across)]
        positions, near = tuple(range(4)), tuple(range(4, 8))
        columns = len(near) * block
        settled = pl.pallas_call(
            functools.partial(near_kernel, plan, block, near),
            in_specs=[vmem] * (6 + len(first_weights + last_weights)),
            out_specs=[vmem, vmem],
            out_shape=[
                jax.ShapeDtypeStruct((channels, columns), BF16),
                jax.ShapeDtypeStruct((comps * m, columns), BF16),
            ],
            scratch_shapes=[pltpu.VMEM((features + EXTRA, columns), BF16)],
            compiler_params=limit(16),
            cost_estimate=pl.CostEstimate(
                flops=4 * columns * channels * features, bytes_accessed=4 * columns * features, transcendentals=0
            ),
            name="near",
        )(*received, own, where, table, *first_weights, *last_weights)
        base, received = 3, relayed
    else:
        positions, base, settled = tuple(range(len(DIRECTIONS))), 0, []

    columns = len(positions) * block
    return pl.pallas_call(
        functools.partial(
            boundary_kernel, plan, block, positions, base, len(received), len(settled), edges
        ),
        grid=(steps,),
        in_specs=[whole(*r.shape) for r in (*received, *settled)]
        + [whole(*own.shape), whole(*where.shape), whole(slots, edges)]
        + [whole(*reverse.shape), flat, whole(comps, m, edges), whole(*table.shape)]
        + [whole(*w.shape) for w in first_weights + last_weights],
        out_specs=[
            pl.BlockSpec((1, 1, channels, width), lambda i: (0, 0, 0, i)),
            pl.BlockSpec((1, 1, comps, m, width), lambda i: (0, 0, 0, 0, i)),
        ],
        out_shape=[
            jax.ShapeDtypeStruct((1, 1, channels, edges), BF16),
            jax.ShapeDtypeStruct((1, 1, comps, m, edges), BF16),
        ],
        scratch_shapes=[
            pltpu.VMEM((channels, columns), BF16),
            pltpu.VMEM((comps * m, columns), BF16),
            pltpu.VMEM((features + EXTRA, columns), BF16),
        ],
        compiler_params=limit(26),
        cost_estimate=pl.CostEstimate(
            flops=2 * edges * slots * features, bytes_accessed=8 * edges * features, transcendentals=0
        ),
        name="boundary",
    )(
        *received, *settled, own, where, merge, reverse, s_inside, t_inside, table,
        *first_weights, *last_weights,
    )


def solution(mesh):
    gx, gy = mesh.shape["gx"], mesh.shape["gy"]

    def body(*args):
        return per_device(gx, gy, *args)

    step = jax.shard_map(
        body,
        mesh=mesh,
        in_specs=(
            P("gx", "gy", None, None),
            P("gx", "gy", None, None, None),
            P("gx", "gy", None, None),
            P("gx", "gy", None),
            P(),
            P("gx", "gy", None),
            P("gx", "gy", None, None),
            P("gx", "gy", None),
        )
        + (P(),) * 12,
        out_specs=(P("gx", "gy", None, None), P("gx", "gy", None, None, None)),
        check_vma=False,
    )
    if not Plan(gx, gy).paired:
        return step
    return step
```

```python
import functools
import math

import jax
import jax.numpy as jnp
from jax import lax
from jax.experimental import pallas as pl
from jax.experimental.pallas import tpu as pltpu
from jax.sharding import PartitionSpec as P


HEADS = 8
DIRECTIONS = ((1, 0), (-1, 0), (0, 1), (0, -1), (1, 1), (1, -1), (-1, 1), (-1, -1))
OPPOSITE = tuple(DIRECTIONS.index((-dx, -dy)) for dx, dy in DIRECTIONS)
EXTRA = 16
BF16 = jnp.bfloat16
F32 = jnp.float32


def ring(gx, gy, dx, dy):
    return tuple(
        (a * gy + b, ((a + dx) % gx) * gy + (b + dy) % gy) for a in range(gx) for b in range(gy)
    )


class Plan:
    def __init__(self, gx, gy):
        self.paired = gx % 2 == 0 and gy == 2
        if self.paired:
            self.orders = ((4, 5, 7, 6, 0, 1, 2, 3), (7, 6, 4, 5, 1, 0, 2, 3))
            self.arrays = ((("wide", 0), ("fold", 4)), (("wide", 2), ("fold", 5)), (("wide", 6),))
            self.facing = (
                (3, 0, 0), (3, 0, 1), (4, 0, 0), (4, 0, 1), (0, 1, 0), (1, 1, 0), (2, 0, 1), (2, 0, 0),
            )
            self.parts = self.arrays + self.arrays[:2]
            even = [(a, a + 1 - 2 * (a % 2)) for a in range(gx)]
            odd = [(a, (a - 1 + 2 * (a % 2)) % gx) for a in range(gx)]
            self.swaps = [
                tuple((a * gy + b, c * gy + b) for a, c in pairs for b in range(gy))
                for pairs in (even, odd)
            ]
            self.across = ring(gx, gy, 0, 1)
        else:
            groups = {}
            for p in (4, 5, 7, 6, 0, 1, 2, 3):
                groups.setdefault(ring(gx, gy, *DIRECTIONS[p]), []).append(p)
            order, self.arrays, place = [], (), {}
            for g, members in enumerate(groups.values()):
                parts = ()
                rest = members
                while rest:
                    taken = 2 if len(rest) > 1 else 1
                    for n, p in enumerate(rest[:taken]):
                        place[p] = (g, len(parts), n)
                    parts += (("wide" if taken == 2 else "fold", len(order)),)
                    order += rest[:taken]
                    rest = rest[taken:]
                self.arrays += (parts,)
            self.orders = (tuple(order),) * 2
            self.parts = self.arrays
            self.facing = tuple(place[OPPOSITE[p]] for p in order)
            self.pairs = list(groups)

    def part_rows(self, kind, features):
        return features + EXTRA if kind == "wide" else features // 2 + EXTRA

    def offset(self, parts, number, features):
        return sum(self.part_rows(kind, features) for kind, _ in parts[:number])

    def rows(self, parts, features):
        return self.offset(parts, len(parts), features)


def pick(odd, pair):
    return pair[0] if pair[0] == pair[1] else jnp.where(odd, pair[1], pair[0])


def mm(a, b):
    return jnp.dot(a, b, preferred_element_type=F32)


def nt(a, b):
    return lax.dot_general(a, b, (((1,), (1,)), ((), ())), preferred_element_type=F32)


def eye(n):
    rows = lax.broadcasted_iota(jnp.int32, (n, n), 0)
    return (rows == lax.broadcasted_iota(jnp.int32, (n, n), 1)).astype(BF16)


def embed(own, table, species):
    picked = table[:, 3:4]
    for j in (2, 1, 0):
        picked = jnp.where(species == j, table[:, j : j + 1], picked)
    return (own.astype(F32) + picked).astype(BF16)


def attend(queries, keys, values):
    channels, _ = queries.shape
    size = channels // HEADS
    product = queries * keys
    parts = []
    for h in range(HEADS):
        rows = slice(h * size, (h + 1) * size)
        score = jnp.sum(product[rows], axis=0, keepdims=True) * (1.0 / math.sqrt(size))
        parts.append(jax.nn.sigmoid(score) * values[rows])
    return jnp.concatenate(parts, axis=0).astype(BF16)


def invariants(own, rev):
    product = [own[k].astype(F32) * rev[k].astype(F32) for k in range(9)]
    return jnp.concatenate(
        [
            product[0],
            product[1] + product[2] + product[3],
            product[4] + product[5] + product[6] + product[7] + product[8],
        ],
        axis=0,
    ).astype(BF16)


def harmonics(vectors):
    x, y, z = vectors[0:1], vectors[1:2], vectors[2:3]
    r2 = x * x + y * y + z * z
    root = math.sqrt(3.0)
    return (
        None,
        x,
        y,
        z,
        root * x * y,
        root * y * z,
        0.5 * (3.0 * z * z - r2),
        root * x * z,
        0.5 * root * (x * x - y * y),
    )


def update_tensors(own, mixed, gate, radial, vectors):
    m = own[0].shape[0]
    harmonic = harmonics(vectors)
    for k in range(9):
        degree = 0 if k == 0 else (1 if k < 4 else 2)
        rows = slice(degree * m, (degree + 1) * m)
        tail = radial[rows] if harmonic[k] is None else radial[rows] * harmonic[k]
        yield k, (own[k].astype(F32) + gate[rows] * mixed[k] + tail).astype(BF16)


def contract(middle, v, w_contract):
    hidden = (v * jax.nn.sigmoid(v)).astype(BF16)
    return (middle.astype(F32) + mm(w_contract, hidden)).astype(BF16)


def fetch(sources, buffers, sem):
    pieces = []
    waiting = list(sources)
    for buffer in buffers:
        at = 0
        while at < buffer.shape[0]:
            source = waiting.pop(0)
            same = source.shape == buffer.shape
            part = buffer if same else buffer.at[pl.ds(at, source.shape[0])]
            pieces.append((source, part))
            at += source.shape[0]
    copies = [pltpu.make_async_copy(*piece, sem.at[n]) for n, piece in enumerate(pieces)]
    for copy in copies:
        copy.start()
    return copies


def prepare_kernel(plan, *refs):
    inputs, (own, where, rows, scalars, tensors), refs = refs[:7], refs[7:12], refs[12:]
    sends, (onehot, *buffers, sem) = refs[: len(plan.arrays)], refs[len(plan.arrays) :]
    comps = tensors.shape[2]
    chunks = [pl.ds(k, min(4, comps - k)) for k in range(0, comps, 4)]
    copies = fetch(
        (*inputs[:6], *[inputs[6].at[0, 0, chunk] for chunk in chunks]),
        (*buffers, scalars, *[tensors.at[0, 0, chunk] for chunk in chunks]),
        sem,
    )
    send_index, counts, species, vectors, reverse = buffers
    channels, edges = scalars.shape[2:]
    comps, m = tensors.shape[2:4]
    block = send_index.shape[-1]
    features = channels + comps * m
    odd = lax.rem(lax.axis_index("gx"), 2) == 1
    lane = lax.broadcasted_iota(jnp.int32, (1, block), 1)
    for copy in copies[:5]:
        copy.wait()

    def live(p):
        return jnp.where(lane < counts[0, 0, p], send_index[0, 0, p : p + 1, :], -1)

    index = jnp.concatenate(
        [
            live(p) if p == q else jnp.where(odd, live(q), live(p))
            for p, q in zip(*plan.orders)
        ],
        axis=1,
    )
    slots = index.shape[1]
    low = lax.broadcasted_iota(jnp.int32, (256, slots), 0).astype(F32).astype(BF16)
    for at in range(0, edges, 256):
        inside = jnp.logical_and(index >= at, index < at + 256)
        key = jnp.where(inside, index - at, -1).astype(F32).astype(BF16)
        onehot[at : at + 256, :] = jnp.where(low == key, BF16(1), BF16(0))
    near = jnp.minimum(reverse[0], edges - 1) * 8
    rows[...] = jnp.concatenate(
        [near[:, j * 128 : (j + 1) * 128] for j in range(edges // 128)], axis=0
    )
    vec = jnp.concatenate([vectors[0, j] for j in range(3)], axis=0)
    high = vec.astype(BF16)
    left = vec - high.astype(F32)
    mid = left.astype(BF16)
    low = (left - mid.astype(F32)).astype(BF16)
    extra = jnp.concatenate(
        [
            jnp.broadcast_to(species[0].astype(F32), (7, edges)),
            high.astype(F32),
            mid.astype(F32),
            low.astype(F32),
        ],
        axis=0,
    ).astype(BF16)
    extra = mm(extra, onehot[...])
    where[0:3, :] = extra[7:10] + extra[10:13] + extra[13:16]
    where[3:8, :] = jnp.zeros((5, slots), F32)
    own[features:, :] = jnp.broadcast_to(extra[0:1], (EXTRA, slots)).astype(BF16)
    copies[5].wait()
    own[:channels, :] = mm(scalars[0, 0], onehot[...]).astype(BF16)
    for copy, chunk in zip(copies[6:], chunks):
        copy.wait()
        piece = tensors[0, 0, chunk].reshape(chunk.size * m, edges)
        own[pl.ds(channels + chunk.start * m, chunk.size * m), :] = mm(
            piece, onehot[...]
        ).astype(BF16)
    half = features // 2
    for send, parts in zip(sends, plan.arrays):
        at = 0
        for kind, j in parts:
            if kind == "wide":
                send[at : at + features + EXTRA, :] = own[:, j * block : (j + 2) * block]
            else:
                piece = own[:, j * block : (j + 1) * block]
                send[at : at + half, :] = jnp.concatenate(
                    [piece[:half], piece[half:features]], axis=1
                )
                send[at + half : at + half + EXTRA, :] = jnp.concatenate(
                    [piece[features:], piece[features:]], axis=1
                )
            at += plan.part_rows(kind, features)


def copy_rows(step, table, rows, gathered):
    per = rows.shape[1]
    width = gathered.shape[0] // 8
    for t in range(rows.shape[0] * per // width):

        @pl.when(step == t)
        def _(first=t * width):
            for e in range(width):
                n = first + e
                source = pl.ds(pl.multiple_of(rows[n // per, n % per], 8), 8)
                gathered[e * 8 : e * 8 + 8, :] = table[source, :]


def interior_kernel(rows, scalars, tensors, *refs):
    inputs, refs = refs[:12], refs[12:]
    middle_out, message_out, tensors_out, edge_rows, gathered, pair_mix, w_shared, *refs = refs
    buffers, sem = refs[:-1], refs[-1]
    (
        w_mixing,
        w_invariant,
        vectors,
        species,
        table,
        w_query,
        w_output,
        w_rev,
        w_mid,
    ) = buffers
    edges = scalars.shape[-1]
    width = gathered.shape[0] // 8
    channels = scalars.shape[2]
    comps, m = tensors.shape[2:4]
    step = pl.program_id(0)
    here = pl.ds(pl.multiple_of(step * width, 128), width)
    pairs = [(k, k + 1) for k in range(0, comps - 1, 2)] + [(comps - 2, comps - 1)]

    @pl.when(step == 0)
    def _():
        copies = fetch(inputs, buffers, sem)
        unit = eye(256)
        half = eye(128)

        def turn(at, j, piece):
            turned = nt(unit, piece)
            for c in range(0, piece.shape[0], 128):
                edge_rows[pl.ds(at * 8 + j + c // 128, 256, stride=8), :] = turned[:, c : c + 128]

        for at in range(0, edges, 256):
            for c in range(0, channels, 256):
                turn(at, c // 128, scalars[0, 0, c : c + 256, at : at + 256])
        for at in range(0, edges, 256):
            n = 0
            while n < len(pairs):
                taken = 2 if n + 2 < len(pairs) else 1
                k = pairs[n][0]
                piece = tensors[0, 0, k : k + 2 * taken, :, at : at + 256].reshape(-1, 256)
                turn(at, channels // 128 + n, piece)
                n += taken
        for copy in copies:
            copy.wait()
        mixing = w_mixing[...].astype(F32)
        zero = jnp.zeros((m, m), F32)
        pair_mix[...] = jnp.concatenate(
            [
                half.astype(F32),
                jnp.concatenate([mixing, zero], axis=1),
                jnp.concatenate([zero, mixing], axis=1),
            ],
            axis=0,
        ).astype(BF16)
        w_shared[...] = nt(unit, w_invariant[...]).astype(BF16)

    copy_rows(step, edge_rows, rows, gathered)

    def feature(j):
        return gathered[pl.ds(j, width, stride=8), :].astype(BF16)

    lead = channels // 128
    s_rev = jnp.concatenate([feature(j) for j in range(lead)], axis=1)
    t_rev, mixed = {}, {}
    for j, (first, second) in enumerate(pairs):
        both = nt(pair_mix[...], feature(lead + j))
        t_rev[first], t_rev[second] = both[:m], both[m : 2 * m]
        mixed[first], mixed[second] = both[2 * m : 3 * m], both[3 * m :]
    embedded = embed(scalars[0, 0, :, here], jnp.transpose(table[...]), species[0, :, here])
    both = nt(w_rev[...], s_rev)
    attended = attend(mm(w_query[...], embedded), both[:channels], both[channels:])
    own_t = [tensors[0, 0, k, :, here] for k in range(comps)]
    middle = (
        embedded.astype(F32)
        + mm(w_output[...], attended)
        + mm(w_shared[...], invariants(own_t, t_rev))
    ).astype(BF16)
    middle_out[:, here] = middle
    spread = mm(w_mid[...], middle)
    message_out[:, here] = spread[:channels].astype(BF16)
    gate = jax.nn.sigmoid(spread[channels : channels + 3 * m])
    radial = spread[channels + 3 * m :]
    vec = jnp.concatenate([vectors[0, j, :, here] for j in range(3)], axis=0)
    for k, new in update_tensors(own_t, mixed, gate, radial, vec):
        tensors_out[k, :, here] = new


def incoming_kernel(plan, block, message, middle, rows, *refs):
    inputs, (scalars_out, merge, edge_rows, gathered, *buffers, sem) = refs[:4], refs[4:]
    reverse, w_expand, w_reverse, w_contract = buffers
    channels, edges = message.shape
    width = gathered.shape[0] // 8
    step = pl.program_id(0)
    here = pl.ds(pl.multiple_of(step * width, 128), width)

    @pl.when(step == 0)
    def _():
        copies = fetch(inputs, buffers, sem)
        unit = eye(256)
        for at in range(0, edges, 256):
            for first in range(0, channels, 256):
                turned = nt(unit, message[first : first + 256, at : at + 256])
                for c in range(0, 256, 128):
                    row = at * 8 + (first + c) // 128
                    edge_rows[pl.ds(row, 256, stride=8), :] = turned[:, c : c + 128]
        for copy in copies:
            copy.wait()

    copy_rows(step, edge_rows, rows, gathered)
    incoming = jnp.concatenate(
        [
            gathered[pl.ds(j, width, stride=8), :].astype(BF16)
            for j in range(channels // 128)
        ],
        axis=1,
    )
    v = mm(w_expand[...], middle[:, here]) + nt(w_reverse[...], incoming)
    scalars_out[:, here] = contract(middle[:, here], v, w_contract[...])
    target = reverse[0, :, here] - edges
    odd = lax.rem(lax.axis_index("gx"), 2) == 1
    low = lax.broadcasted_iota(jnp.int32, (block, width), 0).astype(F32).astype(BF16)
    for j, (p, q) in enumerate(zip(*plan.orders)):
        at = pick(odd, (OPPOSITE[p], OPPOSITE[q])) * block
        inside = jnp.logical_and(target >= at, target < at + block)
        key = jnp.where(inside, target - at, -1).astype(F32).astype(BF16)
        merge[j * block : (j + 1) * block, here] = jnp.where(low == key, BF16(1), BF16(0))


def settle(plan, block, positions, base, received, own, where, table, weights, far, s_new, t_new):
    (
        w_query,
        w_key,
        w_value,
        w_output,
        w_invariant,
        w_message,
        w_gate,
        w_radial,
        w_mixing,
        w_expand,
        w_reverse,
        w_contract,
    ) = weights
    m = w_mixing.shape[0]
    channels = w_query.shape[0]
    comps = t_new.shape[0] // m
    features = channels + comps * m
    columns = slice(positions[0] * block, (positions[-1] + 1) * block)
    slots = len(positions) * block

    def block_of(g, part, n):
        kind, _ = plan.parts[g][part]
        at = plan.offset(plan.parts[g], part, features)
        if kind == "wide":
            return received[g - base][at : at + features + EXTRA, n * block : (n + 1) * block]
        half = features // 2
        upper = received[g - base][at : at + half, :]
        extra = received[g - base][at + half : at + half + EXTRA, :block]
        return jnp.concatenate([upper[:, :block], upper[:, block:], extra], axis=0)

    for j in range(0, len(positions), 2):
        to = slice(j * block, (j + 2) * block)
        (g, part, n), second = (plan.facing[p] for p in positions[j : j + 2])
        if n == 0 and second == (g, part, 1):
            at = plan.offset(plan.parts[g], part, features)
            far[:, to] = received[g - base][at : at + features + EXTRA, :]
        else:
            far[:, to] = jnp.concatenate([block_of(g, part, n), block_of(*second)], axis=1)
    s_own, s_far = own[:channels, columns], far[:channels, :]
    t_own = [own[channels + k * m : channels + (k + 1) * m, columns] for k in range(comps)]
    t_far = [far[channels + k * m : channels + (k + 1) * m, :] for k in range(comps)]
    picks = jnp.transpose(table[...])
    e_own = embed(s_own, picks, own[features : features + 1, columns].astype(F32))
    e_far = embed(s_far, picks, far[features : features + 1, :].astype(F32))
    w_shared = nt(eye(channels), w_invariant[...]).astype(BF16)
    shared = mm(w_shared, invariants(t_own, t_far))
    embedded = jnp.concatenate([e_own, e_far], axis=1)
    w_rev = jnp.concatenate([w_key[...], w_value[...]], axis=0)
    both = mm(w_rev, jnp.concatenate([s_far, s_own], axis=1))
    attended = attend(mm(w_query[...], embedded), both[:channels], both[channels:])
    middles = (
        embedded.astype(F32)
        + mm(w_output[...], attended)
        + jnp.concatenate([shared, shared], axis=1)
    ).astype(BF16)
    middle = middles[:, :slots]
    incoming = mm(w_message[...], middles[:, slots:]).astype(BF16)
    w_mid = jnp.concatenate([w_expand[...], w_gate[...], w_radial[...]], axis=0)
    spread = mm(w_mid, middle)
    hidden = w_expand.shape[0]
    v = spread[:hidden] + mm(w_reverse[...], incoming)
    s_new[...] = contract(middle, v, w_contract[...])
    gate = jax.nn.sigmoid(spread[hidden : hidden + 3 * m])
    radial = spread[hidden + 3 * m :]
    mixed = [mm(w_mixing[...], t_far[k]) for k in range(comps)]
    for k, new in update_tensors(t_own, mixed, gate, radial, where[:, columns]):
        t_new[k * m : (k + 1) * m, :] = new


def near_kernel(plan, block, positions, *refs):
    received, (own, where, table, *refs) = refs[:3], refs[3:]
    weights, (s_new, t_new, far) = refs[:12], refs[12:]
    settle(plan, block, positions, 0, received, own, where, table, weights, far, s_new, t_new)


def boundary_kernel(plan, block, positions, base, count, done, edges, *refs):
    received, refs = refs[:count], refs[count:]
    settled, (own, where, merge, reverse, scalars_in, tensors_in, table, *refs) = (
        refs[:done],
        refs[done:],
    )
    weights, (scalars_out, tensors_out, s_new, t_new, far) = refs[:12], refs[12:]
    comps, m = tensors_in.shape[:2]
    channels = scalars_in.shape[0]

    @pl.when(pl.program_id(0) == 0)
    def _():
        settle(
            plan, block, positions, base, received, own, where, table, weights, far, s_new, t_new
        )

    width = scalars_out.shape[-1]
    here = pl.ds(pl.multiple_of(pl.program_id(0) * width, 128), width)
    first = len(positions) * block
    crosses = jnp.broadcast_to((reverse[0, :, here] >= edges).astype(F32), (m, width))
    crosses = crosses.astype(BF16) > 0

    def spread(new, n):
        total = mm(new[...], merge[:first, here])
        if done:
            total = total + mm(settled[n][...], merge[first:, here])
        return total

    def merged(new, old):
        return jnp.where(crosses, new.astype(BF16), old)

    s_all = spread(s_new, 0)
    for c in range(0, channels, m):
        scalars_out[0, 0, c : c + m] = merged(s_all[c : c + m], scalars_in[c : c + m, here])
    t_all = spread(t_new, 1)
    for k in range(comps):
        tensors_out[0, 0, k] = merged(t_all[k * m : (k + 1) * m], tensors_in[k, :, here])


def resident(*arrays):
    return [pltpu.with_memory_space_constraint(x, pltpu.HBM) for x in arrays]


def whole(*shape):
    return pl.BlockSpec(shape, lambda *_: (0,) * len(shape))


def per_device(gx, gy, *args):
    (
        scalars,
        tensors,
        vectors,
        species,
        table,
        reverse,
        send_index,
        counts,
        w_query,
        w_key,
        w_value,
        w_output,
        w_invariant,
        w_message,
        w_gate,
        w_radial,
        w_mixing,
        w_expand,
        w_reverse,
        w_contract,
    ) = args
    plan = Plan(gx, gy)
    vectors = jnp.transpose(vectors, (0, 2, 1, 3))
    table = jnp.transpose(table)
    w_invariant = jnp.transpose(w_invariant)
    _, _, channels, edges = scalars.shape
    comps, m = tensors.shape[2:4]
    features = channels + comps * m
    block = send_index.shape[-1]
    slots = len(DIRECTIONS) * block
    vmem = pl.BlockSpec(memory_space=pltpu.VMEM)

    def limit(mebibytes):
        return pltpu.CompilerParams(vmem_limit_bytes=mebibytes * 2**20)


    hbm = pl.BlockSpec(memory_space=pltpu.HBM)

    def buffers(*arrays):
        return [pltpu.VMEM(x.shape, x.dtype) for x in arrays] + [
            pltpu.SemaphoreType.DMA((len(arrays),))
        ]

    prepared = (send_index, counts, species, vectors, reverse, scalars, tensors)
    prepared_buffers = buffers(*prepared)
    prepared_buffers[5:] = [pltpu.SemaphoreType.DMA((6 + pl.cdiv(comps, 4),))]
    prepared_buffers[1] = pltpu.SMEM(counts.shape, counts.dtype)
    prepared_buffers.insert(0, pltpu.VMEM((edges, slots), BF16))
    own, where, rows, scalars, tensors, *sends = pl.pallas_call(
        functools.partial(prepare_kernel, plan),
        in_specs=[hbm] * len(prepared),
        out_specs=[vmem] * (5 + len(plan.arrays)),
        out_shape=[
            jax.ShapeDtypeStruct((features + EXTRA, slots), BF16),
            jax.ShapeDtypeStruct((8, slots), F32),
            jax.ShapeDtypeStruct((edges // 128, 128), jnp.int32),
            jax.ShapeDtypeStruct(scalars.shape, BF16),
            jax.ShapeDtypeStruct(tensors.shape, BF16),
        ]
        + [
            jax.ShapeDtypeStruct((plan.rows(parts, features), 2 * block), BF16)
            for parts in plan.arrays
        ],
        scratch_shapes=prepared_buffers,
        compiler_params=limit(24),
        name="prepare",
    )(*resident(*prepared))

    def exchange(x, pairs):
        return lax.ppermute(x, ("gx", "gy"), pairs)

    if plan.paired:
        received = [
            exchange(sends[0], plan.swaps[0]),
            exchange(sends[1], plan.swaps[1]),
            exchange(sends[2], plan.across),
        ]
    else:
        received = [exchange(x, pairs) for x, pairs in zip(sends, plan.pairs)]

    width = 1024 if edges % 1024 == 0 else edges
    steps = edges // width
    flat = whole(channels, edges)
    first_weights = (w_query, w_key, w_value, w_output, w_invariant, w_message, w_gate, w_radial, w_mixing)
    last_weights = (w_expand, w_reverse, w_contract)
    inside = (
        w_mixing, w_invariant, vectors, species, table,
        w_query, w_output, w_key, w_value, w_message, w_gate, w_radial,
    )
    stacked = [pltpu.VMEM((2 * channels, channels), BF16), pltpu.VMEM((channels + 6 * m, channels), BF16)]
    middle, message, t_inside = pl.pallas_call(
        interior_kernel,
        grid=(steps,),
        in_specs=[pl.BlockSpec(memory_space=pltpu.SMEM)]
        + [whole(*scalars.shape), whole(*tensors.shape)]
        + [hbm] * len(inside),
        out_specs=[flat, flat, whole(comps, m, edges)],
        out_shape=[
            jax.ShapeDtypeStruct((channels, edges), BF16),
            jax.ShapeDtypeStruct((channels, edges), BF16),
            jax.ShapeDtypeStruct((comps, m, edges), BF16),
        ],
        scratch_shapes=[
            pltpu.VMEM((edges * 8, 128), F32),
            pltpu.VMEM((width * 8, 128), F32),
            pltpu.VMEM((256, 128), BF16),
            pltpu.VMEM((channels, w_invariant.shape[0]), BF16),
        ]
        + buffers(*inside)[:7]
        + stacked
        + [pltpu.SemaphoreType.DMA((len(inside),))],
        compiler_params=limit(36),
        cost_estimate=pl.CostEstimate(
            flops=2 * edges * edges * features, bytes_accessed=4 * edges * features, transcendentals=0
        ),
        name="interior",
    )(rows, scalars, tensors, *resident(*inside))
    last_weights = (w_expand, w_reverse, w_contract)
    brought = (reverse, *last_weights)
    s_inside, merge = pl.pallas_call(
        functools.partial(incoming_kernel, plan, block),
        grid=(steps,),
        in_specs=[whole(channels, edges), flat, pl.BlockSpec(memory_space=pltpu.SMEM)]
        + [hbm] * len(brought),
        out_specs=[flat, whole(slots, edges)],
        out_shape=[
            jax.ShapeDtypeStruct((channels, edges), BF16),
            jax.ShapeDtypeStruct((slots, edges), BF16),
        ],
        scratch_shapes=[
            pltpu.VMEM((edges * 8, 128), F32),
            pltpu.VMEM((width * 8, 128), F32),
        ]
        + buffers(*brought),
        compiler_params=limit(24),
        cost_estimate=pl.CostEstimate(
            flops=4 * edges * edges * channels, bytes_accessed=8 * edges * channels, transcendentals=0
        ),
        name="incoming",
    )(message, middle, rows, *resident(*brought))
    if plan.paired:
        held = lax.optimization_barrier((received[0], received[1], s_inside))
        received[0], received[1], s_inside = held
        relayed = [exchange(received[0], plan.across), exchange(received[1], plan.across)]
        positions, near = tuple(range(4)), tuple(range(4, 8))
        columns = len(near) * block
        settled = pl.pallas_call(
            functools.partial(near_kernel, plan, block, near),
            in_specs=[vmem] * (6 + len(first_weights + last_weights)),
            out_specs=[vmem, vmem],
            out_shape=[
                jax.ShapeDtypeStruct((channels, columns), BF16),
                jax.ShapeDtypeStruct((comps * m, columns), BF16),
            ],
            scratch_shapes=[pltpu.VMEM((features + EXTRA, columns), BF16)],
            compiler_params=limit(16),
            cost_estimate=pl.CostEstimate(
                flops=4 * columns * channels * features, bytes_accessed=4 * columns * features, transcendentals=0
            ),
            name="near",
        )(*received, own, where, table, *first_weights, *last_weights)
        base, received = 3, relayed
    else:
        positions, base, settled = tuple(range(len(DIRECTIONS))), 0, []

    columns = len(positions) * block
    return pl.pallas_call(
        functools.partial(
            boundary_kernel, plan, block, positions, base, len(received), len(settled), edges
        ),
        grid=(steps,),
        in_specs=[whole(*r.shape) for r in (*received, *settled)]
        + [whole(*own.shape), whole(*where.shape), whole(slots, edges)]
        + [whole(*reverse.shape), flat, whole(comps, m, edges), whole(*table.shape)]
        + [whole(*w.shape) for w in first_weights + last_weights],
        out_specs=[
            pl.BlockSpec((1, 1, channels, width), lambda i: (0, 0, 0, i)),
            pl.BlockSpec((1, 1, comps, m, width), lambda i: (0, 0, 0, 0, i)),
        ],
        out_shape=[
            jax.ShapeDtypeStruct((1, 1, channels, edges), BF16),
            jax.ShapeDtypeStruct((1, 1, comps, m, edges), BF16),
        ],
        scratch_shapes=[
            pltpu.VMEM((channels, columns), BF16),
            pltpu.VMEM((comps * m, columns), BF16),
            pltpu.VMEM((features + EXTRA, columns), BF16),
        ],
        compiler_params=limit(26),
        cost_estimate=pl.CostEstimate(
            flops=2 * edges * slots * features, bytes_accessed=8 * edges * features, transcendentals=0
        ),
        name="boundary",
    )(
        *received, *settled, own, where, merge, reverse, s_inside, t_inside, table,
        *first_weights, *last_weights,
    )


def solution(mesh):
    gx, gy = mesh.shape["gx"], mesh.shape["gy"]

    def body(*args):
        return per_device(gx, gy, *args)

    step = jax.shard_map(
        body,
        mesh=mesh,
        in_specs=(
            P("gx", "gy", None, None),
            P("gx", "gy", None, None, None),
            P("gx", "gy", None, None),
            P("gx", "gy", None),
            P(),
            P("gx", "gy", None),
            P("gx", "gy", None, None),
            P("gx", "gy", None),
        )
        + (P(),) * 12,
        out_specs=(P("gx", "gy", None, None), P("gx", "gy", None, None, None)),
        check_vma=False,
    )
    if not Plan(gx, gy).paired:
        return step
    return step
```

```python
import functools
import math

import jax
import jax.numpy as jnp
from jax import lax
from jax.experimental import pallas as pl
from jax.experimental.pallas import tpu as pltpu
from jax.sharding import PartitionSpec as P


HEADS = 8
DIRECTIONS = ((1, 0), (-1, 0), (0, 1), (0, -1), (1, 1), (1, -1), (-1, 1), (-1, -1))
OPPOSITE = tuple(DIRECTIONS.index((-dx, -dy)) for dx, dy in DIRECTIONS)
EXTRA = 16
BF16 = jnp.bfloat16
F32 = jnp.float32


def ring(gx, gy, dx, dy):
    return tuple(
        (a * gy + b, ((a + dx) % gx) * gy + (b + dy) % gy) for a in range(gx) for b in range(gy)
    )


class Plan:
    def __init__(self, gx, gy):
        self.paired = gx % 2 == 0 and gy == 2
        if self.paired:
            self.orders = ((4, 5, 7, 6, 0, 1, 2, 3), (7, 6, 4, 5, 1, 0, 2, 3))
            self.arrays = ((("wide", 0), ("fold", 4)), (("wide", 2), ("fold", 5)), (("wide", 6),))
            self.facing = (
                (3, 0, 0), (3, 0, 1), (4, 0, 0), (4, 0, 1), (0, 1, 0), (1, 1, 0), (2, 0, 1), (2, 0, 0),
            )
            self.parts = self.arrays + self.arrays[:2]
            even = [(a, a + 1 - 2 * (a % 2)) for a in range(gx)]
            odd = [(a, (a - 1 + 2 * (a % 2)) % gx) for a in range(gx)]
            self.swaps = [
                tuple((a * gy + b, c * gy + b) for a, c in pairs for b in range(gy))
                for pairs in (even, odd)
            ]
            self.across = ring(gx, gy, 0, 1)
        else:
            groups = {}
            for p in (4, 5, 7, 6, 0, 1, 2, 3):
                groups.setdefault(ring(gx, gy, *DIRECTIONS[p]), []).append(p)
            order, self.arrays, place = [], (), {}
            for g, members in enumerate(groups.values()):
                parts = ()
                rest = members
                while rest:
                    taken = 2 if len(rest) > 1 else 1
                    for n, p in enumerate(rest[:taken]):
                        place[p] = (g, len(parts), n)
                    parts += (("wide" if taken == 2 else "fold", len(order)),)
                    order += rest[:taken]
                    rest = rest[taken:]
                self.arrays += (parts,)
            self.orders = (tuple(order),) * 2
            self.parts = self.arrays
            self.facing = tuple(place[OPPOSITE[p]] for p in order)
            self.pairs = list(groups)

    def part_rows(self, kind, features):
        return features + EXTRA if kind == "wide" else features // 2 + EXTRA

    def offset(self, parts, number, features):
        return sum(self.part_rows(kind, features) for kind, _ in parts[:number])

    def rows(self, parts, features):
        return self.offset(parts, len(parts), features)


def pick(odd, pair):
    return pair[0] if pair[0] == pair[1] else jnp.where(odd, pair[1], pair[0])


def mm(a, b):
    return jnp.dot(a, b, preferred_element_type=F32)


def nt(a, b):
    return lax.dot_general(a, b, (((1,), (1,)), ((), ())), preferred_element_type=F32)


def eye(n):
    rows = lax.broadcasted_iota(jnp.int32, (n, n), 0)
    return (rows == lax.broadcasted_iota(jnp.int32, (n, n), 1)).astype(BF16)


def embed(own, table, species):
    picked = table[:, 3:4]
    for j in (2, 1, 0):
        picked = jnp.where(species == j, table[:, j : j + 1], picked)
    return (own.astype(F32) + picked).astype(BF16)


def attend(queries, keys, values):
    channels, _ = queries.shape
    size = channels // HEADS
    product = queries * keys
    parts = []
    for h in range(HEADS):
        rows = slice(h * size, (h + 1) * size)
        score = jnp.sum(product[rows], axis=0, keepdims=True) * (1.0 / math.sqrt(size))
        parts.append(jax.nn.sigmoid(score) * values[rows])
    return jnp.concatenate(parts, axis=0).astype(BF16)


def invariants(own, rev):
    product = [own[k].astype(F32) * rev[k].astype(F32) for k in range(9)]
    return jnp.concatenate(
        [
            product[0],
            product[1] + product[2] + product[3],
            product[4] + product[5] + product[6] + product[7] + product[8],
        ],
        axis=0,
    ).astype(BF16)


def harmonics(vectors):
    x, y, z = vectors[0:1], vectors[1:2], vectors[2:3]
    r2 = x * x + y * y + z * z
    root = math.sqrt(3.0)
    return (
        None,
        x,
        y,
        z,
        root * x * y,
        root * y * z,
        0.5 * (3.0 * z * z - r2),
        root * x * z,
        0.5 * root * (x * x - y * y),
    )


def update_tensors(own, mixed, gate, radial, vectors):
    m = own[0].shape[0]
    harmonic = harmonics(vectors)
    for k in range(9):
        degree = 0 if k == 0 else (1 if k < 4 else 2)
        rows = slice(degree * m, (degree + 1) * m)
        tail = radial[rows] if harmonic[k] is None else radial[rows] * harmonic[k]
        yield k, (own[k].astype(F32) + gate[rows] * mixed[k] + tail).astype(BF16)


def contract(middle, v, w_contract):
    hidden = (v * jax.nn.sigmoid(v)).astype(BF16)
    return (middle.astype(F32) + mm(w_contract, hidden)).astype(BF16)


def fetch(sources, buffers, sem):
    pieces = []
    waiting = list(sources)
    for buffer in buffers:
        at = 0
        while at < buffer.shape[0]:
            source = waiting.pop(0)
            part = buffer if source.shape == buffer.shape else buffer.at[pl.ds(at, source.shape[0])]
            pieces.append((source, part))
            at += source.shape[0]
    copies = [pltpu.make_async_copy(*piece, sem.at[n]) for n, piece in enumerate(pieces)]
    for copy in copies:
        copy.start()
    return copies


def prepare_kernel(plan, *refs):
    inputs, (own, where, rows, scalars, tensors), refs = refs[:7], refs[7:12], refs[12:]
    sends, (onehot, *buffers, sem) = refs[: len(plan.arrays)], refs[len(plan.arrays) :]
    copies = fetch(inputs, (*buffers, scalars, tensors), sem)
    send_index, counts, species, vectors, reverse = buffers
    channels, edges = scalars.shape[2:]
    comps, m = tensors.shape[2:4]
    block = send_index.shape[-1]
    features = channels + comps * m
    odd = lax.rem(lax.axis_index("gx"), 2) == 1
    lane = lax.broadcasted_iota(jnp.int32, (1, block), 1)
    for copy in copies[:5]:
        copy.wait()

    def live(p):
        return jnp.where(lane < counts[0, 0, p], send_index[0, 0, p : p + 1, :], -1)

    index = jnp.concatenate(
        [
            live(p) if p == q else jnp.where(odd, live(q), live(p))
            for p, q in zip(*plan.orders)
        ],
        axis=1,
    )
    slots = index.shape[1]
    low = lax.broadcasted_iota(jnp.int32, (256, slots), 0).astype(F32).astype(BF16)
    for at in range(0, edges, 256):
        inside = jnp.logical_and(index >= at, index < at + 256)
        key = jnp.where(inside, index - at, -1).astype(F32).astype(BF16)
        onehot[at : at + 256, :] = jnp.where(low == key, BF16(1), BF16(0))
    near = jnp.minimum(reverse[0], edges - 1) * 8
    rows[...] = jnp.concatenate(
        [near[:, j * 128 : (j + 1) * 128] for j in range(edges // 128)], axis=0
    )
    vec = jnp.concatenate([vectors[0, j] for j in range(3)], axis=0)
    high = vec.astype(BF16)
    left = vec - high.astype(F32)
    mid = left.astype(BF16)
    low = (left - mid.astype(F32)).astype(BF16)
    extra = jnp.concatenate(
        [
            jnp.broadcast_to(species[0].astype(F32), (7, edges)),
            high.astype(F32),
            mid.astype(F32),
            low.astype(F32),
        ],
        axis=0,
    ).astype(BF16)
    extra = mm(extra, onehot[...])
    where[0:3, :] = extra[7:10] + extra[10:13] + extra[13:16]
    where[3:8, :] = jnp.zeros((5, slots), F32)
    own[features:, :] = jnp.broadcast_to(extra[0:1], (EXTRA, slots)).astype(BF16)
    copies[5].wait()
    own[:channels, :] = mm(scalars[0, 0], onehot[...]).astype(BF16)
    copies[6].wait()
    own[channels:features, :] = mm(
        tensors[0, 0].reshape(comps * m, edges), onehot[...]
    ).astype(BF16)
    half = features // 2
    for send, parts in zip(sends, plan.arrays):
        at = 0
        for kind, j in parts:
            if kind == "wide":
                send[at : at + features + EXTRA, :] = own[:, j * block : (j + 2) * block]
            else:
                piece = own[:, j * block : (j + 1) * block]
                send[at : at + half, :] = jnp.concatenate(
                    [piece[:half], piece[half:features]], axis=1
                )
                send[at + half : at + half + EXTRA, :] = jnp.concatenate(
                    [piece[features:], piece[features:]], axis=1
                )
            at += plan.part_rows(kind, features)


def copy_rows(step, table, rows, gathered):
    per = rows.shape[1]
    width = gathered.shape[0] // 8
    for t in range(rows.shape[0] * per // width):

        @pl.when(step == t)
        def _(first=t * width):
            for e in range(width):
                n = first + e
                source = pl.ds(pl.multiple_of(rows[n // per, n % per], 8), 8)
                gathered[e * 8 : e * 8 + 8, :] = table[source, :]


def interior_kernel(rows, scalars, tensors, *refs):
    inputs, refs = refs[:12], refs[12:]
    middle_out, message_out, tensors_out, edge_rows, gathered, pair_mix, w_shared, *refs = refs
    buffers, sem = refs[:-1], refs[-1]
    (
        w_mixing,
        w_invariant,
        vectors,
        species,
        table,
        w_query,
        w_output,
        w_rev,
        w_mid,
    ) = buffers
    edges = scalars.shape[-1]
    width = gathered.shape[0] // 8
    channels = scalars.shape[2]
    comps, m = tensors.shape[2:4]
    step = pl.program_id(0)
    here = pl.ds(pl.multiple_of(step * width, 128), width)
    pairs = [(k, k + 1) for k in range(0, comps - 1, 2)] + [(comps - 2, comps - 1)]

    @pl.when(step == 0)
    def _():
        copies = fetch(inputs, buffers, sem)
        unit = eye(256)
        half = eye(128)

        def turn(at, j, piece):
            turned = nt(unit, piece)
            for c in range(0, piece.shape[0], 128):
                edge_rows[pl.ds(at * 8 + j + c // 128, 256, stride=8), :] = turned[:, c : c + 128]

        for at in range(0, edges, 256):
            for c in range(0, channels, 256):
                turn(at, c // 128, scalars[0, 0, c : c + 256, at : at + 256])
        for at in range(0, edges, 256):
            n = 0
            while n < len(pairs):
                taken = 2 if n + 2 < len(pairs) else 1
                k = pairs[n][0]
                piece = tensors[0, 0, k : k + 2 * taken, :, at : at + 256].reshape(-1, 256)
                turn(at, channels // 128 + n, piece)
                n += taken
        for copy in copies:
            copy.wait()
        mixing = w_mixing[...].astype(F32)
        zero = jnp.zeros((m, m), F32)
        pair_mix[...] = jnp.concatenate(
            [
                half.astype(F32),
                jnp.concatenate([mixing, zero], axis=1),
                jnp.concatenate([zero, mixing], axis=1),
            ],
            axis=0,
        ).astype(BF16)
        w_shared[...] = nt(unit, w_invariant[...]).astype(BF16)

    copy_rows(step, edge_rows, rows, gathered)

    def feature(j):
        return gathered[pl.ds(j, width, stride=8), :].astype(BF16)

    lead = channels // 128
    s_rev = jnp.concatenate([feature(j) for j in range(lead)], axis=1)
    t_rev, mixed = {}, {}
    for j, (first, second) in enumerate(pairs):
        both = nt(pair_mix[...], feature(lead + j))
        t_rev[first], t_rev[second] = both[:m], both[m : 2 * m]
        mixed[first], mixed[second] = both[2 * m : 3 * m], both[3 * m :]
    embedded = embed(scalars[0, 0, :, here], jnp.transpose(table[...]), species[0, :, here])
    both = nt(w_rev[...], s_rev)
    attended = attend(mm(w_query[...], embedded), both[:channels], both[channels:])
    own_t = [tensors[0, 0, k, :, here] for k in range(comps)]
    middle = (
        embedded.astype(F32)
        + mm(w_output[...], attended)
        + mm(w_shared[...], invariants(own_t, t_rev))
    ).astype(BF16)
    middle_out[:, here] = middle
    spread = mm(w_mid[...], middle)
    message_out[:, here] = spread[:channels].astype(BF16)
    gate = jax.nn.sigmoid(spread[channels : channels + 3 * m])
    radial = spread[channels + 3 * m :]
    vec = jnp.concatenate([vectors[0, j, :, here] for j in range(3)], axis=0)
    for k, new in update_tensors(own_t, mixed, gate, radial, vec):
        tensors_out[k, :, here] = new


def incoming_kernel(plan, block, message, middle, rows, *refs):
    inputs, (scalars_out, merge, edge_rows, gathered, *buffers, sem) = refs[:4], refs[4:]
    reverse, w_expand, w_reverse, w_contract = buffers
    channels, edges = message.shape
    width = gathered.shape[0] // 8
    step = pl.program_id(0)
    here = pl.ds(pl.multiple_of(step * width, 128), width)

    @pl.when(step == 0)
    def _():
        copies = fetch(inputs, buffers, sem)
        unit = eye(256)
        for at in range(0, edges, 256):
            for first in range(0, channels, 256):
                turned = nt(unit, message[first : first + 256, at : at + 256])
                for c in range(0, 256, 128):
                    row = at * 8 + (first + c) // 128
                    edge_rows[pl.ds(row, 256, stride=8), :] = turned[:, c : c + 128]
        for copy in copies:
            copy.wait()

    copy_rows(step, edge_rows, rows, gathered)
    incoming = jnp.concatenate(
        [
            gathered[pl.ds(j, width, stride=8), :].astype(BF16)
            for j in range(channels // 128)
        ],
        axis=1,
    )
    v = mm(w_expand[...], middle[:, here]) + nt(w_reverse[...], incoming)
    scalars_out[:, here] = contract(middle[:, here], v, w_contract[...])
    target = reverse[0, :, here] - edges
    odd = lax.rem(lax.axis_index("gx"), 2) == 1
    low = lax.broadcasted_iota(jnp.int32, (block, width), 0).astype(F32).astype(BF16)
    for j, (p, q) in enumerate(zip(*plan.orders)):
        at = pick(odd, (OPPOSITE[p], OPPOSITE[q])) * block
        inside = jnp.logical_and(target >= at, target < at + block)
        key = jnp.where(inside, target - at, -1).astype(F32).astype(BF16)
        merge[j * block : (j + 1) * block, here] = jnp.where(low == key, BF16(1), BF16(0))


def settle(plan, block, positions, base, received, own, where, table, weights, far, s_new, t_new):
    (
        w_query,
        w_key,
        w_value,
        w_output,
        w_invariant,
        w_message,
        w_gate,
        w_radial,
        w_mixing,
        w_expand,
        w_reverse,
        w_contract,
    ) = weights
    m = w_mixing.shape[0]
    channels = w_query.shape[0]
    comps = t_new.shape[0] // m
    features = channels + comps * m
    columns = slice(positions[0] * block, (positions[-1] + 1) * block)
    slots = len(positions) * block

    def block_of(g, part, n):
        kind, _ = plan.parts[g][part]
        at = plan.offset(plan.parts[g], part, features)
        if kind == "wide":
            return received[g - base][at : at + features + EXTRA, n * block : (n + 1) * block]
        half = features // 2
        upper = received[g - base][at : at + half, :]
        extra = received[g - base][at + half : at + half + EXTRA, :block]
        return jnp.concatenate([upper[:, :block], upper[:, block:], extra], axis=0)

    for j in range(0, len(positions), 2):
        to = slice(j * block, (j + 2) * block)
        (g, part, n), second = (plan.facing[p] for p in positions[j : j + 2])
        if n == 0 and second == (g, part, 1):
            at = plan.offset(plan.parts[g], part, features)
            far[:, to] = received[g - base][at : at + features + EXTRA, :]
        else:
            far[:, to] = jnp.concatenate([block_of(g, part, n), block_of(*second)], axis=1)
    s_own, s_far = own[:channels, columns], far[:channels, :]
    t_own = [own[channels + k * m : channels + (k + 1) * m, columns] for k in range(comps)]
    t_far = [far[channels + k * m : channels + (k + 1) * m, :] for k in range(comps)]
    picks = jnp.transpose(table[...])
    e_own = embed(s_own, picks, own[features : features + 1, columns].astype(F32))
    e_far = embed(s_far, picks, far[features : features + 1, :].astype(F32))
    w_shared = nt(eye(channels), w_invariant[...]).astype(BF16)
    shared = mm(w_shared, invariants(t_own, t_far))
    embedded = jnp.concatenate([e_own, e_far], axis=1)
    w_rev = jnp.concatenate([w_key[...], w_value[...]], axis=0)
    both = mm(w_rev, jnp.concatenate([s_far, s_own], axis=1))
    attended = attend(mm(w_query[...], embedded), both[:channels], both[channels:])
    middles = (
        embedded.astype(F32)
        + mm(w_output[...], attended)
        + jnp.concatenate([shared, shared], axis=1)
    ).astype(BF16)
    middle = middles[:, :slots]
    incoming = mm(w_message[...], middles[:, slots:]).astype(BF16)
    w_mid = jnp.concatenate([w_expand[...], w_gate[...], w_radial[...]], axis=0)
    spread = mm(w_mid, middle)
    hidden = w_expand.shape[0]
    v = spread[:hidden] + mm(w_reverse[...], incoming)
    s_new[...] = contract(middle, v, w_contract[...])
    gate = jax.nn.sigmoid(spread[hidden : hidden + 3 * m])
    radial = spread[hidden + 3 * m :]
    mixed = [mm(w_mixing[...], t_far[k]) for k in range(comps)]
    for k, new in update_tensors(t_own, mixed, gate, radial, where[:, columns]):
        t_new[k * m : (k + 1) * m, :] = new


def near_kernel(plan, block, positions, *refs):
    received, (own, where, table, *refs) = refs[:3], refs[3:]
    weights, (s_new, t_new, far) = refs[:12], refs[12:]
    settle(plan, block, positions, 0, received, own, where, table, weights, far, s_new, t_new)


def boundary_kernel(plan, block, positions, base, count, done, edges, *refs):
    received, refs = refs[:count], refs[count:]
    settled, (own, where, merge, reverse, scalars_in, tensors_in, table, *refs) = (
        refs[:done],
        refs[done:],
    )
    weights, (scalars_out, tensors_out, s_new, t_new, far) = refs[:12], refs[12:]
    comps, m = tensors_in.shape[:2]
    channels = scalars_in.shape[0]

    @pl.when(pl.program_id(0) == 0)
    def _():
        settle(
            plan, block, positions, base, received, own, where, table, weights, far, s_new, t_new
        )

    width = scalars_out.shape[-1]
    here = pl.ds(pl.multiple_of(pl.program_id(0) * width, 128), width)
    first = len(positions) * block
    crosses = jnp.broadcast_to((reverse[0, :, here] >= edges).astype(F32), (m, width))
    crosses = crosses.astype(BF16) > 0

    def spread(new, n):
        total = mm(new[...], merge[:first, here])
        if done:
            total = total + mm(settled[n][...], merge[first:, here])
        return total

    def merged(new, old):
        return jnp.where(crosses, new.astype(BF16), old)

    s_all = spread(s_new, 0)
    for c in range(0, channels, m):
        scalars_out[0, 0, c : c + m] = merged(s_all[c : c + m], scalars_in[c : c + m, here])
    t_all = spread(t_new, 1)
    for k in range(comps):
        tensors_out[0, 0, k] = merged(t_all[k * m : (k + 1) * m], tensors_in[k, :, here])


def resident(*arrays):
    return [pltpu.with_memory_space_constraint(x, pltpu.HBM) for x in arrays]


def whole(*shape):
    return pl.BlockSpec(shape, lambda *_: (0,) * len(shape))


def per_device(gx, gy, *args):
    (
        scalars,
        tensors,
        vectors,
        species,
        table,
        reverse,
        send_index,
        counts,
        w_query,
        w_key,
        w_value,
        w_output,
        w_invariant,
        w_message,
        w_gate,
        w_radial,
        w_mixing,
        w_expand,
        w_reverse,
        w_contract,
    ) = args
    plan = Plan(gx, gy)
    vectors = jnp.transpose(vectors, (0, 2, 1, 3))
    table = jnp.transpose(table)
    w_invariant = jnp.transpose(w_invariant)
    _, _, channels, edges = scalars.shape
    comps, m = tensors.shape[2:4]
    features = channels + comps * m
    block = send_index.shape[-1]
    slots = len(DIRECTIONS) * block
    vmem = pl.BlockSpec(memory_space=pltpu.VMEM)

    def limit(mebibytes):
        return pltpu.CompilerParams(vmem_limit_bytes=mebibytes * 2**20)


    hbm = pl.BlockSpec(memory_space=pltpu.HBM)

    def buffers(*arrays):
        return [pltpu.VMEM(x.shape, x.dtype) for x in arrays] + [
            pltpu.SemaphoreType.DMA((len(arrays),))
        ]

    prepared = (send_index, counts, species, vectors, reverse, scalars, tensors)
    prepared_buffers = buffers(*prepared)
    del prepared_buffers[5:7]
    prepared_buffers[1] = pltpu.SMEM(counts.shape, counts.dtype)
    prepared_buffers.insert(0, pltpu.VMEM((edges, slots), BF16))
    own, where, rows, scalars, tensors, *sends = pl.pallas_call(
        functools.partial(prepare_kernel, plan),
        in_specs=[hbm] * len(prepared),
        out_specs=[vmem] * (5 + len(plan.arrays)),
        out_shape=[
            jax.ShapeDtypeStruct((features + EXTRA, slots), BF16),
            jax.ShapeDtypeStruct((8, slots), F32),
            jax.ShapeDtypeStruct((edges // 128, 128), jnp.int32),
            jax.ShapeDtypeStruct(scalars.shape, BF16),
            jax.ShapeDtypeStruct(tensors.shape, BF16),
        ]
        + [
            jax.ShapeDtypeStruct((plan.rows(parts, features), 2 * block), BF16)
            for parts in plan.arrays
        ],
        scratch_shapes=prepared_buffers,
        compiler_params=limit(24),
        name="prepare",
    )(*resident(*prepared))

    def exchange(x, pairs):
        return lax.ppermute(x, ("gx", "gy"), pairs)

    if plan.paired:
        received = [
            exchange(sends[0], plan.swaps[0]),
            exchange(sends[1], plan.swaps[1]),
            exchange(sends[2], plan.across),
        ]
    else:
        received = [exchange(x, pairs) for x, pairs in zip(sends, plan.pairs)]

    width = 1024 if edges % 1024 == 0 else edges
    steps = edges // width
    flat = whole(channels, edges)
    first_weights = (w_query, w_key, w_value, w_output, w_invariant, w_message, w_gate, w_radial, w_mixing)
    last_weights = (w_expand, w_reverse, w_contract)
    inside = (
        w_mixing, w_invariant, vectors, species, table,
        w_query, w_output, w_key, w_value, w_message, w_gate, w_radial,
    )
    stacked = [pltpu.VMEM((2 * channels, channels), BF16), pltpu.VMEM((channels + 6 * m, channels), BF16)]
    middle, message, t_inside = pl.pallas_call(
        interior_kernel,
        grid=(steps,),
        in_specs=[pl.BlockSpec(memory_space=pltpu.SMEM)]
        + [whole(*scalars.shape), whole(*tensors.shape)]
        + [hbm] * len(inside),
        out_specs=[flat, flat, whole(comps, m, edges)],
        out_shape=[
            jax.ShapeDtypeStruct((channels, edges), BF16),
            jax.ShapeDtypeStruct((channels, edges), BF16),
            jax.ShapeDtypeStruct((comps, m, edges), BF16),
        ],
        scratch_shapes=[
            pltpu.VMEM((edges * 8, 128), F32),
            pltpu.VMEM((width * 8, 128), F32),
            pltpu.VMEM((256, 128), BF16),
            pltpu.VMEM((channels, w_invariant.shape[0]), BF16),
        ]
        + buffers(*inside)[:7]
        + stacked
        + [pltpu.SemaphoreType.DMA((len(inside),))],
        compiler_params=limit(36),
        cost_estimate=pl.CostEstimate(
            flops=2 * edges * edges * features, bytes_accessed=4 * edges * features, transcendentals=0
        ),
        name="interior",
    )(rows, scalars, tensors, *resident(*inside))
    last_weights = (w_expand, w_reverse, w_contract)
    brought = (reverse, *last_weights)
    s_inside, merge = pl.pallas_call(
        functools.partial(incoming_kernel, plan, block),
        grid=(steps,),
        in_specs=[whole(channels, edges), flat, pl.BlockSpec(memory_space=pltpu.SMEM)]
        + [hbm] * len(brought),
        out_specs=[flat, whole(slots, edges)],
        out_shape=[
            jax.ShapeDtypeStruct((channels, edges), BF16),
            jax.ShapeDtypeStruct((slots, edges), BF16),
        ],
        scratch_shapes=[
            pltpu.VMEM((edges * 8, 128), F32),
            pltpu.VMEM((width * 8, 128), F32),
        ]
        + buffers(*brought),
        compiler_params=limit(24),
        cost_estimate=pl.CostEstimate(
            flops=4 * edges * edges * channels, bytes_accessed=8 * edges * channels, transcendentals=0
        ),
        name="incoming",
    )(message, middle, rows, *resident(*brought))
    if plan.paired:
        held = lax.optimization_barrier((received[0], received[1], s_inside))
        received[0], received[1], s_inside = held
        relayed = [exchange(received[0], plan.across), exchange(received[1], plan.across)]
        positions, near = tuple(range(4)), tuple(range(4, 8))
        columns = len(near) * block
        settled = pl.pallas_call(
            functools.partial(near_kernel, plan, block, near),
            in_specs=[vmem] * (6 + len(first_weights + last_weights)),
            out_specs=[vmem, vmem],
            out_shape=[
                jax.ShapeDtypeStruct((channels, columns), BF16),
                jax.ShapeDtypeStruct((comps * m, columns), BF16),
            ],
            scratch_shapes=[pltpu.VMEM((features + EXTRA, columns), BF16)],
            compiler_params=limit(16),
            cost_estimate=pl.CostEstimate(
                flops=4 * columns * channels * features, bytes_accessed=4 * columns * features, transcendentals=0
            ),
            name="near",
        )(*received, own, where, table, *first_weights, *last_weights)
        base, received = 3, relayed
    else:
        positions, base, settled = tuple(range(len(DIRECTIONS))), 0, []

    columns = len(positions) * block
    return pl.pallas_call(
        functools.partial(
            boundary_kernel, plan, block, positions, base, len(received), len(settled), edges
        ),
        grid=(steps,),
        in_specs=[whole(*r.shape) for r in (*received, *settled)]
        + [whole(*own.shape), whole(*where.shape), whole(slots, edges)]
        + [whole(*reverse.shape), flat, whole(comps, m, edges), whole(*table.shape)]
        + [whole(*w.shape) for w in first_weights + last_weights],
        out_specs=[
            pl.BlockSpec((1, 1, channels, width), lambda i: (0, 0, 0, i)),
            pl.BlockSpec((1, 1, comps, m, width), lambda i: (0, 0, 0, 0, i)),
        ],
        out_shape=[
            jax.ShapeDtypeStruct((1, 1, channels, edges), BF16),
            jax.ShapeDtypeStruct((1, 1, comps, m, edges), BF16),
        ],
        scratch_shapes=[
            pltpu.VMEM((channels, columns), BF16),
            pltpu.VMEM((comps * m, columns), BF16),
            pltpu.VMEM((features + EXTRA, columns), BF16),
        ],
        compiler_params=limit(26),
        cost_estimate=pl.CostEstimate(
            flops=2 * edges * slots * features, bytes_accessed=8 * edges * features, transcendentals=0
        ),
        name="boundary",
    )(
        *received, *settled, own, where, merge, reverse, s_inside, t_inside, table,
        *first_weights, *last_weights,
    )


def solution(mesh):
    gx, gy = mesh.shape["gx"], mesh.shape["gy"]

    def body(*args):
        return per_device(gx, gy, *args)

    step = jax.shard_map(
        body,
        mesh=mesh,
        in_specs=(
            P("gx", "gy", None, None),
            P("gx", "gy", None, None, None),
            P("gx", "gy", None, None),
            P("gx", "gy", None),
            P(),
            P("gx", "gy", None),
            P("gx", "gy", None, None),
            P("gx", "gy", None),
        )
        + (P(),) * 12,
        out_specs=(P("gx", "gy", None, None), P("gx", "gy", None, None, None)),
        check_vma=False,
    )
    if not Plan(gx, gy).paired:
        return step
    return step
```
